256 devices in a mesh: section: 4 (over x), ctx: 32 (over z, y), tp: 2 (over core).
Axes of the slice: x: 4, y: 4, z: 8, core: 2. Of those that a mesh axis runs over, the one named last changes fastest.
Arguments:
- hidden: bfloat16 [4, 4096, 8192], P('section', 'ctx', 'tp')
- gain: bfloat16 [4, 8192], P('section', 'tp'), may hold values from 0.5 to 1.5
- queries: bfloat16 [4, 4096, 32, 128], P('section', 'ctx', 'tp')
- key_value_weight: bfloat16 [4, 8192, 4, 2, 128], P('section', 'ctx', 'tp')
- adapt_down: bfloat16 [4, 16, 4096], P('section', None, 'tp'), may hold values from -1 to 1
- adapt_up: bfloat16 [4, 16, 8192], P('section', None, 'tp'), may hold values from -0.75 to 0.75
- out_grad: bfloat16 [4, 4096, 8192], P('section', 'ctx', 'tp'), may hold values from -6 to 6
- doc_ids: int32 [4096], P('ctx'), may hold values from 0 to 63, never falling along the last dimension, each value on 1 to 3072 neighbouring positions
Outputs:
- attention_out: bfloat16 [4, 4096, 4096], P('section', 'ctx', 'tp')
- adapter_out: bfloat16 [4, 4096, 8192], P('section', 'ctx', 'tp')
- grad_down: float32 [4, 16, 4096], P('section', None, 'tp')
- grad_up: float32 [4, 16, 8192], P('section', None, 'tp')
The draws below stay inside these ranges and needn't reach their ends.
Inputs may be any that keep to these rules, and one draw needn't show every extreme that they name: doc_ids never falls along the sequence; a document spans at most three quarters of 4096 tokens, and one spans exactly that.
All inputs are finite; a program needn't handle non-finite values.
Results may differ from the reference program's by a relative error of at most 0.022.
Values may be sent and summed in bfloat16 or wider, within the bound.
A program may use at most 128 MiB of HBM per device.

```python
import math
import jax
import jax.numpy as jnp
import numpy as np
from jax import lax

MODEL_WIDTH = 8192
HEAD_SIZE = 128
GROUP = 8
R = 16
LAYER_SECTIONS = 4
SEQUENCE_TOKENS = 4096
KEYVALUE_HEADS = 4
HQ = 32
QW = 4096
DOCS = 64


def spike_plan(key):
    random_seed_key = jax.random.fold_in(key, 4242)
    pair_count = max(2, SEQUENCE_TOKENS // 512)
    column = jax.random.randint(jax.random.fold_in(random_seed_key, 1), (), 0, MODEL_WIDTH)
    pair_starts = jax.random.randint(jax.random.fold_in(random_seed_key, 2), (LAYER_SECTIONS, pair_count), 0, SEQUENCE_TOKENS - 1)
    lift_size = jax.random.uniform(jax.random.fold_in(random_seed_key, 3), (LAYER_SECTIONS, pair_count), minval=2.0, maxval=3.0)
    pair_step = jax.random.uniform(jax.random.fold_in(random_seed_key, 4), (LAYER_SECTIONS, pair_count), minval=0.02, maxval=0.08)
    strength = jax.random.uniform(jax.random.fold_in(random_seed_key, 5), (LAYER_SECTIONS, pair_count), minval=2.0, maxval=4.0)
    sign_flags = jax.random.randint(jax.random.fold_in(random_seed_key, 6), (KEYVALUE_HEADS, HEAD_SIZE), 0, 2)
    half_width = HEAD_SIZE // 2
    dim_index = jnp.arange(HEAD_SIZE)
    planted = dim_index % half_width >= half_width - 4
    sign_table = jnp.where(planted[None, :], 2.0 * sign_flags.astype(jnp.float32) - 1.0, 0.0)
    row_index = jnp.arange(SEQUENCE_TOKENS)
    first_rows = row_index[None, None, :] == pair_starts[:, :, None]
    second_rows = row_index[None, None, :] == pair_starts[:, :, None] + 1
    either_rows = first_rows | second_rows
    lifted = jnp.max(jnp.where(first_rows, lift_size[:, :, None], jnp.where(second_rows, (lift_size * (1.0 + pair_step))[:, :, None], 0.0)), axis=1)
    marked = jnp.any(either_rows, axis=1)
    pushed = jnp.max(jnp.where(either_rows, strength[:, :, None], 0.0), axis=1)
    return (column, marked, lifted, pushed, planted, sign_table)


def draw_hidden(key, part):
    column, marked, lifted, pushed, planted, sign_table = spike_plan(key)
    noise_key = jax.random.fold_in(key, 11)
    noise_field = jax.random.truncated_normal(noise_key, -6.0, 6.0, (LAYER_SECTIONS, SEQUENCE_TOKENS, MODEL_WIDTH))
    spike_hit = (jnp.arange(MODEL_WIDTH) == column)[None, None, :] & marked[:, :, None]
    spike_value = lifted * MODEL_WIDTH ** 0.5
    return jnp.where(spike_hit, spike_value[:, :, None], noise_field).astype(jnp.bfloat16)


def draw_queries(key, part):
    column, marked, lifted, pushed, planted, sign_table = spike_plan(key)
    noise_key = jax.random.fold_in(key, 21)
    noise_field = jax.random.truncated_normal(noise_key, -6.0, 6.0, (LAYER_SECTIONS, SEQUENCE_TOKENS, HQ, HEAD_SIZE))
    head_signs = jnp.repeat(sign_table, GROUP, axis=0)
    boost = (pushed * HEAD_SIZE ** 0.5)[:, :, None, None] * head_signs[None, None, :, :]
    return (noise_field + boost).astype(jnp.bfloat16)


def draw_key_value_weight(key, part):
    column, marked, lifted, pushed, planted, sign_table = spike_plan(key)
    weight_scale = MODEL_WIDTH ** (-0.5)
    noise_key = jax.random.fold_in(key, 31)
    complete_shape = (LAYER_SECTIONS, MODEL_WIDTH, KEYVALUE_HEADS, 2, HEAD_SIZE)
    noise_field = jax.random.truncated_normal(noise_key, -4.0, 4.0, complete_shape) * weight_scale
    spike_hit = (jnp.arange(MODEL_WIDTH) == column)[None, :, None, None, None] & (jnp.arange(2) == 0)[None, None, None, :, None] & planted[None, None, None, None, :]
    planted_value = 16.0 * weight_scale * sign_table[None, None, :, None, :]
    return jnp.where(spike_hit, planted_value, noise_field).astype(jnp.bfloat16)


def levels(own_key, dims, split, least, high):
    factor_of = 1.0
    for position, parts in split:
        steps = jax.random.uniform(jax.random.fold_in(jax.random.fold_in(own_key, 6), position), (parts,), jnp.float32, least / len(split), high / len(split))
        factor_of = factor_of * jnp.repeat(jnp.exp(steps), dims[position] // parts).reshape((-1,) + (1,) * (len(dims) - 1 - position))
    return factor_of


def length_profile(count, total, most, skew):
    loads = [(1 << 20) // math.isqrt(standing ** skew) + 1 for standing in range(2, count + 1)]
    surplus, counts = total - most - (count - 1), [1] * (count - 1)
    while surplus > 0:
        free = [i for i in range(count - 1) if counts[i] < most]
        pool, budget = sum([loads[i] for i in free]), surplus
        for i in free:
            extra = min(most - counts[i], max(1, budget * loads[i] // pool), surplus)
            counts[i] = counts[i] + extra
            surplus = surplus - extra
    return np.array([most] + counts)


def uneven(rng, number_of, total, reach, slope):
    if number_of == 2:
        one = jax.random.randint(rng, (), max(1, total - reach), min(reach, total - 1) + 1)
        return jnp.stack([one, total - one])
    tallies = jnp.asarray(length_profile(number_of, total, reach, slope), jnp.int32)
    couples = (number_of - 1) // 2
    giver, taker = tallies[1:1 + 2 * couples:2], tallies[2:2 + 2 * couples:2]
    slack = jnp.minimum(giver - 1, reach - taker)
    shifted = jax.random.randint(jax.random.fold_in(rng, 1), (couples,), 0, 1 << 20) % (slack + 1)
    tallies = tallies.at[1:1 + 2 * couples:2].set(giver - shifted).at[2:2 + 2 * couples:2].set(taker + shifted)
    return tallies[jax.random.permutation(jax.random.fold_in(rng, 2), number_of)]


def normal_values(stream_key, shape, spread, most, shards=(), kind=jnp.bfloat16):
    loudness = levels(stream_key, shape, shards, -0.22, 0.18) if shards else 1.0
    drawn = jax.random.normal(stream_key, shape, jnp.float32) * spread * loudness
    return jnp.minimum(jnp.maximum(drawn, -most), most).astype(kind)


def setup_inputs(seed: int = 0) -> dict:
    arg_keys = jax.random.split(jax.random.key(seed), 9)
    return {
        "hidden": draw_hidden(jax.random.fold_in(arg_keys[8], 71), 0),
        "gain": jnp.clip(1.0 + 0.1 * jax.random.normal(arg_keys[1], (LAYER_SECTIONS, MODEL_WIDTH), jnp.float32), 0.5, 1.5).astype(jnp.bfloat16),
        "queries": draw_queries(jax.random.fold_in(arg_keys[8], 71), 0),
        "key_value_weight": draw_key_value_weight(jax.random.fold_in(arg_keys[8], 71), 0),
        "adapt_down": normal_values(arg_keys[4], (LAYER_SECTIONS, R, QW), (2 * R) ** -0.5, 1.0, ((0, 4), (2, 2))),
        "adapt_up": normal_values(arg_keys[5], (LAYER_SECTIONS, R, MODEL_WIDTH), (4 * R) ** -0.5, 0.75, ((0, 4), (2, 2))),
        "out_grad": normal_values(arg_keys[6], (LAYER_SECTIONS, SEQUENCE_TOKENS, MODEL_WIDTH), 1.0, 6.0, ((0, 4), (1, 32), (2, 2))),
        "doc_ids": jnp.searchsorted(jnp.cumsum(uneven(arg_keys[7], DOCS, SEQUENCE_TOKENS, (3 * SEQUENCE_TOKENS) // 4, 1)), jnp.arange(SEQUENCE_TOKENS), side="right").astype(jnp.int32),
    }


def rotate(head_values, positions):
    half_width = head_values.shape[-1] // 2
    freqs = 1000000.0 ** (-jnp.arange(half_width, dtype=jnp.float32) * 2.0 / head_values.shape[-1])
    angles = positions.astype(jnp.float32)[:, None] * freqs[None, :]
    cosine = jnp.cos(angles)[:, None, :]
    sine_table = jnp.sin(angles)[:, None, :]
    first_half = head_values[..., :half_width]
    second_half = head_values[..., half_width:]
    return jnp.concatenate([first_half * cosine - second_half * sine_table, second_half * cosine + first_half * sine_table], axis=-1)

def one_section(hidden, gain, queries, key_value_weight, adapt_down, adapt_up, out_grad, doc_ids):
    widened = hidden.astype(jnp.float32)
    normalized_rows = (widened * lax.rsqrt(lax.optimization_barrier(jnp.mean(widened * widened, axis=1, keepdims=True)) + 1e-06) * gain.astype(jnp.float32)).astype(jnp.bfloat16)
    positions = jnp.arange(SEQUENCE_TOKENS, dtype=jnp.int32)
    rotated_query = rotate(queries.astype(jnp.float32), positions).astype(jnp.bfloat16)
    key_value_rows = jnp.dot(normalized_rows, key_value_weight.reshape(MODEL_WIDTH, KEYVALUE_HEADS * 2 * HEAD_SIZE), preferred_element_type=jnp.float32).reshape(SEQUENCE_TOKENS, KEYVALUE_HEADS, 2, HEAD_SIZE)
    rotated_keys = rotate(key_value_rows[:, :, 0], positions).astype(jnp.bfloat16)
    value_rows = key_value_rows[:, :, 1].astype(jnp.bfloat16)
    allowed = (positions[None, :] <= positions[:, None]) & (doc_ids[None, :] == doc_ids[:, None])
    query_heads = rotated_query.transpose(1, 0, 2)
    key_heads = jnp.repeat(rotated_keys.transpose(1, 0, 2), GROUP, axis=0)
    value_heads = jnp.repeat(value_rows.transpose(1, 0, 2), GROUP, axis=0)

    def attend_head(items):
        head_query, head_keys, head_values = items
        scores = jnp.dot(head_query, head_keys.T, preferred_element_type=jnp.float32) * HEAD_SIZE ** (-0.5)
        scores = jnp.where(allowed, scores, -1e+30)
        row_top = lax.optimization_barrier(jnp.max(scores, axis=1, keepdims=True))
        weights = jnp.where(allowed, jnp.exp(scores - row_top), 0.0)
        weight_sum = lax.optimization_barrier(jnp.sum(weights, axis=1, keepdims=True))
        return jnp.dot(weights.astype(jnp.bfloat16), head_values, preferred_element_type=jnp.float32) / weight_sum
    heads_out = lax.map(attend_head, (query_heads, key_heads, value_heads))
    attended = heads_out.transpose(1, 0, 2).reshape(SEQUENCE_TOKENS, QW).astype(jnp.bfloat16)
    low_rows = jnp.dot(attended, adapt_down.T, preferred_element_type=jnp.float32).astype(jnp.bfloat16)
    adapter_rows = jnp.dot(low_rows, adapt_up, preferred_element_type=jnp.float32).astype(jnp.bfloat16)
    back_rows = jnp.dot(out_grad, adapt_up.T, preferred_element_type=jnp.float32).astype(jnp.bfloat16)
    up_raw = jnp.dot(low_rows.T, out_grad, preferred_element_type=jnp.float32)
    down_raw = jnp.dot(back_rows.T, attended, preferred_element_type=jnp.float32)
    return (attended, adapter_rows, down_raw, up_raw)

def reference(hidden, gain, queries, key_value_weight, adapt_down, adapt_up, out_grad, doc_ids):
    attended_all = []
    adapter_all = []
    downs = []
    uppers = []
    for section_index in range(LAYER_SECTIONS):
        attended, adapter_rows, down_raw, up_raw = one_section(hidden[section_index], gain[section_index], queries[section_index], key_value_weight[section_index], adapt_down[section_index], adapt_up[section_index], out_grad[section_index], doc_ids)
        attended_all.append(attended)
        adapter_all.append(adapter_rows)
        downs.append(down_raw)
        uppers.append(up_raw)
    down_all = jnp.stack(downs)
    up_all = jnp.stack(uppers)
    squares = jnp.sum(down_all * down_all) + jnp.sum(up_all * up_all)
    ceiling = 0.5 * math.sqrt(LAYER_SECTIONS * R * (QW + MODEL_WIDTH))
    factor = jnp.minimum(1.0, ceiling / (jnp.sqrt(squares) + 1e-06))
    return (jnp.stack(attended_all), jnp.stack(adapter_all), down_all * factor, up_all * factor)
```

```python
import math

import jax
import jax.numpy as jnp
from jax import lax
from jax.experimental import pallas as pl
from jax.experimental.pallas import tpu as pltpu
from jax.sharding import PartitionSpec as P

MESH = pl.DeviceIdType.MESH
NY = 4
F32 = jnp.float32
BF16 = jnp.bfloat16


def remote(src, dst, send_sem, recv_sem, **where):
    return pltpu.make_async_remote_copy(
        src_ref=src,
        dst_ref=dst,
        send_sem=send_sem,
        recv_sem=recv_sem,
        device_id=where,
        device_id_type=MESH,
    )


def position():
    ctx = lax.axis_index("ctx")
    return ctx // NY, ctx % NY, lax.axis_index("tp")


class Ring:
    def __init__(self, nz, block, half, send, recv, sib_send=None, sib_recv=None):
        self.nz, self.steps = nz, nz // 2
        self.block, self.half = block, half
        self.send, self.recv = send, recv
        self.sib_send, self.sib_recv = sib_send, sib_recv
        self.z, self.y, self.t = position()

    def origin(self, d, s):
        return (self.z - s + self.nz) % self.nz if d == 0 else (self.z + s) % self.nz

    def neighbour(self, d):
        z = (self.z + 1) % self.nz if d == 0 else (self.z + self.nz - 1) % self.nz
        return dict(ctx=z * NY + self.y, tp=self.t)

    def piece(self, zi, d, s):
        return self.half(zi, d, self.t) if s == self.steps else self.block(zi, self.t)

    def hop(self, d, s, src=None):
        piece = self.piece(self.origin(d, s - 1), d, s)
        return remote(
            piece if src is None else src,
            piece,
            self.send.at[d, s - 1],
            self.recv.at[d, s - 1],
            **self.neighbour(d),
        )

    def arrival(self, d, s):
        piece = self.piece(self.origin(d, s), d, s)
        return remote(
            piece, piece, self.send.at[d, s - 1], self.recv.at[d, s - 1], **self.neighbour(d)
        )

    def aside(self, index, zi, core, src=None):
        piece = self.block(zi, core)
        return remote(
            piece if src is None else src,
            piece,
            self.sib_send.at[index],
            self.sib_recv.at[index],
            tp=1 - self.t,
        )

    def start(self, src=None):
        for d in (0, 1):
            self.hop(d, 1, src).start()
        if self.sib_send is not None:
            self.aside(0, self.z, self.t, src).start()

    def step(self, s):
        for d in (0, 1):
            self.arrival(d, s).wait_recv()
            self.hop(d, s + 1).start()
            if self.sib_send is not None:
                self.aside(2 * s - 1 + d, self.origin(d, s), self.t).start()

    def final(self):
        for d in (0, 1):
            self.arrival(d, self.steps).wait_recv()
        if self.sib_send is not None:
            self.aside(self.nz - 1, self.origin(0, self.steps), self.t).start()

    def asides(self):
        yield 0, self.z
        for s in range(1, self.steps):
            for d in (0, 1):
                yield 2 * s - 1 + d, self.origin(d, s)
        yield self.nz - 1, self.origin(0, self.steps)

    def wait_sibling(self):
        for index, zi in self.asides():
            self.aside(index, zi, 1 - self.t).wait_recv()

    def drain(self):
        for d in (0, 1):
            for s in range(1, self.steps + 1):
                self.hop(d, s).wait_send()
        if self.sib_send is not None:
            for index, zi in self.asides():
                self.aside(index, zi, self.t).wait_send()


def gather_kernel(
    nz,
    hid_ref,
    gain_ref,
    w_ref,
    q_ref,
    cos_ref,
    sin_ref,
    grad_ref,
    up_ref,
    down_ref,
    doc_ref,
    q_out,
    k_out,
    v_out,
    doc_out,
    back_out,
    down_out,
    w_buf,
    normed,
    x_buf,
    square_src,
    square_in,
    back_src,
    back_in,
    down_buf,
    doc_in,
    k_part,
    k_in,
    v_part,
    v_in,
    w_send,
    w_recv,
    ws_send,
    ws_recv,
    kv_send,
    kv_recv,
    kvs_send,
    kvs_recv,
    d_send,
    d_recv,
    x_send,
    x_recv,
    q_send,
    q_recv,
    rs_send,
    rs_recv,
    dy_send,
    dy_recv,
    pair_send,
    pair_recv,
):
    z, y, t = position()
    rows, width = hid_ref.shape
    depth = w_ref.shape[1]
    cols = depth * nz // 2
    head_dim = k_out.shape[-1]
    toks = 2 * rows
    home = y // 2

    barrier = pltpu.get_barrier_semaphore()
    for oz in (1, nz - 1):
        pl.semaphore_signal(
            barrier,
            inc=1,
            device_id=dict(ctx=(z + oz) % nz * NY + y, tp=t),
            device_id_type=MESH,
        )
    for oy in range(NY):
        for ot in range(2):
            if oy or ot:
                pl.semaphore_signal(
                    barrier,
                    inc=1,
                    device_id=dict(ctx=z * NY + (y + oy) % NY, tp=(t + ot) % 2),
                    device_id_type=MESH,
                )
    pl.semaphore_wait(barrier, 2 + 2 * NY - 1)

    def w_block(p):
        return lambda zi, core: w_buf.at[p, core, pl.ds(pl.multiple_of(zi * depth, depth), depth)]

    def w_half(p):
        return lambda zi, h, core: w_buf.at[
            p, core, pl.ds(pl.multiple_of(zi * depth + h * (depth // 2), depth // 2), depth // 2)
        ]

    def kv_half(buf):
        return lambda zi, h, core: buf.at[zi, core, pl.ds(h * (toks // 2), toks // 2)]

    w_rings = [
        Ring(nz, w_block(p), w_half(p), w_send.at[p], w_recv.at[p], ws_send.at[p], ws_recv.at[p])
        for p in (0, 1)
    ]
    kv_rings = [
        Ring(
            nz,
            lambda zi, core, buf=buf: buf.at[zi, core],
            kv_half(buf),
            kv_send.at[p],
            kv_recv.at[p],
            kvs_send.at[p],
            kvs_recv.at[p],
        )
        for p, buf in ((0, k_out), (1, v_out))
    ]

    w_rings[0].start(w_ref.at[0])
    sibling = dict(tp=1 - t)

    def doc_copy(oy):
        return remote(
            doc_ref,
            doc_in.at[oy - 1],
            dy_send.at[oy - 1],
            dy_recv.at[oy - 1],
            ctx=z * NY + (y + oy) % NY,
        )

    for oy in range(1, NY):
        doc_copy(oy).start()

    def down_copy(core):
        return remote(down_ref, down_buf.at[core], pair_send.at[0], pair_recv.at[0], **sibling)

    down_copy(t).start()

    hid = hid_ref[...].astype(F32)
    square = jnp.sum(hid * hid, axis=1, keepdims=True)
    square_src[...] = jnp.broadcast_to(square, square_src.shape)
    square_copy = remote(square_src, square_in, pair_send.at[1], pair_recv.at[1], **sibling)
    square_copy.start()
    down_buf[t] = down_ref[...]
    w_buf[0, t, pl.ds(pl.multiple_of(z * depth, depth), depth), :] = w_ref[0]
    w_buf[1, t, pl.ds(pl.multiple_of(z * depth, depth), depth), :] = w_ref[1]
    square_copy.wait_recv()
    mean = (square_src[:, :1] + square_in[:, :1]) * (1.0 / (2 * width))
    scale = lax.rsqrt(mean + 1e-06)

    def x_dest(b, core):
        return x_buf.at[pl.ds(b * rows, rows), pl.ds(pl.multiple_of(core * cols, cols), cols)]

    def x_copy(oy):
        yd = (y + oy) % NY
        return remote(
            normed.at[yd],
            x_dest(y % 2, t),
            x_send.at[oy],
            x_recv.at[y % 2, t],
            ctx=z * NY + yd,
            tp=home,
        )

    for yd in range(NY):
        for zl in range(nz // 2):
            start = (zl * NY + yd) * depth
            piece = hid_ref[:, start : start + depth].astype(F32)
            gain = gain_ref[:, start : start + depth].astype(F32)
            normed[yd, :, zl * depth : (zl + 1) * depth] = (piece * scale * gain).astype(BF16)
    for oy in range(1, NY):
        x_copy(oy).start()

    @pl.when(t != home)
    def _():
        x_copy(0).start()

    @pl.when(t == home)
    def _():
        x_buf[
            pl.ds(pl.multiple_of((y % 2) * rows, rows), rows),
            pl.ds(pl.multiple_of(t * cols, cols), cols),
        ] = normed[y]

    back_src[...] = lax.dot_general(
        up_ref[...], grad_ref[...], (((1,), (1,)), ((), ())), preferred_element_type=F32
    )
    back_copy = remote(back_src, back_in, pair_send.at[2], pair_recv.at[2], **sibling)
    back_copy.start()

    steps = nz // 2
    for s in range(1, steps):
        w_rings[0].step(s)
    w_rings[1].start(w_ref.at[1])
    w_rings[0].final()

    back_copy.wait_recv()
    back_out[...] = (back_src[...] + back_in[...]).astype(BF16)
    down_copy(1 - t).wait_recv()
    down_out[...] = down_buf[
        home, :, pl.ds(pl.multiple_of((y % 2) * down_out.shape[1], 128), down_out.shape[1])
    ]

    for oy in range(1, NY):
        doc_copy(oy).wait_recv()
    line = lax.broadcasted_iota(jnp.int32, doc_ref.shape, 0)
    group = jnp.where(line == y, doc_ref[...], 0)
    for oy in range(1, NY):
        group = jnp.where(line == (y + NY - oy) % NY, doc_in[oy - 1], group)
    doc_out[z] = group

    def doc_pass(d, s):
        zi = (z - s + 1 + nz) % nz if d == 0 else (z + s - 1) % nz
        to = (z + 1) % nz if d == 0 else (z + nz - 1) % nz
        return remote(
            doc_out.at[zi], doc_out.at[zi], d_send.at[d, s - 1], d_recv.at[d, s - 1], ctx=to * NY + y
        )

    def doc_arrive(d, s):
        zi = (z - s + nz) % nz if d == 0 else (z + s) % nz
        to = (z + 1) % nz if d == 0 else (z + nz - 1) % nz
        return remote(
            doc_out.at[zi], doc_out.at[zi], d_send.at[d, s - 1], d_recv.at[d, s - 1], ctx=to * NY + y
        )

    doc_hops = [(0, s) for s in range(1, steps + 1)] + [(1, s) for s in range(1, steps)]

    def doc_step(s):
        for d in (0, 1):
            if (d, s) in doc_hops:
                doc_arrive(d, s).wait_recv()
                if (d, s + 1) in doc_hops:
                    doc_pass(d, s + 1).start()

    for d in (0, 1):
        if (d, 1) in doc_hops:
            doc_pass(d, 1).start()

    if steps > 1:
        w_rings[1].step(1)

    def x_wait():
        for b in range(2):
            for core in range(2):
                src_y = 2 * t + b

                @pl.when(jnp.logical_or(src_y != y, t != core))
                def _():
                    dest = x_dest(b, core)
                    remote(
                        dest, dest, x_send.at[0], x_recv.at[b, core], **sibling
                    ).wait_recv()

    def project(p, part):
        for core in range(2):
            partial = jnp.dot(x_buf[...], w_buf[p, core], preferred_element_type=F32)
            for hl in range(2):
                part[2 * core + hl] = partial[:, hl * head_dim : (hl + 1) * head_dim].astype(part.dtype)

    def scatter_copy(p, oy):
        part, into = ((k_part, k_in), (v_part, v_in))[p]
        yd = (y + oy) % NY
        return remote(
            part.at[yd],
            into.at[oy - 1],
            rs_send.at[p, oy - 1],
            rs_recv.at[p, oy - 1],
            ctx=z * NY + yd,
        )

    def collect(p):
        part, into = ((k_part, k_in), (v_part, v_in))[p]
        for oy in range(1, NY):
            scatter_copy(p, oy).wait_recv()
        total = part[y].astype(F32)
        for oy in range(1, NY):
            total = total + into[oy - 1].astype(F32)
        return total

    x_wait()
    w_rings[0].wait_sibling()
    project(0, k_part)
    for oy in range(1, NY):
        scatter_copy(0, oy).start()
    for s in range(2, steps):
        w_rings[1].step(s)
        doc_step(s - 1)
    w_rings[1].final()
    w_rings[1].wait_sibling()
    project(1, v_part)
    for oy in range(1, NY):
        scatter_copy(1, oy).start()

    def q_dest(b):
        return q_out.at[:, pl.ds(b * rows, rows)]

    def q_copy(kvl):
        return remote(
            q_ref.at[kvl],
            q_dest(y % 2),
            q_send.at[kvl],
            q_recv.at[y % 2],
            ctx=z * NY + 2 * t + kvl,
            tp=home,
        )

    for kvl in range(2):
        own = jnp.logical_and(2 * t + kvl == y, home == t)

        @pl.when(jnp.logical_not(own))
        def _():
            q_copy(kvl).start()

        @pl.when(own)
        def _():
            q_out[:, pl.ds(pl.multiple_of((y % 2) * rows, rows), rows), :] = q_ref[kvl]

    keys = collect(0)
    k_out[z, t] = (keys * cos_ref[...] + pltpu.roll(keys, head_dim // 2, 1) * sin_ref[...]).astype(BF16)
    kv_rings[0].start()
    v_out[z, t] = collect(1).astype(BF16)
    kv_rings[1].start()
    for s in range(1, steps):
        kv_rings[0].step(s)
        kv_rings[1].step(s)
    kv_rings[0].final()
    kv_rings[1].final()
    for s in range(max(1, steps - 1), steps + 1):
        doc_step(s)
    kv_rings[0].wait_sibling()
    kv_rings[1].wait_sibling()

    for b in range(2):

        @pl.when(jnp.logical_or(2 * t + b != y, home != t))
        def _():
            dest = q_dest(b)
            remote(dest, dest, q_send.at[0], q_recv.at[b], **sibling).wait_recv()

    for ring in w_rings + kv_rings:
        ring.drain()
    for oy in range(1, NY):
        doc_copy(oy).wait_send()
        x_copy(oy).wait_send()
        scatter_copy(0, oy).wait_send()
        scatter_copy(1, oy).wait_send()

    @pl.when(t != home)
    def _():
        x_copy(0).wait_send()

    for kvl in range(2):

        @pl.when(jnp.logical_not(jnp.logical_and(2 * t + kvl == y, home == t)))
        def _():
            q_copy(kvl).wait_send()

    for d, s in doc_hops:
        doc_pass(d, s).wait_send()
    down_copy(t).wait_send()
    square_copy.wait_send()
    back_copy.wait_send()


def attend_kernel(q_ref, k_ref, v_ref, doc_ref, doc_smem, down_ref, out_ref, low_ref, top, total, acc):
    z, y, t = position()
    heads, toks, head_dim = q_ref.shape
    rows = toks // 2
    keys = k_ref.shape[1]
    factor = head_dim ** (-0.5) * math.log2(math.e)

    turned = jnp.transpose(doc_ref[z].astype(F32))
    lane = lax.broadcasted_iota(jnp.int32, turned.shape, 1)
    q_doc = jnp.concatenate(
        [
            jnp.sum(jnp.where(lane == 2 * t + b, turned, 0.0), axis=1, keepdims=True)
            for b in range(2)
        ],
        axis=0,
    )
    q_pos = t * toks + lax.broadcasted_iota(jnp.int32, (toks, keys), 0)
    k_pos = lax.broadcasted_iota(jnp.int32, (toks, keys), 1)
    first_doc = doc_smem[z, 2 * t, 0]

    def block(kb, first):
        k_doc = jnp.concatenate([doc_ref[kb, b : b + 1, :] for b in range(NY)], axis=1).astype(F32)
        allowed = k_doc == q_doc
        if first:
            allowed = jnp.logical_and(allowed, k_pos <= q_pos)
        bias = jnp.where(allowed, 0.0, -1e30)
        k = k_ref[kb]
        v = v_ref[kb]
        for h in range(heads):
            scores = (
                lax.dot_general(q_ref[h], k, (((1,), (1,)), ((), ())), preferred_element_type=F32)
                + bias
            )
            peak = jnp.max(scores, axis=1, keepdims=True)
            if first:
                new_top = peak
            else:
                old_top = top[h]
                new_top = jnp.maximum(old_top, peak)
                shrink = jnp.exp2((old_top - new_top) * factor)
            weights = jnp.exp2((scores - new_top) * factor)
            part_sum = jnp.sum(weights, axis=1, keepdims=True)
            part = jnp.dot(weights.astype(BF16), v, preferred_element_type=F32)
            top[h] = new_top
            if first:
                total[h] = part_sum
                acc[h] = part
            else:
                total[h] = total[h] * shrink + part_sum
                acc[h] = acc[h] * shrink + part

    block(z, True)

    def body(i, carry):
        kb = z - 1 - i

        @pl.when(doc_smem[kb, NY - 1, rows - 1] >= first_doc)
        def _():
            block(kb, False)

        return carry

    lax.fori_loop(0, z, body, 0)
    for h in range(heads):
        out_ref[:, h * head_dim : (h + 1) * head_dim] = (acc[h] / total[h]).astype(BF16)
    low_ref[...] = lax.dot_general(
        down_ref[...], out_ref[...], (((1,), (1,)), ((), ())), preferred_element_type=F32
    )


def adapt_kernel(
    nz,
    ceiling,
    sections,
    att_ref,
    low_ref,
    grad_ref,
    up_ref,
    back_ref,
    att_out,
    adapter_out,
    gdown_out,
    gup_out,
    low_src,
    low_in,
    red_src,
    red_in,
    all_buf,
    sq_src,
    sq_in,
    att_send,
    att_recv,
    low_send,
    low_recv,
    red_send,
    red_recv,
    all_send,
    all_recv,
    sq_send,
    sq_recv,
):
    z, y, t = position()
    section = lax.axis_index("section")
    count = nz * NY
    me = z * NY + y
    home = y // 2
    rows = att_out.shape[0]
    half_cols = att_ref.shape[1]
    rank = up_ref.shape[0]

    barrier = pltpu.get_barrier_semaphore()

    def greet(o, carry):
        pl.semaphore_signal(
            barrier, inc=1, device_id=dict(ctx=(me + o) % count, tp=t), device_id_type=MESH
        )
        return carry

    lax.fori_loop(1, count, greet, 0)
    for oy in range(NY):
        pl.semaphore_signal(
            barrier,
            inc=1,
            device_id=dict(ctx=z * NY + (y + oy) % NY, tp=1 - t),
            device_id_type=MESH,
        )
    for osec in range(1, sections):
        for ot in range(2):
            pl.semaphore_signal(
                barrier,
                inc=1,
                device_id=dict(section=(section + osec) % sections, tp=(t + ot) % 2),
                device_id_type=MESH,
            )
    pl.semaphore_wait(barrier, count - 1 + NY + 2 * (sections - 1))

    def low_copy(b, core):
        return remote(
            low_src.at[b],
            low_in.at[y],
            low_send.at[b, core],
            low_recv.at[y],
            ctx=z * NY + 2 * t + b,
            tp=core,
        )

    def low_own(b, core):
        return jnp.logical_and(2 * t + b == y, t == core)

    for b in range(2):
        low_src[b] = low_ref[:, b * rows : (b + 1) * rows]
    for b in range(2):
        for core in range(2):

            @pl.when(jnp.logical_not(low_own(b, core)))
            def _():
                low_copy(b, core).start()

            @pl.when(low_own(b, core))
            def _():
                low_in[y] = low_src[b]

    def att_dest(kvl):
        return att_out.at[:, pl.ds(pl.multiple_of(kvl * half_cols, half_cols), half_cols)]

    def att_copy(b):
        return remote(
            att_ref.at[pl.ds(b * rows, rows)],
            att_dest(y % 2),
            att_send.at[b],
            att_recv.at[y % 2],
            ctx=z * NY + 2 * t + b,
            tp=home,
        )

    def att_own(b):
        return jnp.logical_and(2 * t + b == y, home == t)

    for b in range(2):

        @pl.when(jnp.logical_not(att_own(b)))
        def _():
            att_copy(b).start()

        @pl.when(att_own(b))
        def _():
            att_out[:, pl.ds(pl.multiple_of((y % 2) * half_cols, half_cols), half_cols)] = att_ref[
                b * rows : (b + 1) * rows
            ]

    for src_y in range(NY):

        @pl.when(jnp.logical_or(src_y != y, home != t))
        def _():
            remote(
                low_in.at[src_y], low_in.at[src_y], low_send.at[0, 0], low_recv.at[src_y], tp=1 - t
            ).wait_recv()

    low = low_in[0]
    for src_y in range(1, NY):
        low = low + low_in[src_y]
    low = low.astype(BF16)

    for c in range(count):
        red_src[c, 0:rank, :] = jnp.dot(
            low, grad_ref[:, c * 128 : (c + 1) * 128], preferred_element_type=F32
        ).astype(BF16)

    for kvl in range(2):

        @pl.when(jnp.logical_or(2 * t + kvl != y, home != t))
        def _():
            dest = att_dest(kvl)
            remote(dest, dest, att_send.at[0], att_recv.at[kvl], tp=1 - t).wait_recv()

    down = jnp.dot(back_ref[...], att_out[...], preferred_element_type=F32)
    blocks = count // 2
    pad = jnp.zeros((8, 128), F32)
    for c in range(count):
        r0 = 8 * (c // blocks)
        c0 = 128 * (c % blocks)
        red_src[c, rank : rank + 16, :] = jnp.concatenate(
            [down[r0 : r0 + 8, c0 : c0 + 128], pad], axis=0
        ).astype(BF16)

    def red_copy(o):
        to = (me + o) % count
        return remote(
            red_src.at[to], red_in.at[o - 1], red_send.at[o - 1], red_recv.at[o - 1], ctx=to
        )

    def red_start(o, carry):
        red_copy(o).start()
        return carry

    lax.fori_loop(1, count, red_start, 0)

    adapter_out[...] = lax.dot_general(
        low, up_ref[...], (((0,), (0,)), ((), ())), preferred_element_type=F32
    ).astype(BF16)

    def red_add(o, sum_so_far):
        red_copy(o).wait_recv()
        return sum_so_far + red_in[o - 1].astype(F32)

    summed = lax.fori_loop(1, count, red_add, red_src[me].astype(F32))
    square = jnp.sum(jnp.sum(summed * summed, axis=1, keepdims=True), axis=0, keepdims=True)
    sq_src[...] = jnp.broadcast_to(square, sq_src.shape)

    peers = [(osec, ot) for osec in range(sections) for ot in range(2) if osec or ot]

    def sq_copy(i):
        osec, ot = peers[i]
        return remote(
            sq_src,
            sq_in.at[i],
            sq_send.at[i],
            sq_recv.at[i],
            section=(section + osec) % sections,
            tp=(t + ot) % 2,
        )

    for i in range(len(peers)):
        sq_copy(i).start()
    squares = sq_src[...]
    for i in range(len(peers)):
        sq_copy(i).wait_recv()
        squares = squares + sq_in[i]
    high = squares.astype(BF16)
    rest = (squares - high.astype(F32)).astype(BF16)
    line = lax.broadcasted_iota(jnp.int32, (8, 128), 0)
    tail = jnp.where(line < 4, high.astype(F32), rest.astype(F32))
    all_buf[me] = jnp.concatenate([summed[: rank + 8], tail], axis=0).astype(BF16)

    def all_copy(o):
        to = (me + o) % count
        return remote(all_buf.at[me], all_buf.at[me], all_send.at[o - 1], all_recv.at[o - 1], ctx=to)

    def all_arrive(o):
        of = (me - o + count) % count
        return remote(all_buf.at[of], all_buf.at[of], all_send.at[o - 1], all_recv.at[o - 1], ctx=of)

    def all_start(o, carry):
        all_copy(o).start()
        return carry

    lax.fori_loop(1, count, all_start, 0)

    def all_wait(o, carry):
        all_arrive(o).wait_recv()
        return carry

    lax.fori_loop(1, count, all_wait, 0)
    norm = jnp.zeros((8, 128), F32)
    for c in range(count):
        norm = norm + all_buf[c, rank : rank + 16, :].astype(F32)[8:]
    total = norm[0:1, 0:1] + norm[4:5, 0:1]
    clip = jnp.minimum(1.0, ceiling / (jnp.sqrt(total) + 1e-06))
    for c in range(count):
        r0 = 8 * (c // blocks)
        c0 = 128 * (c % blocks)
        gup_out[:, c * 128 : (c + 1) * 128] = all_buf[c, 0:rank, :].astype(F32) * clip
        gdown_out[r0 : r0 + 8, c0 : c0 + 128] = (
            all_buf[c, rank : rank + 16, :].astype(F32)[:8] * clip
        )

    def drain(o, carry):
        red_copy(o).wait_send()
        all_copy(o).wait_send()
        return carry

    lax.fori_loop(1, count, drain, 0)
    for i in range(len(peers)):
        sq_copy(i).wait_send()
    for b in range(2):

        @pl.when(jnp.logical_not(att_own(b)))
        def _():
            att_copy(b).wait_send()

        for core in range(2):

            @pl.when(jnp.logical_not(low_own(b, core)))
            def _():
                low_copy(b, core).wait_send()


def rope_tables(positions, head_dim):
    freqs = 1000000.0 ** (-jnp.arange(head_dim // 2, dtype=F32) * 2.0 / head_dim)
    angles = positions.astype(F32)[:, None] * freqs[None, :]
    cosine, sine = jnp.cos(angles), jnp.sin(angles)
    return jnp.concatenate([cosine, cosine], axis=1), jnp.concatenate([-sine, sine], axis=1)


def per_device(hidden, gain, queries, key_value_weight, adapt_down, adapt_up, out_grad, doc_ids):
    nz = lax.axis_size("ctx") // NY
    sections = lax.axis_size("section")
    rows, width = hidden.shape[1:]
    depth, kv_count = key_value_weight.shape[1:3]
    head_dim = key_value_weight.shape[-1]
    heads = queries.shape[2]
    group = heads // kv_count
    rank, local_query = adapt_down.shape[1:]
    toks = 2 * rows
    z, y, t = position()

    start = (z * 2 + t) * toks
    home_start = (z * NY + y) * rows
    cos_k, sin_k = rope_tables(start + jnp.arange(toks, dtype=jnp.int32), head_dim)
    cos_q, sin_q = rope_tables(home_start + jnp.arange(rows, dtype=jnp.int32), head_dim)
    q = queries[0].astype(F32)
    turned = jnp.concatenate([q[..., head_dim // 2 :], q[..., : head_dim // 2]], axis=-1)
    q = (q * cos_q[:, None, :] + turned * sin_q[:, None, :]).astype(BF16)
    q = q.reshape(rows, kv_count, group, head_dim).transpose(1, 2, 0, 3)
    w = key_value_weight[0].transpose(2, 0, 1, 3).reshape(2, depth, kv_count * head_dim)
    docs = jnp.broadcast_to(doc_ids[None, :], (8, rows))

    vmem = pl.BlockSpec(memory_space=pltpu.VMEM)
    smem = pl.BlockSpec(memory_space=pltpu.SMEM)
    dma = pltpu.SemaphoreType.DMA
    steps = nz // 2
    v_type = BF16
    q_all, k_all, v_all, doc_all, back, down = pl.pallas_call(
        lambda *refs: gather_kernel(nz, *refs),
        out_shape=(
            jax.ShapeDtypeStruct((group, toks, head_dim), BF16),
            jax.ShapeDtypeStruct((nz, 2, toks, head_dim), BF16),
            jax.ShapeDtypeStruct((nz, 2, toks, head_dim), BF16),
            jax.ShapeDtypeStruct((nz, 8, rows), jnp.int32),
            jax.ShapeDtypeStruct((rank, rows), BF16),
            jax.ShapeDtypeStruct((rank, local_query // 2), BF16),
        ),
        in_specs=[vmem] * 10,
        out_specs=[vmem] * 6,
        scratch_shapes=[
            pltpu.VMEM((2, 2, nz * depth, kv_count * head_dim), BF16),
            pltpu.VMEM((NY, rows, depth * nz // 2), BF16),
            pltpu.VMEM((toks, depth * nz), BF16),
            pltpu.VMEM((rows, 128), F32),
            pltpu.VMEM((rows, 128), F32),
            pltpu.VMEM((rank, rows), F32),
            pltpu.VMEM((rank, rows), F32),
            pltpu.VMEM((2, rank, local_query), BF16),
            pltpu.VMEM((NY - 1, 8, rows), jnp.int32),
            pltpu.VMEM((NY, toks, head_dim), F32),
            pltpu.VMEM((NY - 1, toks, head_dim), F32),
            pltpu.VMEM((NY, toks, head_dim), v_type),
            pltpu.VMEM((NY - 1, toks, head_dim), v_type),
            dma((2, 2, steps)),
            dma((2, 2, steps)),
            dma((2, nz)),
            dma((2, nz)),
            dma((2, 2, steps)),
            dma((2, 2, steps)),
            dma((2, nz)),
            dma((2, nz)),
            dma((2, steps)),
            dma((2, steps)),
            dma((NY,)),
            dma((2, 2)),
            dma((2,)),
            dma((2,)),
            dma((2, NY - 1)),
            dma((2, NY - 1)),
            dma((NY - 1,)),
            dma((NY - 1,)),
            dma((3,)),
            dma((3,)),
        ],
        compiler_params=pltpu.CompilerParams(collective_id=0, has_side_effects=True),
        name="gather",
    )(hidden[0], gain, w, q, cos_k, sin_k, out_grad[0], adapt_up[0], adapt_down[0], docs)

    keys = NY * rows
    attended, low = pl.pallas_call(
        attend_kernel,
        out_shape=(
            jax.ShapeDtypeStruct((toks, group * head_dim), BF16),
            jax.ShapeDtypeStruct((rank, toks), F32),
        ),
        in_specs=[vmem, vmem, vmem, vmem, smem, vmem],
        out_specs=[vmem, vmem],
        scratch_shapes=[
            pltpu.VMEM((group, toks, 1), F32),
            pltpu.VMEM((group, toks, 1), F32),
            pltpu.VMEM((group, toks, head_dim), F32),
        ],
        name="attend",
    )(
        q_all,
        k_all.reshape(nz, keys, head_dim),
        v_all.reshape(nz, keys, head_dim),
        doc_all,
        doc_all,
        down,
    )

    count = nz * NY
    chunk = rank + 16
    ceiling = 0.5 * math.sqrt(sections * rank * (local_query + width) * 2)
    peers = 2 * sections - 1
    return pl.pallas_call(
        lambda *refs: adapt_kernel(nz, ceiling, sections, *refs),
        out_shape=(
            jax.ShapeDtypeStruct((rows, local_query), BF16),
            jax.ShapeDtypeStruct((rows, width), BF16),
            jax.ShapeDtypeStruct((rank, local_query), F32),
            jax.ShapeDtypeStruct((rank, width), F32),
        ),
        in_specs=[vmem] * 5,
        out_specs=[vmem] * 4,
        scratch_shapes=[
            pltpu.VMEM((2, rank, rows), F32),
            pltpu.VMEM((NY, rank, rows), F32),
            pltpu.VMEM((count, chunk, 128), BF16),
            pltpu.VMEM((count - 1, chunk, 128), BF16),
            pltpu.VMEM((count, chunk, 128), BF16),
            pltpu.VMEM((8, 128), F32),
            pltpu.VMEM((peers, 8, 128), F32),
            dma((2,)),
            dma((2,)),
            dma((2, 2)),
            dma((NY,)),
            dma((count - 1,)),
            dma((count - 1,)),
            dma((count - 1,)),
            dma((count - 1,)),
            dma((peers,)),
            dma((peers,)),
        ],
        compiler_params=pltpu.CompilerParams(collective_id=1, has_side_effects=True),
        name="adapt",
    )(attended, low, out_grad[0], adapt_up[0], back)


def solution(mesh):
    def step(*args):
        return tuple(out[None] for out in per_device(*args))

    return jax.shard_map(
        step,
        mesh=mesh,
        in_specs=(
            P("section", "ctx", "tp"),
            P("section", "tp"),
            P("section", "ctx", "tp", None),
            P("section", "ctx", "tp", None, None),
            P("section", None, "tp"),
            P("section", None, "tp"),
            P("section", "ctx", "tp"),
            P("ctx"),
        ),
        out_specs=(
            P("section", "ctx", "tp"),
            P("section", "ctx", "tp"),
            P("section", None, "tp"),
            P("section", None, "tp"),
        ),
        check_vma=False,
    )
```

```python
import math

import jax
import jax.numpy as jnp
from jax import lax
from jax.experimental import pallas as pl
from jax.experimental.pallas import tpu as pltpu
from jax.sharding import PartitionSpec as P

MESH = pl.DeviceIdType.MESH
NY = 4
F32 = jnp.float32
BF16 = jnp.bfloat16


def remote(src, dst, send_sem, recv_sem, **where):
    return pltpu.make_async_remote_copy(
        src_ref=src,
        dst_ref=dst,
        send_sem=send_sem,
        recv_sem=recv_sem,
        device_id=where,
        device_id_type=MESH,
    )


def position():
    ctx = lax.axis_index("ctx")
    return ctx // NY, ctx % NY, lax.axis_index("tp")


class Ring:
    def __init__(self, nz, block, half, send, recv, sib_send=None, sib_recv=None):
        self.nz, self.steps = nz, nz // 2
        self.block, self.half = block, half
        self.send, self.recv = send, recv
        self.sib_send, self.sib_recv = sib_send, sib_recv
        self.z, self.y, self.t = position()

    def origin(self, d, s):
        return (self.z - s + self.nz) % self.nz if d == 0 else (self.z + s) % self.nz

    def neighbour(self, d):
        z = (self.z + 1) % self.nz if d == 0 else (self.z + self.nz - 1) % self.nz
        return dict(ctx=z * NY + self.y, tp=self.t)

    def piece(self, zi, d, s):
        return self.half(zi, d, self.t) if s == self.steps else self.block(zi, self.t)

    def hop(self, d, s, src=None):
        piece = self.piece(self.origin(d, s - 1), d, s)
        return remote(
            piece if src is None else src,
            piece,
            self.send.at[d, s - 1],
            self.recv.at[d, s - 1],
            **self.neighbour(d),
        )

    def arrival(self, d, s):
        piece = self.piece(self.origin(d, s), d, s)
        return remote(
            piece, piece, self.send.at[d, s - 1], self.recv.at[d, s - 1], **self.neighbour(d)
        )

    def aside(self, index, zi, core, src=None):
        piece = self.block(zi, core)
        return remote(
            piece if src is None else src,
            piece,
            self.sib_send.at[index],
            self.sib_recv.at[index],
            tp=1 - self.t,
        )

    def start(self, src=None):
        for d in (0, 1):
            self.hop(d, 1, src).start()
        if self.sib_send is not None:
            self.aside(0, self.z, self.t, src).start()

    def step(self, s):
        for d in (0, 1):
            self.arrival(d, s).wait_recv()
            self.hop(d, s + 1).start()
            if self.sib_send is not None:
                self.aside(2 * s - 1 + d, self.origin(d, s), self.t).start()

    def final(self):
        for d in (0, 1):
            self.arrival(d, self.steps).wait_recv()
        if self.sib_send is not None:
            self.aside(self.nz - 1, self.origin(0, self.steps), self.t).start()

    def asides(self):
        yield 0, self.z
        for s in range(1, self.steps):
            for d in (0, 1):
                yield 2 * s - 1 + d, self.origin(d, s)
        yield self.nz - 1, self.origin(0, self.steps)

    def wait_aside(self, index, zi):
        self.aside(index, zi, 1 - self.t).wait_recv()

    def wait_sibling(self):
        for index, zi in self.asides():
            self.wait_aside(index, zi)

    def drain(self):
        for d in (0, 1):
            for s in range(1, self.steps + 1):
                self.hop(d, s).wait_send()
        if self.sib_send is not None:
            for index, zi in self.asides():
                self.aside(index, zi, self.t).wait_send()


def main_kernel(
    nz,
    sections,
    hid_ref,
    gain_ref,
    w_ref,
    q_ref,
    cos_ref,
    sin_ref,
    grad_ref,
    up_ref,
    down_ref,
    doc_ref,
    att_out,
    low_out,
    all_buf,
    sq_all,
    w_buf,
    normed,
    x_buf,
    square_src,
    square_in,
    back_part,
    back_in,
    back_own,
    back_all,
    down_buf,
    doc_in,
    doc_all,
    k_part,
    k_in,
    v_part,
    v_in,
    k_all,
    v_all,
    q_all,
    bias_ref,
    top,
    total,
    acc,
    att,
    low_src,
    low_in,
    red_src,
    red_in,
    dred_src,
    dred_in,
    sq_src,
    sq_in,
    w_send,
    w_recv,
    ws_send,
    ws_recv,
    kv_send,
    kv_recv,
    kvs_send,
    kvs_recv,
    d_send,
    d_recv,
    x_send,
    x_recv,
    q_send,
    q_recv,
    rs_send,
    rs_recv,
    dy_send,
    dy_recv,
    pair_send,
    pair_recv,
    back_send,
    back_recv,
    att_send,
    att_recv,
    low_send,
    low_recv,
    red_send,
    red_recv,
    dred_send,
    dred_recv,
    all_send,
    all_recv,
    sq_send,
    sq_recv,
    sqa_send,
    sqa_recv,
):
    z, y, t = position()
    section = lax.axis_index("section")
    rows, width = hid_ref.shape
    depth = w_ref.shape[1]
    cols = depth * nz // 2
    head_dim = k_all.shape[-1]
    heads = q_all.shape[0]
    toks = 2 * rows
    keys = 2 * toks
    rank = up_ref.shape[0]
    count = nz * NY
    me = z * NY + y
    steps = nz // 2
    home = y // 2
    sibling = dict(tp=1 - t)
    peers = [(osec, ot) for osec in range(sections) for ot in range(2) if osec or ot]

    barrier = pltpu.get_barrier_semaphore()

    def greet(**where):
        pl.semaphore_signal(barrier, inc=1, device_id=where, device_id_type=MESH)

    greet(ctx=(z + 1) % nz * NY + y)
    greet(ctx=(z + nz - 1) % nz * NY + y)
    for oy in range(NY):
        for ot in range(2):
            if oy or ot:
                greet(ctx=z * NY + (y + oy) % NY, tp=(t + ot) % 2)
    for osec, ot in peers:
        if osec:
            greet(section=(section + osec) % sections, tp=(t + ot) % 2)
    pl.semaphore_wait(barrier, 2 + 2 * NY - 1 + 2 * (sections - 1))

    def w_block(p):
        return lambda zi, core: w_buf.at[p, core, pl.ds(pl.multiple_of(zi * depth, depth), depth)]

    def w_half(p):
        return lambda zi, h, core: w_buf.at[
            p, core, pl.ds(pl.multiple_of(zi * depth + h * (depth // 2), depth // 2), depth // 2)
        ]

    def kv_block(buf):
        return lambda zi, core: buf.at[zi, core]

    def kv_half(buf):
        size = buf.shape[2] // 2
        return lambda zi, h, core: buf.at[zi, core, pl.ds(h * size, size)]

    w_rings = [
        Ring(nz, w_block(p), w_half(p), w_send.at[p], w_recv.at[p], ws_send.at[p], ws_recv.at[p])
        for p in (0, 1)
    ]
    kv_rings = [
        Ring(nz, kv_block(buf), kv_half(buf), kv_send.at[p], kv_recv.at[p], kvs_send.at[p], kvs_recv.at[p])
        for p, buf in ((0, k_all), (1, v_all))
    ]

    w_rings[0].start(w_ref.at[0])
    w_rings[1].start(w_ref.at[1])

    doc_own = doc_in.at[0]
    doc_in[0] = jnp.broadcast_to(doc_ref[...], doc_in.shape[1:])

    def doc_copy(oy):
        return remote(
            doc_own,
            doc_in.at[oy],
            dy_send.at[oy - 1],
            dy_recv.at[oy - 1],
            ctx=z * NY + (y + oy) % NY,
        )

    for oy in range(1, NY):
        doc_copy(oy).start()

    def down_copy(core):
        return remote(down_ref, down_buf.at[core], pair_send.at[0], pair_recv.at[0], **sibling)

    hid = hid_ref[...].astype(F32)
    square = jnp.sum(hid * hid, axis=1, keepdims=True)
    square_src[...] = jnp.broadcast_to(square, square_src.shape)
    square_copy = remote(square_src, square_in, pair_send.at[1], pair_recv.at[1], **sibling)
    square_copy.start()
    down_copy(t).start()
    down_buf[t] = down_ref[...]
    own_rows = pl.ds(pl.multiple_of(z * depth, depth), depth)
    w_buf[0, t, own_rows, :] = w_ref[0]
    w_buf[1, t, own_rows, :] = w_ref[1]
    square_copy.wait_recv()
    mean = (square_src[:, :1] + square_in[:, :1]) * (1.0 / (2 * width))
    scale = lax.rsqrt(mean + 1e-06)

    def x_dest(b, core):
        return x_buf.at[pl.ds(b * rows, rows), pl.ds(pl.multiple_of(core * cols, cols), cols)]

    def x_copy(oy):
        yd = (y + oy) % NY
        return remote(
            normed.at[yd],
            x_dest(y % 2, t),
            x_send.at[oy],
            x_recv.at[y % 2, t],
            ctx=z * NY + yd,
            tp=home,
        )

    for yd in range(NY):
        for zl in range(nz // 2):
            start = (zl * NY + yd) * depth
            piece = hid_ref[:, start : start + depth].astype(F32)
            gain = gain_ref[:, start : start + depth].astype(F32)
            normed[yd, :, zl * depth : (zl + 1) * depth] = (piece * scale * gain).astype(BF16)
    for oy in range(1, NY):
        x_copy(oy).start()

    @pl.when(t != home)
    def _():
        x_copy(0).start()

    @pl.when(t == home)
    def _():
        x_buf[
            pl.ds(pl.multiple_of((y % 2) * rows, rows), rows),
            pl.ds(pl.multiple_of(t * cols, cols), cols),
        ] = normed[y]

    def q_dest(b):
        return q_all.at[:, pl.ds(b * rows, rows)]

    def q_copy(kvl):
        return remote(
            q_ref.at[kvl],
            q_dest(y % 2),
            q_send.at[kvl],
            q_recv.at[y % 2],
            ctx=z * NY + 2 * t + kvl,
            tp=home,
        )

    def home_own(kvl):
        return jnp.logical_and(2 * t + kvl == y, home == t)

    for kvl in range(2):

        @pl.when(jnp.logical_not(home_own(kvl)))
        def _():
            q_copy(kvl).start()

        @pl.when(home_own(kvl))
        def _():
            q_all[:, pl.ds(pl.multiple_of((y % 2) * rows, rows), rows), :] = q_ref[kvl]

    for oy in range(1, NY):
        doc_copy(oy).wait_recv()
    line = lax.broadcasted_iota(jnp.int32, doc_in.shape[1:], 0)
    group = jnp.where(line == y, doc_in[0], 0)
    for oy in range(1, NY):
        group = jnp.where(line == (y + NY - oy) % NY, doc_in[oy], group)
    doc_all[z] = group

    def doc_pass(d, s):
        zi = (z - s + 1 + nz) % nz if d == 0 else (z + s - 1) % nz
        to = (z + 1) % nz if d == 0 else (z + nz - 1) % nz
        return remote(
            doc_all.at[zi], doc_all.at[zi], d_send.at[d, s - 1], d_recv.at[d, s - 1], ctx=to * NY + y
        )

    def doc_arrive(d, s):
        zi = (z - s + nz) % nz if d == 0 else (z + s) % nz
        to = (z + 1) % nz if d == 0 else (z + nz - 1) % nz
        return remote(
            doc_all.at[zi], doc_all.at[zi], d_send.at[d, s - 1], d_recv.at[d, s - 1], ctx=to * NY + y
        )

    doc_hops = [(0, s) for s in range(1, steps + 1)] + [(1, s) for s in range(1, steps)]

    def doc_step(s):
        for d in (0, 1):
            if (d, s) in doc_hops:
                doc_arrive(d, s).wait_recv()
                if (d, s + 1) in doc_hops:
                    doc_pass(d, s + 1).start()

    for d in (0, 1):
        if (d, 1) in doc_hops:
            doc_pass(d, 1).start()

    back_part[...] = lax.dot_general(
        up_ref[...], grad_ref[...], (((1,), (1,)), ((), ())), preferred_element_type=F32
    )
    back_copy = remote(back_part, back_in, pair_send.at[2], pair_recv.at[2], **sibling)
    back_copy.start()

    def back_pass(oy):
        return remote(
            back_own,
            back_all.at[y % 2],
            back_send.at[oy - 1],
            back_recv.at[y % 2],
            ctx=z * NY + (y + oy) % NY,
        )

    for s in range(1, steps):
        w_rings[0].step(s)
        w_rings[1].step(s)
        doc_step(s)
        if s == 1:
            back_copy.wait_recv()
            back_own[...] = (back_part[...] + back_in[...]).astype(BF16)

            @pl.when(t == home)
            def _():
                for oy in range(1, NY):
                    back_pass(oy).start()
                back_all[y % 2] = back_own[...]

    def x_wait():
        for b in range(2):
            for core in range(2):

                @pl.when(jnp.logical_or(2 * t + b != y, t != core))
                def _():
                    dest = x_dest(b, core)
                    remote(dest, dest, x_send.at[0], x_recv.at[b, core], **sibling).wait_recv()

    def project(p, part):
        for core in range(2):
            partial = jnp.dot(x_buf[...], w_buf[p, core], preferred_element_type=F32)
            for hl in range(2):
                part[2 * core + hl] = partial[:, hl * head_dim : (hl + 1) * head_dim].astype(part.dtype)

    def scatter_copy(p, oy):
        part, into = ((k_part, k_in), (v_part, v_in))[p]
        yd = (y + oy) % NY
        return remote(
            part.at[yd],
            into.at[oy - 1],
            rs_send.at[p, oy - 1],
            rs_recv.at[p, oy - 1],
            ctx=z * NY + yd,
        )

    def collect(p):
        part, into = ((k_part, k_in), (v_part, v_in))[p]
        for oy in range(1, NY):
            scatter_copy(p, oy).wait_recv()
        whole = part[y].astype(F32)
        for oy in range(1, NY):
            whole = whole + into[oy - 1].astype(F32)
        return whole

    def rope(v):
        return (v * cos_ref[...] + pltpu.roll(v, head_dim // 2, 1) * sin_ref[...]).astype(BF16)

    x_wait()
    w_rings[0].final()
    w_rings[0].wait_sibling()
    project(0, k_part)
    for oy in range(1, NY):
        scatter_copy(0, oy).start()
    w_rings[1].final()
    w_rings[1].wait_sibling()
    project(1, v_part)
    for oy in range(1, NY):
        scatter_copy(1, oy).start()

    for b in range(2):

        @pl.when(jnp.logical_or(2 * t + b != y, home != t))
        def _():
            dest = q_dest(b)
            remote(dest, dest, q_send.at[0], q_recv.at[b], **sibling).wait_recv()

    for h in range(heads):
        q_all[h] = rope(q_all[h].astype(F32))
    doc_step(steps)
    q_doc = jnp.concatenate(
        [
            jnp.sum(jnp.where(line == 2 * t + b, doc_all[z].astype(F32), 0.0), axis=0, keepdims=True)
            for b in range(2)
        ],
        axis=1,
    )

    k_all[z, t] = rope(collect(0))
    kv_rings[0].start()
    v_all[z, t] = jnp.transpose(collect(1)).astype(BF16)
    kv_rings[1].start()

    factor = head_dim ** (-0.5) * math.log2(math.e)

    def block(kb, first):
        turned = jnp.transpose(doc_all[kb].astype(F32))
        k_doc = jnp.concatenate([turned[:, j : j + 1] for j in range(NY)], axis=0)
        allowed = k_doc == q_doc
        if first:
            q_pos = t * toks + lax.broadcasted_iota(jnp.int32, (keys, toks), 1)
            k_pos = lax.broadcasted_iota(jnp.int32, (keys, toks), 0)
            allowed = jnp.logical_and(allowed, k_pos <= q_pos)
        bias_ref[...] = jnp.where(allowed, 0.0, -1e30)

        def head(h):
            q = q_all[h]
            scores = [
                lax.dot_general(
                    k_all[kb, core], q, (((1,), (1,)), ((), ())), preferred_element_type=F32
                )
                + bias_ref[core * toks : (core + 1) * toks, :]
                for core in range(2)
            ]
            peak = jnp.maximum(
                jnp.max(scores[0], axis=0, keepdims=True), jnp.max(scores[1], axis=0, keepdims=True)
            )
            if first:
                new_top = peak
            else:
                old_top = top[h]
                new_top = jnp.maximum(old_top, peak)
                shrink = jnp.exp2((old_top - new_top) * factor)
            weights = [jnp.exp2((s - new_top) * factor) for s in scores]
            part_sum = jnp.sum(weights[0], axis=0, keepdims=True) + jnp.sum(
                weights[1], axis=0, keepdims=True
            )
            part = jnp.dot(
                v_all[kb, 0], weights[0].astype(BF16), preferred_element_type=F32
            ) + jnp.dot(v_all[kb, 1], weights[1].astype(BF16), preferred_element_type=F32)
            top[h] = new_top
            if first:
                total[h] = part_sum
                acc[h] = part
            else:
                total[h] = total[h] * shrink + part_sum
                acc[h] = acc[h] * shrink + part

        def pair(i, carry):
            head(2 * i)
            head(2 * i + 1)
            return carry

        lax.fori_loop(0, heads // 2, pair, 0)

    def await_aside(index, zi):
        for ring in kv_rings:
            ring.wait_aside(index, zi)

    def attend_step(s):
        for d in (0, 1):
            zi = kv_rings[0].origin(d, s)
            await_aside(2 * s - 1 + d, zi)

            @pl.when(zi < z)
            def _():
                block(zi, False)

    await_aside(0, z)
    block(z, True)
    for s in range(1, steps):
        kv_rings[0].step(s)
        kv_rings[1].step(s)
        if s > 1:
            attend_step(s - 1)
    if steps > 1:
        attend_step(steps - 1)
    kv_rings[0].final()
    kv_rings[1].final()
    last = kv_rings[0].origin(0, steps)
    await_aside(nz - 1, last)

    @pl.when(last < z)
    def _():
        block(last, False)

    down_copy(1 - t).wait_recv()
    half_cols = heads * head_dim
    low = None
    for h in range(heads):
        out = acc[h] / total[h]
        factor_cols = down_buf[
            home, :, pl.ds(pl.multiple_of((y % 2) * half_cols + h * head_dim, head_dim), head_dim)
        ]
        part = jnp.dot(factor_cols, out.astype(BF16), preferred_element_type=F32)
        low = part if low is None else low + part
        att[:, h * head_dim : (h + 1) * head_dim] = jnp.transpose(out).astype(BF16)

    def low_copy(b, core):
        return remote(
            low_src.at[b],
            low_in.at[y],
            low_send.at[b, core],
            low_recv.at[y],
            ctx=z * NY + 2 * t + b,
            tp=core,
        )

    def low_own(b, core):
        return jnp.logical_and(2 * t + b == y, t == core)

    for b in range(2):
        low_src[b] = low[:, b * rows : (b + 1) * rows]
    for b in range(2):
        for core in range(2):

            @pl.when(jnp.logical_not(low_own(b, core)))
            def _():
                low_copy(b, core).start()

            @pl.when(low_own(b, core))
            def _():
                low_in[y] = low_src[b]

    for b in range(2):

        @pl.when(2 * t + b != y)
        def _():
            remote(
                back_all.at[b], back_all.at[b], back_send.at[0], back_recv.at[b], **sibling
            ).wait_recv()

    back = jnp.concatenate([back_all[0], back_all[1]], axis=1)
    down_part = jnp.dot(back, att[...], preferred_element_type=F32)
    for r in range(2):
        for h in range(heads):
            dred_src[r * heads + h] = down_part[8 * r : 8 * r + 8, h * 128 : (h + 1) * 128].astype(BF16)
    blocks = count // 2

    def dred_owner(i):
        return (i // heads) * blocks + (y % 2) * heads + i % heads

    def dred_copy(i):
        return remote(
            dred_src.at[i],
            dred_in.at[2 * z + t],
            dred_send.at[i],
            dred_recv.at[2 * z + t],
            ctx=dred_owner(i),
            tp=home,
        )

    def dred_own(i):
        return jnp.logical_and(dred_owner(i) == me, home == t)

    def dred_start(i, carry):
        @pl.when(jnp.logical_not(dred_own(i)))
        def _():
            dred_copy(i).start()

        @pl.when(dred_own(i))
        def _():
            dred_in[2 * z + t] = dred_src[i]

        return carry

    lax.fori_loop(0, 2 * heads, dred_start, 0)

    for src_y in range(NY):

        @pl.when(jnp.logical_or(src_y != y, home != t))
        def _():
            remote(
                low_in.at[src_y], low_in.at[src_y], low_send.at[0, 0], low_recv.at[src_y], **sibling
            ).wait_recv()

    low = low_in[0]
    for src_y in range(1, NY):
        low = low + low_in[src_y]
    low = low.astype(BF16)
    low_out[...] = low

    for c in range(count):
        red_src[c] = jnp.dot(
            low, grad_ref[:, c * 128 : (c + 1) * 128], preferred_element_type=F32
        ).astype(BF16)

    def red_copy(o):
        to = (me + o) % count
        return remote(
            red_src.at[to], red_in.at[o - 1], red_send.at[o - 1], red_recv.at[o - 1], ctx=to
        )

    def red_start(o, carry):
        red_copy(o).start()
        return carry

    lax.fori_loop(1, count, red_start, 0)

    def att_dest(kvl):
        return att_out.at[:, pl.ds(pl.multiple_of(kvl * half_cols, half_cols), half_cols)]

    def att_copy(b):
        return remote(
            att.at[pl.ds(b * rows, rows)],
            att_dest(y % 2),
            att_send.at[b],
            att_recv.at[y % 2],
            ctx=z * NY + 2 * t + b,
            tp=home,
        )

    for b in range(2):

        @pl.when(jnp.logical_not(home_own(b)))
        def _():
            att_copy(b).start()

        @pl.when(home_own(b))
        def _():
            att_out[:, pl.ds(pl.multiple_of((y % 2) * half_cols, half_cols), half_cols)] = att[
                b * rows : (b + 1) * rows
            ]

    down_y = 2 * t + (me % blocks) // heads

    def dred_add(i, carry):
        @pl.when(jnp.logical_or(down_y != y, i != 2 * z + t))
        def _():
            remote(
                dred_in.at[i], dred_in.at[i], dred_send.at[0], dred_recv.at[i], **sibling
            ).wait_recv()

        return carry + dred_in[i].astype(F32)

    down_sum = lax.fori_loop(0, 2 * nz, dred_add, jnp.zeros((8, 128), F32))

    def red_add(o, so_far):
        red_copy(o).wait_recv()
        return so_far + red_in[o - 1].astype(F32)

    up_sum = lax.fori_loop(1, count, red_add, red_src[me].astype(F32))
    all_buf[me] = jnp.concatenate([up_sum, down_sum], axis=0).astype(BF16)
    squares = jnp.sum(up_sum * up_sum, axis=0, keepdims=True) + jnp.sum(
        down_sum * down_sum, axis=0, keepdims=True
    )
    sq_src[...] = jnp.broadcast_to(jnp.sum(squares, axis=1, keepdims=True), sq_src.shape)

    def sq_copy(i):
        osec, ot = peers[i]
        return remote(
            sq_src,
            sq_in.at[i],
            sq_send.at[i],
            sq_recv.at[i],
            section=(section + osec) % sections,
            tp=(t + ot) % 2,
        )

    for i in range(len(peers)):
        sq_copy(i).start()

    def spread(buf, sends, recvs):
        def copy(o):
            to = (me + o) % count
            return remote(buf.at[me], buf.at[me], sends.at[o - 1], recvs.at[o - 1], ctx=to)

        def arrive(o):
            of = (me - o + count) % count
            return remote(buf.at[of], buf.at[of], sends.at[o - 1], recvs.at[o - 1], ctx=of)

        def each(act):
            def one(o, carry):
                act(o)
                return carry

            lax.fori_loop(1, count, one, 0)

        return (
            lambda: each(lambda o: copy(o).start()),
            lambda: each(lambda o: arrive(o).wait_recv()),
            lambda: each(lambda o: copy(o).wait_send()),
        )

    all_start, all_wait, all_drain = spread(all_buf, all_send, all_recv)
    sqa_start, sqa_wait, sqa_drain = spread(sq_all, sqa_send, sqa_recv)
    all_start()
    squares = sq_src[...]
    for i in range(len(peers)):
        sq_copy(i).wait_recv()
        squares = squares + sq_in[i]
    sq_all[me] = squares
    sqa_start()

    for ring in w_rings + kv_rings:
        ring.drain()
    for oy in range(1, NY):
        doc_copy(oy).wait_send()
        x_copy(oy).wait_send()
        scatter_copy(0, oy).wait_send()
        scatter_copy(1, oy).wait_send()

    @pl.when(t != home)
    def _():
        x_copy(0).wait_send()

    @pl.when(t == home)
    def _():
        for oy in range(1, NY):
            back_pass(oy).wait_send()

    for d, s in doc_hops:
        doc_pass(d, s).wait_send()
    down_copy(t).wait_send()
    square_copy.wait_send()
    back_copy.wait_send()
    for b in range(2):

        @pl.when(jnp.logical_not(home_own(b)))
        def _():
            q_copy(b).wait_send()
            att_copy(b).wait_send()

        for core in range(2):

            @pl.when(jnp.logical_not(low_own(b, core)))
            def _():
                low_copy(b, core).wait_send()

    def dred_drain(i, carry):
        @pl.when(jnp.logical_not(dred_own(i)))
        def _():
            dred_copy(i).wait_send()

        return carry

    lax.fori_loop(0, 2 * heads, dred_drain, 0)

    def red_drain(o, carry):
        red_copy(o).wait_send()
        return carry

    lax.fori_loop(1, count, red_drain, 0)
    for kvl in range(2):

        @pl.when(jnp.logical_or(2 * t + kvl != y, home != t))
        def _():
            dest = att_dest(kvl)
            remote(dest, dest, att_send.at[0], att_recv.at[kvl], **sibling).wait_recv()

    all_wait()
    all_drain()
    for i in range(len(peers)):
        sq_copy(i).wait_send()
    sqa_wait()
    sqa_drain()


def finish_kernel(ceiling, att_ref, low_ref, all_ref, sq_ref, up_ref, att_out, adapter_out, gdown_out, gup_out):
    count = all_ref.shape[0]
    rank = low_ref.shape[0]
    blocks = count // 2
    norm = sq_ref[0]
    for c in range(1, count):
        norm = norm + sq_ref[c]
    clip = jnp.minimum(1.0, ceiling / (jnp.sqrt(norm[0:1, 0:1]) + 1e-06))
    for c in range(count):
        r0 = 8 * (c // blocks)
        c0 = 128 * (c % blocks)
        gup_out[:, c * 128 : (c + 1) * 128] = all_ref[c, 0:rank, :].astype(F32) * clip
        gdown_out[r0 : r0 + 8, c0 : c0 + 128] = all_ref[c, rank : rank + 8, :].astype(F32) * clip
    att_out[...] = att_ref[...]
    adapter_out[...] = lax.dot_general(
        low_ref[...], up_ref[...], (((0,), (0,)), ((), ())), preferred_element_type=F32
    ).astype(BF16)


def rope_tables(positions, head_dim):
    lane = jnp.arange(head_dim, dtype=jnp.int32)
    half = head_dim // 2
    freqs = 1000000.0 ** (-(lane % half).astype(F32) * 2.0 / head_dim)
    angles = positions.astype(F32)[:, None] * freqs[None, :]
    return jnp.cos(angles), jnp.where(lane[None, :] < half, -jnp.sin(angles), jnp.sin(angles))


def per_device(hidden, gain, queries, key_value_weight, adapt_down, adapt_up, out_grad, doc_ids):
    nz = lax.axis_size("ctx") // NY
    sections = lax.axis_size("section")
    rows, width = hidden.shape[1:]
    depth, kv_count = key_value_weight.shape[1:3]
    head_dim = key_value_weight.shape[-1]
    heads = queries.shape[2]
    group = heads // kv_count
    rank, local_query = adapt_down.shape[1:]
    toks = 2 * rows
    z, y, t = position()

    start = (z * 2 + t) * toks
    cos, sin = rope_tables(start + jnp.arange(toks, dtype=jnp.int32), head_dim)
    q = queries[0].transpose(1, 0, 2).reshape(kv_count, group, rows, head_dim)
    w = key_value_weight[0].transpose(2, 0, 1, 3).reshape(2, depth, kv_count * head_dim)

    vmem = pl.BlockSpec(memory_space=pltpu.VMEM)
    dma = pltpu.SemaphoreType.DMA
    steps = nz // 2
    count = nz * NY
    peers = 2 * sections - 1
    chunk = rank + 8
    att, low, summed, squares = pl.pallas_call(
        lambda *refs: main_kernel(nz, sections, *refs),
        out_shape=(
            jax.ShapeDtypeStruct((rows, local_query), BF16),
            jax.ShapeDtypeStruct((rank, rows), BF16),
            jax.ShapeDtypeStruct((count, chunk, 128), BF16),
            jax.ShapeDtypeStruct((count, 8, 128), F32),
        ),
        in_specs=[vmem] * 10,
        out_specs=[vmem] * 4,
        scratch_shapes=[
            pltpu.VMEM((2, 2, nz * depth, kv_count * head_dim), BF16),
            pltpu.VMEM((NY, rows, depth * nz // 2), BF16),
            pltpu.VMEM((toks, depth * nz), BF16),
            pltpu.VMEM((rows, 128), F32),
            pltpu.VMEM((rows, 128), F32),
            pltpu.VMEM((rank, rows), F32),
            pltpu.VMEM((rank, rows), F32),
            pltpu.VMEM((rank, rows), BF16),
            pltpu.VMEM((2, rank, rows), BF16),
            pltpu.VMEM((2, rank, local_query), BF16),
            pltpu.VMEM((NY, 8, rows), jnp.int32),
            pltpu.VMEM((nz, 8, rows), jnp.int32),
            pltpu.VMEM((NY, toks, head_dim), F32),
            pltpu.VMEM((NY - 1, toks, head_dim), F32),
            pltpu.VMEM((NY, toks, head_dim), BF16),
            pltpu.VMEM((NY - 1, toks, head_dim), BF16),
            pltpu.VMEM((nz, 2, toks, head_dim), BF16),
            pltpu.VMEM((nz, 2, head_dim, toks), BF16),
            pltpu.VMEM((group, toks, head_dim), BF16),
            pltpu.VMEM((2 * toks, toks), F32),
            pltpu.VMEM((group, 1, toks), F32),
            pltpu.VMEM((group, 1, toks), F32),
            pltpu.VMEM((group, head_dim, toks), F32),
            pltpu.VMEM((toks, group * head_dim), BF16),
            pltpu.VMEM((2, rank, rows), F32),
            pltpu.VMEM((NY, rank, rows), F32),
            pltpu.VMEM((count, rank, 128), BF16),
            pltpu.VMEM((count - 1, rank, 128), BF16),
            pltpu.VMEM((2 * group, 8, 128), BF16),
            pltpu.VMEM((2 * nz, 8, 128), BF16),
            pltpu.VMEM((8, 128), F32),
            pltpu.VMEM((peers, 8, 128), F32),
            dma((2, 2, steps)),
            dma((2, 2, steps)),
            dma((2, nz)),
            dma((2, nz)),
            dma((2, 2, steps)),
            dma((2, 2, steps)),
            dma((2, nz)),
            dma((2, nz)),
            dma((2, steps)),
            dma((2, steps)),
            dma((NY,)),
            dma((2, 2)),
            dma((2,)),
            dma((2,)),
            dma((2, NY - 1)),
            dma((2, NY - 1)),
            dma((NY - 1,)),
            dma((NY - 1,)),
            dma((3,)),
            dma((3,)),
            dma((NY - 1,)),
            dma((2,)),
            dma((2,)),
            dma((2,)),
            dma((2, 2)),
            dma((NY,)),
            dma((count - 1,)),
            dma((count - 1,)),
            dma((2 * group,)),
            dma((2 * nz,)),
            dma((count - 1,)),
            dma((count - 1,)),
            dma((peers,)),
            dma((peers,)),
            dma((count - 1,)),
            dma((count - 1,)),
        ],
        compiler_params=pltpu.CompilerParams(collective_id=0, has_side_effects=True),
        name="main",
    )(hidden[0], gain, w, q, cos, sin, out_grad[0], adapt_up[0], adapt_down[0], doc_ids[None])

    ceiling = 0.5 * math.sqrt(sections * rank * (local_query + width) * 2)
    return pl.pallas_call(
        lambda *refs: finish_kernel(ceiling, *refs),
        out_shape=(
            jax.ShapeDtypeStruct((rows, local_query), BF16),
            jax.ShapeDtypeStruct((rows, width), BF16),
            jax.ShapeDtypeStruct((rank, local_query), F32),
            jax.ShapeDtypeStruct((rank, width), F32),
        ),
        in_specs=[vmem] * 5,
        out_specs=[vmem] * 4,
        name="finish",
    )(att, low, summed, squares, adapt_up[0])


def solution(mesh):
    def step(*args):
        return tuple(out[None] for out in per_device(*args))

    return jax.shard_map(
        step,
        mesh=mesh,
        in_specs=(
            P("section", "ctx", "tp"),
            P("section", "tp"),
            P("section", "ctx", "tp", None),
            P("section", "ctx", "tp", None, None),
            P("section", None, "tp"),
            P("section", None, "tp"),
            P("section", "ctx", "tp"),
            P("ctx"),
        ),
        out_specs=(
            P("section", "ctx", "tp"),
            P("section", "ctx", "tp"),
            P("section", None, "tp"),
            P("section", None, "tp"),
        ),
        check_vma=False,
    )
```

```python
import math

import jax
import jax.numpy as jnp
from jax import lax
from jax.experimental import pallas as pl
from jax.experimental.pallas import tpu as pltpu
from jax.sharding import PartitionSpec as P

MESH = pl.DeviceIdType.MESH
NY = 4
F32 = jnp.float32
BF16 = jnp.bfloat16


def remote(src, dst, send_sem, recv_sem, **where):
    return pltpu.make_async_remote_copy(
        src_ref=src,
        dst_ref=dst,
        send_sem=send_sem,
        recv_sem=recv_sem,
        device_id=where,
        device_id_type=MESH,
    )


def position():
    ctx = lax.axis_index("ctx")
    return ctx // NY, ctx % NY, lax.axis_index("tp")


class Ring:
    def __init__(self, nz, block, half, send, recv, sib_send=None, sib_recv=None):
        self.nz, self.steps = nz, nz // 2
        self.block, self.half = block, half
        self.send, self.recv = send, recv
        self.sib_send, self.sib_recv = sib_send, sib_recv
        self.z, self.y, self.t = position()

    def origin(self, d, s):
        return (self.z - s + self.nz) % self.nz if d == 0 else (self.z + s) % self.nz

    def neighbour(self, d):
        z = (self.z + 1) % self.nz if d == 0 else (self.z + self.nz - 1) % self.nz
        return dict(ctx=z * NY + self.y, tp=self.t)

    def piece(self, zi, d, s):
        return self.half(zi, d, self.t) if s == self.steps else self.block(zi, self.t)

    def hop(self, d, s, src=None):
        piece = self.piece(self.origin(d, s - 1), d, s)
        return remote(
            piece if src is None else src,
            piece,
            self.send.at[d, s - 1],
            self.recv.at[d, s - 1],
            **self.neighbour(d),
        )

    def arrival(self, d, s):
        piece = self.piece(self.origin(d, s), d, s)
        return remote(
            piece, piece, self.send.at[d, s - 1], self.recv.at[d, s - 1], **self.neighbour(d)
        )

    def aside(self, index, zi, core, src=None):
        piece = self.block(zi, core)
        return remote(
            piece if src is None else src,
            piece,
            self.sib_send.at[index],
            self.sib_recv.at[index],
            tp=1 - self.t,
        )

    def start(self, src=None):
        for d in (0, 1):
            self.hop(d, 1, src).start()
        if self.sib_send is not None:
            self.aside(0, self.z, self.t, src).start()

    def step(self, s):
        for d in (0, 1):
            self.arrival(d, s).wait_recv()
            self.hop(d, s + 1).start()
            if self.sib_send is not None:
                self.aside(2 * s - 1 + d, self.origin(d, s), self.t).start()

    def final(self):
        for d in (0, 1):
            self.arrival(d, self.steps).wait_recv()
        if self.sib_send is not None:
            self.aside(self.nz - 1, self.origin(0, self.steps), self.t).start()

    def asides(self):
        yield 0, self.z
        for s in range(1, self.steps):
            for d in (0, 1):
                yield 2 * s - 1 + d, self.origin(d, s)
        yield self.nz - 1, self.origin(0, self.steps)

    def wait_aside(self, index, zi):
        self.aside(index, zi, 1 - self.t).wait_recv()

    def wait_sibling(self):
        for index, zi in self.asides():
            self.wait_aside(index, zi)

    def drain(self):
        for d in (0, 1):
            for s in range(1, self.steps + 1):
                self.hop(d, s).wait_send()
        if self.sib_send is not None:
            for index, zi in self.asides():
                self.aside(index, zi, self.t).wait_send()


def main_kernel(
    nz,
    sections,
    hid_hbm,
    gain_ref,
    w_ref,
    q_hbm,
    freq_ref,
    grad_hbm,
    up_hbm,
    down_hbm,
    doc_ref,
    att_out,
    low_out,
    all_buf,
    sq_all,
    hid_ref,
    q_raw,
    q_ref,
    grad_ref,
    up_ref,
    down_ref,
    cos_ref,
    sin_ref,
    w_buf,
    normed,
    x_buf,
    square_src,
    square_in,
    back_part,
    back_in,
    back_own,
    back_all,
    down_buf,
    doc_in,
    doc_all,
    k_part,
    k_in,
    v_part,
    v_in,
    k_all,
    v_all,
    q_all,
    bias_ref,
    top,
    total,
    acc,
    att,
    low_src,
    low_in,
    red_src,
    red_in,
    dred_src,
    dred_in,
    sq_src,
    sq_in,
    w_send,
    w_recv,
    ws_send,
    ws_recv,
    kv_send,
    kv_recv,
    kvs_send,
    kvs_recv,
    d_send,
    d_recv,
    x_send,
    x_recv,
    q_send,
    q_recv,
    rs_send,
    rs_recv,
    dy_send,
    dy_recv,
    pair_send,
    pair_recv,
    back_send,
    back_recv,
    att_send,
    att_recv,
    low_send,
    low_recv,
    red_send,
    red_recv,
    dred_send,
    dred_recv,
    all_send,
    all_recv,
    sq_send,
    sq_recv,
    sqa_send,
    sqa_recv,
    load_sem,
    own_sem,
):
    z, y, t = position()
    section = lax.axis_index("section")
    rows, width = hid_ref.shape
    depth = w_ref.shape[1]
    cols = depth * nz // 2
    head_dim = k_all.shape[-1]
    heads = q_all.shape[0]
    toks = 2 * rows
    keys = 2 * toks
    rank = up_ref.shape[0]
    count = nz * NY
    me = z * NY + y
    steps = nz // 2
    home = y // 2
    sibling = dict(tp=1 - t)
    peers = [(osec, ot) for osec in range(sections) for ot in range(2) if osec or ot]

    barrier = pltpu.get_barrier_semaphore()

    def greet(**where):
        pl.semaphore_signal(barrier, inc=1, device_id=where, device_id_type=MESH)

    greet(ctx=(z + 1) % nz * NY + y)
    greet(ctx=(z + nz - 1) % nz * NY + y)
    for oy in range(NY):
        for ot in range(2):
            if oy or ot:
                greet(ctx=z * NY + (y + oy) % NY, tp=(t + ot) % 2)
    for osec, ot in peers:
        if osec:
            greet(section=(section + osec) % sections, tp=(t + ot) % 2)
    slab = rows // 4
    hid_loads = [
        pltpu.make_async_copy(
            hid_hbm.at[pl.ds(i * slab, slab)], hid_ref.at[pl.ds(i * slab, slab)], load_sem.at[i]
        )
        for i in range(4)
    ]
    late_loads = [
        pltpu.make_async_copy(src, dst, load_sem.at[4 + i])
        for i, (src, dst) in enumerate(
            ((q_hbm, q_raw), (grad_hbm, grad_ref), (up_hbm, up_ref), (down_hbm, down_ref))
        )
    ]
    for load in hid_loads:
        load.start()
    pl.semaphore_wait(barrier, 2 + 2 * NY - 1 + 2 * (sections - 1))

    def w_block(p):
        return lambda zi, core: w_buf.at[p, core, pl.ds(pl.multiple_of(zi * depth, depth), depth)]

    def w_half(p):
        return lambda zi, h, core: w_buf.at[
            p, core, pl.ds(pl.multiple_of(zi * depth + h * (depth // 2), depth // 2), depth // 2)
        ]

    def kv_block(buf):
        return lambda zi, core: buf.at[zi, core]

    def kv_half(buf):
        size = buf.shape[2] // 2
        return lambda zi, h, core: buf.at[zi, core, pl.ds(h * size, size)]

    w_rings = [
        Ring(nz, w_block(p), w_half(p), w_send.at[p], w_recv.at[p], ws_send.at[p], ws_recv.at[p])
        for p in (0, 1)
    ]
    kv_rings = [
        Ring(nz, kv_block(buf), kv_half(buf), kv_send.at[p], kv_recv.at[p], kvs_send.at[p], kvs_recv.at[p])
        for p, buf in ((0, k_all), (1, v_all))
    ]

    w_rings[0].start(w_ref.at[0])
    w_rings[1].start(w_ref.at[1])
    own_rows = pl.ds(pl.multiple_of(z * depth, depth), depth)
    own_loads = [
        pltpu.make_async_copy(w_ref.at[p], w_buf.at[p, t, own_rows], own_sem.at[p]) for p in (0, 1)
    ]
    for load in late_loads + own_loads:
        load.start()

    doc_own = doc_in.at[0]
    doc_in[0] = jnp.broadcast_to(doc_ref[...], doc_in.shape[1:])

    def doc_copy(oy):
        return remote(
            doc_own,
            doc_in.at[oy],
            dy_send.at[oy - 1],
            dy_recv.at[oy - 1],
            ctx=z * NY + (y + oy) % NY,
        )

    for oy in range(1, NY):
        doc_copy(oy).start()

    def down_copy(core):
        return remote(down_ref, down_buf.at[core], pair_send.at[0], pair_recv.at[0], **sibling)

    for i, load in enumerate(hid_loads):
        load.wait()
        hid = hid_ref[i * slab : (i + 1) * slab, :].astype(F32)
        square = jnp.sum(hid * hid, axis=1, keepdims=True)
        square_src[i * slab : (i + 1) * slab, :] = jnp.broadcast_to(square, (slab, 128))
    square_copy = remote(square_src, square_in, pair_send.at[1], pair_recv.at[1], **sibling)
    square_copy.start()
    square_copy.wait_recv()
    mean = (square_src[:, :1] + square_in[:, :1]) * (1.0 / (2 * width))
    scale = lax.rsqrt(mean + 1e-06)

    def x_dest(b, core):
        return x_buf.at[pl.ds(b * rows, rows), pl.ds(pl.multiple_of(core * cols, cols), cols)]

    def x_copy(oy):
        yd = (y + oy) % NY
        return remote(
            normed.at[yd],
            x_dest(y % 2, t),
            x_send.at[oy],
            x_recv.at[y % 2, t],
            ctx=z * NY + yd,
            tp=home,
        )

    for yd in range(NY):
        for zl in range(nz // 2):
            start = (zl * NY + yd) * depth
            piece = hid_ref[:, start : start + depth].astype(F32)
            gain = gain_ref[:, start : start + depth].astype(F32)
            normed[yd, :, zl * depth : (zl + 1) * depth] = (piece * scale * gain).astype(BF16)
    for oy in range(1, NY):
        x_copy(oy).start()

    @pl.when(t != home)
    def _():
        x_copy(0).start()

    @pl.when(t == home)
    def _():
        x_buf[
            pl.ds(pl.multiple_of((y % 2) * rows, rows), rows),
            pl.ds(pl.multiple_of(t * cols, cols), cols),
        ] = normed[y]

    late_loads[0].wait()
    turned_q = jnp.transpose(q_raw[...].astype(F32), (1, 0, 2)).astype(BF16)
    q_ref[...] = turned_q.reshape(q_ref.shape)

    def q_dest(b):
        return q_all.at[:, pl.ds(b * rows, rows)]

    def q_copy(kvl):
        return remote(
            q_ref.at[kvl],
            q_dest(y % 2),
            q_send.at[kvl],
            q_recv.at[y % 2],
            ctx=z * NY + 2 * t + kvl,
            tp=home,
        )

    def home_own(kvl):
        return jnp.logical_and(2 * t + kvl == y, home == t)

    for kvl in range(2):

        @pl.when(jnp.logical_not(home_own(kvl)))
        def _():
            q_copy(kvl).start()

        @pl.when(home_own(kvl))
        def _():
            q_all[:, pl.ds(pl.multiple_of((y % 2) * rows, rows), rows), :] = q_ref[kvl]

    for oy in range(1, NY):
        doc_copy(oy).wait_recv()
    line = lax.broadcasted_iota(jnp.int32, doc_in.shape[1:], 0)
    group = jnp.where(line == y, doc_in[0], 0)
    for oy in range(1, NY):
        group = jnp.where(line == (y + NY - oy) % NY, doc_in[oy], group)
    doc_all[z] = group

    def doc_pass(d, s):
        zi = (z - s + 1 + nz) % nz if d == 0 else (z + s - 1) % nz
        to = (z + 1) % nz if d == 0 else (z + nz - 1) % nz
        return remote(
            doc_all.at[zi], doc_all.at[zi], d_send.at[d, s - 1], d_recv.at[d, s - 1], ctx=to * NY + y
        )

    def doc_arrive(d, s):
        zi = (z - s + nz) % nz if d == 0 else (z + s) % nz
        to = (z + 1) % nz if d == 0 else (z + nz - 1) % nz
        return remote(
            doc_all.at[zi], doc_all.at[zi], d_send.at[d, s - 1], d_recv.at[d, s - 1], ctx=to * NY + y
        )

    doc_hops = [(0, s) for s in range(1, steps + 1)] + [(1, s) for s in range(1, steps)]

    def doc_step(s):
        for d in (0, 1):
            if (d, s) in doc_hops:
                doc_arrive(d, s).wait_recv()
                if (d, s + 1) in doc_hops:
                    doc_pass(d, s + 1).start()

    for d in (0, 1):
        if (d, 1) in doc_hops:
            doc_pass(d, 1).start()

    late_loads[3].wait()
    down_copy(t).start()
    down_buf[t] = down_ref[...]
    late_loads[1].wait()
    late_loads[2].wait()
    back_part[...] = lax.dot_general(
        up_ref[...], grad_ref[...], (((1,), (1,)), ((), ())), preferred_element_type=F32
    )
    back_copy = remote(back_part, back_in, pair_send.at[2], pair_recv.at[2], **sibling)
    back_copy.start()

    def back_pass(oy):
        return remote(
            back_own,
            back_all.at[y % 2],
            back_send.at[oy - 1],
            back_recv.at[y % 2],
            ctx=z * NY + (y + oy) % NY,
        )

    for s in range(1, steps):
        w_rings[0].step(s)
        w_rings[1].step(s)
        doc_step(s)
        if s == 2:
            lane = lax.broadcasted_iota(jnp.int32, cos_ref.shape, 1)
            token = lax.broadcasted_iota(jnp.int32, cos_ref.shape, 0) + (z * 2 + t) * toks
            angles = token.astype(F32) * freq_ref[...]
            cos_ref[...] = jnp.cos(angles)
            sine = jnp.sin(angles)
            sin_ref[...] = jnp.where(lane < head_dim // 2, -sine, sine)
        if s == 1:
            back_copy.wait_recv()
            back_own[...] = (back_part[...] + back_in[...]).astype(BF16)

            @pl.when(t == home)
            def _():
                for oy in range(1, NY):
                    back_pass(oy).start()
                back_all[y % 2] = back_own[...]

    def x_wait():
        for b in range(2):
            for core in range(2):

                @pl.when(jnp.logical_or(2 * t + b != y, t != core))
                def _():
                    dest = x_dest(b, core)
                    remote(dest, dest, x_send.at[0], x_recv.at[b, core], **sibling).wait_recv()

    def project(p, part):
        for core in range(2):
            partial = jnp.dot(x_buf[...], w_buf[p, core], preferred_element_type=F32)
            for hl in range(2):
                part[2 * core + hl] = partial[:, hl * head_dim : (hl + 1) * head_dim].astype(part.dtype)

    def scatter_copy(p, oy):
        part, into = ((k_part, k_in), (v_part, v_in))[p]
        yd = (y + oy) % NY
        return remote(
            part.at[yd],
            into.at[oy - 1],
            rs_send.at[p, oy - 1],
            rs_recv.at[p, oy - 1],
            ctx=z * NY + yd,
        )

    def collect(p):
        part, into = ((k_part, k_in), (v_part, v_in))[p]
        for oy in range(1, NY):
            scatter_copy(p, oy).wait_recv()
        whole = part[y].astype(F32)
        for oy in range(1, NY):
            whole = whole + into[oy - 1].astype(F32)
        return whole

    def rope(v):
        return (v * cos_ref[...] + pltpu.roll(v, head_dim // 2, 1) * sin_ref[...]).astype(BF16)

    x_wait()
    for load in own_loads:
        load.wait()
    w_rings[0].final()
    w_rings[0].wait_sibling()
    project(0, k_part)
    for oy in range(1, NY):
        scatter_copy(0, oy).start()
    w_rings[1].final()
    w_rings[1].wait_sibling()
    project(1, v_part)
    for oy in range(1, NY):
        scatter_copy(1, oy).start()

    for b in range(2):

        @pl.when(jnp.logical_or(2 * t + b != y, home != t))
        def _():
            dest = q_dest(b)
            remote(dest, dest, q_send.at[0], q_recv.at[b], **sibling).wait_recv()

    for h in range(heads):
        q_all[h] = rope(q_all[h].astype(F32))
    doc_step(steps)
    q_doc = jnp.concatenate(
        [
            jnp.sum(jnp.where(line == 2 * t + b, doc_all[z].astype(F32), 0.0), axis=0, keepdims=True)
            for b in range(2)
        ],
        axis=1,
    )

    k_all[z, t] = rope(collect(0))
    kv_rings[0].start()
    v_all[z, t] = jnp.transpose(collect(1)).astype(BF16)
    kv_rings[1].start()

    factor = head_dim ** (-0.5) * math.log2(math.e)

    def block(kb, first):
        turned = jnp.transpose(doc_all[kb].astype(F32))
        k_doc = jnp.concatenate([turned[:, j : j + 1] for j in range(NY)], axis=0)
        allowed = k_doc == q_doc
        if first:
            q_pos = t * toks + lax.broadcasted_iota(jnp.int32, (keys, toks), 1)
            k_pos = lax.broadcasted_iota(jnp.int32, (keys, toks), 0)
            allowed = jnp.logical_and(allowed, k_pos <= q_pos)
        bias_ref[...] = jnp.where(allowed, 0.0, -1e30)

        def head(h):
            q = q_all[h]
            scores = [
                lax.dot_general(
                    k_all[kb, core], q, (((1,), (1,)), ((), ())), preferred_element_type=F32
                )
                + bias_ref[core * toks : (core + 1) * toks, :]
                for core in range(2)
            ]
            peak = jnp.maximum(
                jnp.max(scores[0], axis=0, keepdims=True), jnp.max(scores[1], axis=0, keepdims=True)
            )
            if first:
                new_top = peak
            else:
                old_top = top[h]
                new_top = jnp.maximum(old_top, peak)
                shrink = jnp.exp2((old_top - new_top) * factor)
            weights = [jnp.exp2((s - new_top) * factor) for s in scores]
            part_sum = jnp.sum(weights[0], axis=0, keepdims=True) + jnp.sum(
                weights[1], axis=0, keepdims=True
            )
            part = jnp.dot(
                v_all[kb, 0], weights[0].astype(BF16), preferred_element_type=F32
            ) + jnp.dot(v_all[kb, 1], weights[1].astype(BF16), preferred_element_type=F32)
            top[h] = new_top
            if first:
                total[h] = part_sum
                acc[h] = part
            else:
                total[h] = total[h] * shrink + part_sum
                acc[h] = acc[h] * shrink + part

        for h in range(heads):
            head(h)

    def await_aside(index, zi):
        for ring in kv_rings:
            ring.wait_aside(index, zi)

    def attend_step(s):
        def one(d, carry):
            zi = jnp.where(d == 0, z - s + nz, z + s) % nz
            await_aside(2 * s - 1 + d, zi)

            @pl.when(zi < z)
            def _():
                block(zi, False)

            return carry

        lax.fori_loop(0, 2, one, 0)

    await_aside(0, z)
    block(z, True)
    for s in range(1, steps):
        kv_rings[0].step(s)
        kv_rings[1].step(s)
        attend_step(s)
    kv_rings[0].final()
    kv_rings[1].final()
    last = kv_rings[0].origin(0, steps)
    await_aside(nz - 1, last)

    @pl.when(last < z)
    def _():
        block(last, False)

    down_copy(1 - t).wait_recv()
    half_cols = heads * head_dim
    low = None
    for h in range(heads):
        out = acc[h] / total[h]
        factor_cols = down_buf[
            home, :, pl.ds(pl.multiple_of((y % 2) * half_cols + h * head_dim, head_dim), head_dim)
        ]
        part = jnp.dot(factor_cols, out.astype(BF16), preferred_element_type=F32)
        low = part if low is None else low + part
        att[:, h * head_dim : (h + 1) * head_dim] = jnp.transpose(out).astype(BF16)

    def low_copy(b, core):
        return remote(
            low_src.at[b],
            low_in.at[y],
            low_send.at[b, core],
            low_recv.at[y],
            ctx=z * NY + 2 * t + b,
            tp=core,
        )

    def low_own(b, core):
        return jnp.logical_and(2 * t + b == y, t == core)

    for b in range(2):
        low_src[b] = low[:, b * rows : (b + 1) * rows]
    for b in range(2):
        for core in range(2):

            @pl.when(jnp.logical_not(low_own(b, core)))
            def _():
                low_copy(b, core).start()

            @pl.when(low_own(b, core))
            def _():
                low_in[y] = low_src[b]

    for b in range(2):

        @pl.when(2 * t + b != y)
        def _():
            remote(
                back_all.at[b], back_all.at[b], back_send.at[0], back_recv.at[b], **sibling
            ).wait_recv()

    back = jnp.concatenate([back_all[0], back_all[1]], axis=1)
    down_part = jnp.dot(back, att[...], preferred_element_type=F32)
    for r in range(2):
        for h in range(heads):
            dred_src[r * heads + h] = down_part[8 * r : 8 * r + 8, h * 128 : (h + 1) * 128].astype(BF16)
    blocks = count // 2

    def dred_owner(i):
        return (i // heads) * blocks + (y % 2) * heads + i % heads

    def dred_copy(i):
        return remote(
            dred_src.at[i],
            dred_in.at[2 * z + t],
            dred_send.at[i],
            dred_recv.at[2 * z + t],
            ctx=dred_owner(i),
            tp=home,
        )

    def dred_own(i):
        return jnp.logical_and(dred_owner(i) == me, home == t)

    def dred_start(i, carry):
        @pl.when(jnp.logical_not(dred_own(i)))
        def _():
            dred_copy(i).start()

        @pl.when(dred_own(i))
        def _():
            dred_in[2 * z + t] = dred_src[i]

        return carry

    lax.fori_loop(0, 2 * heads, dred_start, 0)

    for src_y in range(NY):

        @pl.when(jnp.logical_or(src_y != y, home != t))
        def _():
            remote(
                low_in.at[src_y], low_in.at[src_y], low_send.at[0, 0], low_recv.at[src_y], **sibling
            ).wait_recv()

    low = low_in[0]
    for src_y in range(1, NY):
        low = low + low_in[src_y]
    low = low.astype(BF16)
    low_out[...] = low

    for c in range(count):
        red_src[c] = jnp.dot(
            low, grad_ref[:, c * 128 : (c + 1) * 128], preferred_element_type=F32
        ).astype(BF16)

    def red_copy(o):
        to = (me + o) % count
        return remote(
            red_src.at[to], red_in.at[o - 1], red_send.at[o - 1], red_recv.at[o - 1], ctx=to
        )

    def red_start(o, carry):
        red_copy(o).start()
        return carry

    lax.fori_loop(1, count, red_start, 0)

    def att_dest(kvl):
        return att_out.at[:, pl.ds(pl.multiple_of(kvl * half_cols, half_cols), half_cols)]

    def att_copy(b):
        return remote(
            att.at[pl.ds(b * rows, rows)],
            att_dest(y % 2),
            att_send.at[b],
            att_recv.at[y % 2],
            ctx=z * NY + 2 * t + b,
            tp=home,
        )

    for b in range(2):

        @pl.when(jnp.logical_not(home_own(b)))
        def _():
            att_copy(b).start()

        @pl.when(home_own(b))
        def _():
            att_out[:, pl.ds(pl.multiple_of((y % 2) * half_cols, half_cols), half_cols)] = att[
                b * rows : (b + 1) * rows
            ]

    down_y = 2 * t + (me % blocks) // heads

    def dred_add(i, carry):
        @pl.when(jnp.logical_or(down_y != y, i != 2 * z + t))
        def _():
            remote(
                dred_in.at[i], dred_in.at[i], dred_send.at[0], dred_recv.at[i], **sibling
            ).wait_recv()

        return carry + dred_in[i].astype(F32)

    down_sum = lax.fori_loop(0, 2 * nz, dred_add, jnp.zeros((8, 128), F32))

    def red_add(o, so_far):
        red_copy(o).wait_recv()
        return so_far + red_in[o - 1].astype(F32)

    up_sum = lax.fori_loop(1, count, red_add, red_src[me].astype(F32))
    all_buf[me] = jnp.concatenate([up_sum, down_sum], axis=0).astype(BF16)
    squares = jnp.sum(up_sum * up_sum, axis=0, keepdims=True) + jnp.sum(
        down_sum * down_sum, axis=0, keepdims=True
    )
    sq_src[...] = jnp.broadcast_to(jnp.sum(squares, axis=1, keepdims=True), sq_src.shape)

    def sq_copy(i):
        osec, ot = peers[i]
        return remote(
            sq_src,
            sq_in.at[i],
            sq_send.at[i],
            sq_recv.at[i],
            section=(section + osec) % sections,
            tp=(t + ot) % 2,
        )

    for i in range(len(peers)):
        sq_copy(i).start()

    def spread(buf, sends, recvs):
        def copy(o):
            to = (me + o) % count
            return remote(buf.at[me], buf.at[me], sends.at[o - 1], recvs.at[o - 1], ctx=to)

        def arrive(o):
            of = (me - o + count) % count
            return remote(buf.at[of], buf.at[of], sends.at[o - 1], recvs.at[o - 1], ctx=of)

        def each(act):
            def one(o, carry):
                act(o)
                return carry

            lax.fori_loop(1, count, one, 0)

        return (
            lambda: each(lambda o: copy(o).start()),
            lambda: each(lambda o: arrive(o).wait_recv()),
            lambda: each(lambda o: copy(o).wait_send()),
        )

    all_start, all_wait, all_drain = spread(all_buf, all_send, all_recv)
    sqa_start, sqa_wait, sqa_drain = spread(sq_all, sqa_send, sqa_recv)
    all_start()
    squares = sq_src[...]
    for i in range(len(peers)):
        sq_copy(i).wait_recv()
        squares = squares + sq_in[i]
    sq_all[me] = squares
    sqa_start()

    for ring in w_rings + kv_rings:
        ring.drain()
    for oy in range(1, NY):
        doc_copy(oy).wait_send()
        x_copy(oy).wait_send()
        scatter_copy(0, oy).wait_send()
        scatter_copy(1, oy).wait_send()

    @pl.when(t != home)
    def _():
        x_copy(0).wait_send()

    @pl.when(t == home)
    def _():
        for oy in range(1, NY):
            back_pass(oy).wait_send()

    for d, s in doc_hops:
        doc_pass(d, s).wait_send()
    down_copy(t).wait_send()
    square_copy.wait_send()
    back_copy.wait_send()
    for b in range(2):

        @pl.when(jnp.logical_not(home_own(b)))
        def _():
            q_copy(b).wait_send()
            att_copy(b).wait_send()

        for core in range(2):

            @pl.when(jnp.logical_not(low_own(b, core)))
            def _():
                low_copy(b, core).wait_send()

    def dred_drain(i, carry):
        @pl.when(jnp.logical_not(dred_own(i)))
        def _():
            dred_copy(i).wait_send()

        return carry

    lax.fori_loop(0, 2 * heads, dred_drain, 0)

    def red_drain(o, carry):
        red_copy(o).wait_send()
        return carry

    lax.fori_loop(1, count, red_drain, 0)
    for kvl in range(2):

        @pl.when(jnp.logical_or(2 * t + kvl != y, home != t))
        def _():
            dest = att_dest(kvl)
            remote(dest, dest, att_send.at[0], att_recv.at[kvl], **sibling).wait_recv()

    all_wait()
    all_drain()
    for i in range(len(peers)):
        sq_copy(i).wait_send()
    sqa_wait()
    sqa_drain()


def finish_kernel(
    ceiling,
    att_hbm,
    low_hbm,
    all_hbm,
    sq_hbm,
    up_hbm,
    att_out,
    adapter_out,
    gdown_out,
    gup_out,
    att_ref,
    low_ref,
    all_ref,
    sq_ref,
    up_ref,
    adapter,
    gdown,
    gup,
    in_sem,
    out_sem,
):
    count = all_ref.shape[0]
    rank, rows = low_ref.shape
    width = up_ref.shape[1]
    blocks = count // 2
    ins = [
        pltpu.make_async_copy(src, dst, in_sem.at[i])
        for i, (src, dst) in enumerate(
            (
                (low_hbm, low_ref),
                (up_hbm, up_ref),
                (sq_hbm, sq_ref),
                (all_hbm, all_ref),
                (att_hbm.at[pl.ds(0, rows // 2)], att_ref.at[pl.ds(0, rows // 2)]),
                (att_hbm.at[pl.ds(rows // 2, rows // 2)], att_ref.at[pl.ds(rows // 2, rows // 2)]),
            )
        )
    ]
    outs = []

    def put(src, dst):
        copy = pltpu.make_async_copy(src, dst, out_sem.at[len(outs)])
        copy.start()
        outs.append(copy)

    for copy in ins:
        copy.start()
    ins[0].wait()
    ins[1].wait()
    part = rows // 4
    low = jnp.transpose(low_ref[...].astype(F32)).astype(BF16)
    for i in range(4):
        adapter[i * part : (i + 1) * part, :] = jnp.dot(
            low[i * part : (i + 1) * part], up_ref[...], preferred_element_type=F32
        ).astype(BF16)
        put(adapter.at[pl.ds(i * part, part)], adapter_out.at[pl.ds(i * part, part)])
    for i in range(2):
        ins[4 + i].wait()
        half = pl.ds(i * (rows // 2), rows // 2)
        put(att_ref.at[half], att_out.at[half])
    ins[2].wait()
    ins[3].wait()
    norm = sq_ref[0]
    for c in range(1, count):
        norm = norm + sq_ref[c]
    clip = jnp.minimum(1.0, ceiling / (jnp.sqrt(norm[0:1, 0:1]) + 1e-06))
    for c in range(count):
        r0 = 8 * (c // blocks)
        c0 = 128 * (c % blocks)
        gup[:, c * 128 : (c + 1) * 128] = all_ref[c, 0:rank, :].astype(F32) * clip
        gdown[r0 : r0 + 8, c0 : c0 + 128] = all_ref[c, rank : rank + 8, :].astype(F32) * clip
    put(gup, gup_out)
    put(gdown, gdown_out)
    for copy in outs:
        copy.wait()


def per_device(hidden, gain, queries, key_value_weight, adapt_down, adapt_up, out_grad, doc_ids):
    nz = lax.axis_size("ctx") // NY
    sections = lax.axis_size("section")
    rows, width = hidden.shape[1:]
    depth, kv_count = key_value_weight.shape[1:3]
    head_dim = key_value_weight.shape[-1]
    heads = queries.shape[2]
    group = heads // kv_count
    rank, local_query = adapt_down.shape[1:]
    toks = 2 * rows
    half = head_dim // 2
    freqs = 1000000.0 ** (-jnp.arange(half, dtype=F32) * 2.0 / head_dim)
    freqs = jnp.concatenate([freqs, freqs])[None]
    w = key_value_weight[0].transpose(2, 0, 1, 3).reshape(2, depth, kv_count * head_dim)

    vmem = pl.BlockSpec(memory_space=pltpu.VMEM)
    hbm = pl.BlockSpec(memory_space=pl.ANY)
    dma = pltpu.SemaphoreType.DMA
    steps = nz // 2
    count = nz * NY
    peers = 2 * sections - 1
    chunk = rank + 8
    att, low, summed, squares = pl.pallas_call(
        lambda *refs: main_kernel(nz, sections, *refs),
        out_shape=(
            jax.ShapeDtypeStruct((rows, local_query), BF16),
            jax.ShapeDtypeStruct((rank, rows), BF16),
            jax.ShapeDtypeStruct((count, chunk, 128), BF16),
            jax.ShapeDtypeStruct((count, 8, 128), F32),
        ),
        in_specs=[hbm, vmem, hbm, hbm, vmem, hbm, hbm, hbm, vmem],
        out_specs=[vmem] * 4,
        scratch_shapes=[
            pltpu.VMEM((rows, width), BF16),
            pltpu.VMEM((rows, heads, head_dim), BF16),
            pltpu.VMEM((kv_count, group, rows, head_dim), BF16),
            pltpu.VMEM((rows, width), BF16),
            pltpu.VMEM((rank, width), BF16),
            pltpu.VMEM((rank, local_query), BF16),
            pltpu.VMEM((toks, head_dim), F32),
            pltpu.VMEM((toks, head_dim), F32),
            pltpu.VMEM((2, 2, nz * depth, kv_count * head_dim), BF16),
            pltpu.VMEM((NY, rows, depth * nz // 2), BF16),
            pltpu.VMEM((toks, depth * nz), BF16),
            pltpu.VMEM((rows, 128), F32),
            pltpu.VMEM((rows, 128), F32),
            pltpu.VMEM((rank, rows), F32),
            pltpu.VMEM((rank, rows), F32),
            pltpu.VMEM((rank, rows), BF16),
            pltpu.VMEM((2, rank, rows), BF16),
            pltpu.VMEM((2, rank, local_query), BF16),
            pltpu.VMEM((NY, 8, rows), jnp.int32),
            pltpu.VMEM((nz, 8, rows), jnp.int32),
            pltpu.VMEM((NY, toks, head_dim), F32),
            pltpu.VMEM((NY - 1, toks, head_dim), F32),
            pltpu.VMEM((NY, toks, head_dim), BF16),
            pltpu.VMEM((NY - 1, toks, head_dim), BF16),
            pltpu.VMEM((nz, 2, toks, head_dim), BF16),
            pltpu.VMEM((nz, 2, head_dim, toks), BF16),
            pltpu.VMEM((group, toks, head_dim), BF16),
            pltpu.VMEM((2 * toks, toks), F32),
            pltpu.VMEM((group, 1, toks), F32),
            pltpu.VMEM((group, 1, toks), F32),
            pltpu.VMEM((group, head_dim, toks), F32),
            pltpu.VMEM((toks, group * head_dim), BF16),
            pltpu.VMEM((2, rank, rows), F32),
            pltpu.VMEM((NY, rank, rows), F32),
            pltpu.VMEM((count, rank, 128), BF16),
            pltpu.VMEM((count - 1, rank, 128), BF16),
            pltpu.VMEM((2 * group, 8, 128), BF16),
            pltpu.VMEM((2 * nz, 8, 128), BF16),
            pltpu.VMEM((8, 128), F32),
            pltpu.VMEM((peers, 8, 128), F32),
            dma((2, 2, steps)),
            dma((2, 2, steps)),
            dma((2, nz)),
            dma((2, nz)),
            dma((2, 2, steps)),
            dma((2, 2, steps)),
            dma((2, nz)),
            dma((2, nz)),
            dma((2, steps)),
            dma((2, steps)),
            dma((NY,)),
            dma((2, 2)),
            dma((2,)),
            dma((2,)),
            dma((2, NY - 1)),
            dma((2, NY - 1)),
            dma((NY - 1,)),
            dma((NY - 1,)),
            dma((3,)),
            dma((3,)),
            dma((NY - 1,)),
            dma((2,)),
            dma((2,)),
            dma((2,)),
            dma((2, 2)),
            dma((NY,)),
            dma((count - 1,)),
            dma((count - 1,)),
            dma((2 * group,)),
            dma((2 * nz,)),
            dma((count - 1,)),
            dma((count - 1,)),
            dma((peers,)),
            dma((peers,)),
            dma((count - 1,)),
            dma((count - 1,)),
            dma((8,)),
            dma((2,)),
        ],
        compiler_params=pltpu.CompilerParams(collective_id=0, has_side_effects=True),
        name="main",
    )(
        hidden[0],
        gain,
        w,
        queries[0],
        freqs,
        out_grad[0],
        adapt_up[0],
        adapt_down[0],
        doc_ids[None],
    )

    ceiling = 0.5 * math.sqrt(sections * rank * (local_query + width) * 2)
    return pl.pallas_call(
        lambda *refs: finish_kernel(ceiling, *refs),
        out_shape=(
            jax.ShapeDtypeStruct((rows, local_query), BF16),
            jax.ShapeDtypeStruct((rows, width), BF16),
            jax.ShapeDtypeStruct((rank, local_query), F32),
            jax.ShapeDtypeStruct((rank, width), F32),
        ),
        in_specs=[hbm] * 5,
        out_specs=[hbm] * 4,
        scratch_shapes=[
            pltpu.VMEM((rows, local_query), BF16),
            pltpu.VMEM((rank, rows), BF16),
            pltpu.VMEM((count, chunk, 128), BF16),
            pltpu.VMEM((count, 8, 128), F32),
            pltpu.VMEM((rank, width), BF16),
            pltpu.VMEM((rows, width), BF16),
            pltpu.VMEM((rank, local_query), F32),
            pltpu.VMEM((rank, width), F32),
            dma((6,)),
            dma((8,)),
        ],
        name="finish",
    )(att, low, summed, squares, adapt_up[0])


def solution(mesh):
    def step(*args):
        return tuple(out[None] for out in per_device(*args))

    return jax.shard_map(
        step,
        mesh=mesh,
        in_specs=(
            P("section", "ctx", "tp"),
            P("section", "tp"),
            P("section", "ctx", "tp", None),
            P("section", "ctx", "tp", None, None),
            P("section", None, "tp"),
            P("section", None, "tp"),
            P("section", "ctx", "tp"),
            P("ctx"),
        ),
        out_specs=(
            P("section", "ctx", "tp"),
            P("section", "ctx", "tp"),
            P("section", None, "tp"),
            P("section", None, "tp"),
        ),
        check_vma=False,
    )
```

```python
import math

import jax
import jax.numpy as jnp
from jax import lax
from jax.experimental import pallas as pl
from jax.experimental.pallas import tpu as pltpu
from jax.sharding import PartitionSpec as P

MESH = pl.DeviceIdType.MESH
NY = 4
PIECE = 64
F32 = jnp.float32
BF16 = jnp.bfloat16


def remote(src, dst, send_sem, recv_sem, **where):
    return pltpu.make_async_remote_copy(
        src_ref=src,
        dst_ref=dst,
        send_sem=send_sem,
        recv_sem=recv_sem,
        device_id=where,
        device_id_type=MESH,
    )


def position():
    ctx = lax.axis_index("ctx")
    return ctx // NY, ctx % NY, lax.axis_index("tp")


class Ring:
    def __init__(self, nz, block, half, send, recv, sib_send=None, sib_recv=None):
        self.nz, self.steps = nz, nz // 2
        self.block, self.half = block, half
        self.send, self.recv = send, recv
        self.sib_send, self.sib_recv = sib_send, sib_recv
        self.z, self.y, self.t = position()

    def origin(self, d, s):
        return (self.z - s + self.nz) % self.nz if d == 0 else (self.z + s) % self.nz

    def neighbour(self, d):
        z = (self.z + 1) % self.nz if d == 0 else (self.z + self.nz - 1) % self.nz
        return dict(ctx=z * NY + self.y, tp=self.t)

    def piece(self, zi, d, s):
        return self.half(zi, d, self.t) if s == self.steps else self.block(zi, self.t)

    def hop(self, d, s, src=None):
        piece = self.piece(self.origin(d, s - 1), d, s)
        return remote(
            piece if src is None else src,
            piece,
            self.send.at[d, s - 1],
            self.recv.at[d, s - 1],
            **self.neighbour(d),
        )

    def arrival(self, d, s):
        piece = self.piece(self.origin(d, s), d, s)
        return remote(
            piece, piece, self.send.at[d, s - 1], self.recv.at[d, s - 1], **self.neighbour(d)
        )

    def aside(self, index, zi, core, src=None):
        piece = self.block(zi, core)
        return remote(
            piece if src is None else src,
            piece,
            self.sib_send.at[index],
            self.sib_recv.at[index],
            tp=1 - self.t,
        )

    def start(self, src=None):
        for d in (0, 1):
            self.hop(d, 1, src).start()
        if self.sib_send is not None:
            self.aside(0, self.z, self.t, src).start()

    def step(self, s):
        for d in (0, 1):
            self.arrival(d, s).wait_recv()
            self.hop(d, s + 1).start()
            if self.sib_send is not None:
                self.aside(2 * s - 1 + d, self.origin(d, s), self.t).start()

    def final(self):
        for d in (0, 1):
            self.arrival(d, self.steps).wait_recv()
        if self.sib_send is not None:
            self.aside(self.nz - 1, self.origin(0, self.steps), self.t).start()

    def asides(self):
        yield 0, self.z
        for s in range(1, self.steps):
            for d in (0, 1):
                yield 2 * s - 1 + d, self.origin(d, s)
        yield self.nz - 1, self.origin(0, self.steps)

    def wait_aside(self, index, zi):
        self.aside(index, zi, 1 - self.t).wait_recv()

    def wait_sibling(self):
        for index, zi in self.asides():
            self.wait_aside(index, zi)

    def drain(self):
        for d in (0, 1):
            for s in range(1, self.steps + 1):
                self.hop(d, s).wait_send()
        if self.sib_send is not None:
            for index, zi in self.asides():
                self.aside(index, zi, self.t).wait_send()


def main_kernel(
    nz,
    sections,
    hid_hbm,
    gain_ref,
    w_ref,
    q_hbm,
    freq_ref,
    grad_hbm,
    up_hbm,
    down_hbm,
    doc_ref,
    att_out,
    low_out,
    all_buf,
    sq_all,
    hid_ref,
    q_raw,
    q_ref,
    grad_ref,
    up_ref,
    down_ref,
    cos_ref,
    sin_ref,
    w_buf,
    normed,
    x_buf,
    square_src,
    square_in,
    back_part,
    back_in,
    back_own,
    back_all,
    down_buf,
    doc_in,
    doc_all,
    k_part,
    k_in,
    v_part,
    v_in,
    k_all,
    v_all,
    q_all,
    bias_ref,
    top,
    s_buf,
    p_buf,
    v_ext,
    acc,
    att,
    low_src,
    low_in,
    red_src,
    red_in,
    dred_src,
    dred_in,
    sq_src,
    sq_in,
    w_send,
    w_recv,
    ws_send,
    ws_recv,
    kv_send,
    kv_recv,
    kvs_send,
    kvs_recv,
    d_send,
    d_recv,
    x_send,
    x_recv,
    q_send,
    q_recv,
    rs_send,
    rs_recv,
    dy_send,
    dy_recv,
    pair_send,
    pair_recv,
    back_send,
    back_recv,
    att_send,
    att_recv,
    low_send,
    low_recv,
    red_send,
    red_recv,
    dred_send,
    dred_recv,
    all_send,
    all_recv,
    sq_send,
    sq_recv,
    sqa_send,
    sqa_recv,
    load_sem,
    own_sem,
):
    z, y, t = position()
    section = lax.axis_index("section")
    rows, width = hid_ref.shape
    depth = w_ref.shape[1]
    cols = depth * nz // 2
    head_dim = k_all.shape[-1]
    heads = q_all.shape[0]
    toks = 2 * rows
    keys = 2 * toks
    rank = up_ref.shape[0]
    count = nz * NY
    me = z * NY + y
    steps = nz // 2
    home = y // 2
    sibling = dict(tp=1 - t)
    peers = [(osec, ot) for osec in range(sections) for ot in range(2) if osec or ot]

    barrier = pltpu.get_barrier_semaphore()

    def greet(**where):
        pl.semaphore_signal(barrier, inc=1, device_id=where, device_id_type=MESH)

    greet(ctx=(z + 1) % nz * NY + y)
    greet(ctx=(z + nz - 1) % nz * NY + y)
    for oy in range(NY):
        for ot in range(2):
            if oy or ot:
                greet(ctx=z * NY + (y + oy) % NY, tp=(t + ot) % 2)
    for osec, ot in peers:
        if osec:
            greet(section=(section + osec) % sections, tp=(t + ot) % 2)
    slab = rows // 4
    hid_loads = [
        pltpu.make_async_copy(
            hid_hbm.at[pl.ds(i * slab, slab)], hid_ref.at[pl.ds(i * slab, slab)], load_sem.at[i]
        )
        for i in range(4)
    ]
    late_loads = [
        pltpu.make_async_copy(src, dst, load_sem.at[4 + i])
        for i, (src, dst) in enumerate(
            ((q_hbm, q_raw), (grad_hbm, grad_ref), (up_hbm, up_ref), (down_hbm, down_ref))
        )
    ]
    for load in hid_loads:
        load.start()
    pl.semaphore_wait(barrier, 2 + 2 * NY - 1 + 2 * (sections - 1))

    def w_block(p):
        return lambda zi, core: w_buf.at[p, core, pl.ds(pl.multiple_of(zi * depth, depth), depth)]

    def w_half(p):
        return lambda zi, h, core: w_buf.at[
            p, core, pl.ds(pl.multiple_of(zi * depth + h * (depth // 2), depth // 2), depth // 2)
        ]

    def kv_block(buf):
        return lambda zi, core: buf.at[zi, core]

    def kv_half(buf):
        size = buf.shape[2] // 2
        return lambda zi, h, core: buf.at[zi, core, pl.ds(h * size, size)]

    w_rings = [
        Ring(nz, w_block(p), w_half(p), w_send.at[p], w_recv.at[p], ws_send.at[p], ws_recv.at[p])
        for p in (0, 1)
    ]
    kv_rings = [
        Ring(nz, kv_block(buf), kv_half(buf), kv_send.at[p], kv_recv.at[p], kvs_send.at[p], kvs_recv.at[p])
        for p, buf in ((0, k_all), (1, v_all))
    ]

    w_rings[0].start(w_ref.at[0])
    w_rings[1].start(w_ref.at[1])
    own_rows = pl.ds(pl.multiple_of(z * depth, depth), depth)
    own_loads = [
        pltpu.make_async_copy(w_ref.at[p], w_buf.at[p, t, own_rows], own_sem.at[p]) for p in (0, 1)
    ]
    for load in late_loads + own_loads:
        load.start()

    doc_own = doc_in.at[0]
    doc_in[0] = jnp.broadcast_to(doc_ref[...], doc_in.shape[1:])

    def doc_copy(oy):
        return remote(
            doc_own,
            doc_in.at[oy],
            dy_send.at[oy - 1],
            dy_recv.at[oy - 1],
            ctx=z * NY + (y + oy) % NY,
        )

    for oy in range(1, NY):
        doc_copy(oy).start()

    def down_copy(core):
        return remote(down_ref, down_buf.at[core], pair_send.at[0], pair_recv.at[0], **sibling)

    for i, load in enumerate(hid_loads):
        load.wait()
        hid = hid_ref[i * slab : (i + 1) * slab, :].astype(F32)
        square = jnp.sum(hid * hid, axis=1, keepdims=True)
        square_src[i * slab : (i + 1) * slab, :] = jnp.broadcast_to(square, (slab, 128))
    square_copy = remote(square_src, square_in, pair_send.at[1], pair_recv.at[1], **sibling)
    square_copy.start()
    square_copy.wait_recv()
    mean = (square_src[:, :1] + square_in[:, :1]) * (1.0 / (2 * width))
    scale = lax.rsqrt(mean + 1e-06)

    def x_dest(b, core):
        return x_buf.at[pl.ds(b * rows, rows), pl.ds(pl.multiple_of(core * cols, cols), cols)]

    def x_copy(oy):
        yd = (y + oy) % NY
        return remote(
            normed.at[yd],
            x_dest(y % 2, t),
            x_send.at[oy],
            x_recv.at[y % 2, t],
            ctx=z * NY + yd,
            tp=home,
        )

    for yd in range(NY):
        for zl in range(nz // 2):
            start = (zl * NY + yd) * depth
            piece = hid_ref[:, start : start + depth].astype(F32)
            gain = gain_ref[:, start : start + depth].astype(F32)
            normed[yd, :, zl * depth : (zl + 1) * depth] = (piece * scale * gain).astype(BF16)
    for oy in range(1, NY):
        x_copy(oy).start()

    @pl.when(t != home)
    def _():
        x_copy(0).start()

    @pl.when(t == home)
    def _():
        x_buf[
            pl.ds(pl.multiple_of((y % 2) * rows, rows), rows),
            pl.ds(pl.multiple_of(t * cols, cols), cols),
        ] = normed[y]

    late_loads[0].wait()
    turned_q = jnp.transpose(q_raw[...].astype(F32), (1, 0, 2)).astype(BF16)
    q_ref[...] = turned_q.reshape(q_ref.shape)

    def q_dest(b):
        return q_all.at[:, pl.ds(b * rows, rows)]

    def q_copy(kvl):
        return remote(
            q_ref.at[kvl],
            q_dest(y % 2),
            q_send.at[kvl],
            q_recv.at[y % 2],
            ctx=z * NY + 2 * t + kvl,
            tp=home,
        )

    def home_own(kvl):
        return jnp.logical_and(2 * t + kvl == y, home == t)

    for kvl in range(2):

        @pl.when(jnp.logical_not(home_own(kvl)))
        def _():
            q_copy(kvl).start()

        @pl.when(home_own(kvl))
        def _():
            q_all[:, pl.ds(pl.multiple_of((y % 2) * rows, rows), rows), :] = q_ref[kvl]

    for oy in range(1, NY):
        doc_copy(oy).wait_recv()
    line = lax.broadcasted_iota(jnp.int32, doc_in.shape[1:], 0)
    group = jnp.where(line == y, doc_in[0], 0)
    for oy in range(1, NY):
        group = jnp.where(line == (y + NY - oy) % NY, doc_in[oy], group)
    doc_all[z] = group

    def doc_pass(d, s):
        zi = (z - s + 1 + nz) % nz if d == 0 else (z + s - 1) % nz
        to = (z + 1) % nz if d == 0 else (z + nz - 1) % nz
        return remote(
            doc_all.at[zi], doc_all.at[zi], d_send.at[d, s - 1], d_recv.at[d, s - 1], ctx=to * NY + y
        )

    def doc_arrive(d, s):
        zi = (z - s + nz) % nz if d == 0 else (z + s) % nz
        to = (z + 1) % nz if d == 0 else (z + nz - 1) % nz
        return remote(
            doc_all.at[zi], doc_all.at[zi], d_send.at[d, s - 1], d_recv.at[d, s - 1], ctx=to * NY + y
        )

    doc_hops = [(0, s) for s in range(1, steps + 1)] + [(1, s) for s in range(1, steps)]

    def doc_step(s):
        for d in (0, 1):
            if (d, s) in doc_hops:
                doc_arrive(d, s).wait_recv()
                if (d, s + 1) in doc_hops:
                    doc_pass(d, s + 1).start()

    for d in (0, 1):
        if (d, 1) in doc_hops:
            doc_pass(d, 1).start()

    late_loads[3].wait()
    down_copy(t).start()
    down_buf[t] = down_ref[...]
    late_loads[1].wait()
    late_loads[2].wait()
    back_part[...] = lax.dot_general(
        up_ref[...], grad_ref[...], (((1,), (1,)), ((), ())), preferred_element_type=F32
    )
    back_copy = remote(back_part, back_in, pair_send.at[2], pair_recv.at[2], **sibling)
    back_copy.start()

    def back_pass(oy):
        return remote(
            back_own,
            back_all.at[y % 2],
            back_send.at[oy - 1],
            back_recv.at[y % 2],
            ctx=z * NY + (y + oy) % NY,
        )

    for s in range(1, steps):
        w_rings[0].step(s)
        w_rings[1].step(s)
        doc_step(s)
        if s == 2:
            lane = lax.broadcasted_iota(jnp.int32, cos_ref.shape, 1)
            token = lax.broadcasted_iota(jnp.int32, cos_ref.shape, 0) + (z * 2 + t) * toks
            angles = token.astype(F32) * freq_ref[...]
            cos_ref[...] = jnp.cos(angles)
            sine = jnp.sin(angles)
            sin_ref[...] = jnp.where(lane < head_dim // 2, -sine, sine)
        if s == 1:
            back_copy.wait_recv()
            back_own[...] = (back_part[...] + back_in[...]).astype(BF16)

            @pl.when(t == home)
            def _():
                for oy in range(1, NY):
                    back_pass(oy).start()
                back_all[y % 2] = back_own[...]

    def x_wait():
        for b in range(2):
            for core in range(2):

                @pl.when(jnp.logical_or(2 * t + b != y, t != core))
                def _():
                    dest = x_dest(b, core)
                    remote(dest, dest, x_send.at[0], x_recv.at[b, core], **sibling).wait_recv()

    def project(p, part):
        for core in range(2):
            partial = jnp.dot(x_buf[...], w_buf[p, core], preferred_element_type=F32)
            for hl in range(2):
                part[2 * core + hl] = partial[:, hl * head_dim : (hl + 1) * head_dim].astype(part.dtype)

    def scatter_copy(p, oy):
        part, into = ((k_part, k_in), (v_part, v_in))[p]
        yd = (y + oy) % NY
        return remote(
            part.at[yd],
            into.at[oy - 1],
            rs_send.at[p, oy - 1],
            rs_recv.at[p, oy - 1],
            ctx=z * NY + yd,
        )

    def collect(p):
        part, into = ((k_part, k_in), (v_part, v_in))[p]
        for oy in range(1, NY):
            scatter_copy(p, oy).wait_recv()
        whole = part[y].astype(F32)
        for oy in range(1, NY):
            whole = whole + into[oy - 1].astype(F32)
        return whole

    def rope(v):
        return (v * cos_ref[...] + pltpu.roll(v, head_dim // 2, 1) * sin_ref[...]).astype(BF16)

    x_wait()
    for load in own_loads:
        load.wait()
    w_rings[0].final()
    w_rings[0].wait_sibling()
    project(0, k_part)
    for oy in range(1, NY):
        scatter_copy(0, oy).start()
    w_rings[1].final()
    w_rings[1].wait_sibling()
    project(1, v_part)
    for oy in range(1, NY):
        scatter_copy(1, oy).start()

    for b in range(2):

        @pl.when(jnp.logical_or(2 * t + b != y, home != t))
        def _():
            dest = q_dest(b)
            remote(dest, dest, q_send.at[0], q_recv.at[b], **sibling).wait_recv()

    for h in range(heads):
        q_all[h] = rope(q_all[h].astype(F32))
    doc_step(steps)
    q_doc = jnp.concatenate(
        [
            jnp.sum(jnp.where(line == 2 * t + b, doc_all[z].astype(F32), 0.0), axis=0, keepdims=True)
            for b in range(2)
        ],
        axis=1,
    )

    k_all[z, t] = rope(collect(0))
    kv_rings[0].start()
    v_all[z, t] = jnp.transpose(collect(1)).astype(BF16)
    kv_rings[1].start()

    factor = head_dim ** (-0.5) * math.log2(math.e)

    def block(kb, first):
        turned = jnp.transpose(doc_all[kb].astype(F32))
        k_doc = jnp.concatenate([turned[:, j : j + 1] for j in range(NY)], axis=0)
        allowed = k_doc == q_doc
        if first:
            q_pos = t * toks + lax.broadcasted_iota(jnp.int32, (keys, toks), 1)
            k_pos = lax.broadcasted_iota(jnp.int32, (keys, toks), 0)
            allowed = jnp.logical_and(allowed, k_pos <= q_pos)
        bias_ref[...] = jnp.where(allowed, 0.0, -1e30)

        for core in range(2):
            v_ext[:head_dim, core * toks : (core + 1) * toks] = v_all[kb, core]

        tops, shrinks = {}, {}

        def score(h):
            q = q_all[h]
            slot = h % 2
            peak = None
            for core in range(2):
                scores = (
                    lax.dot_general(
                        k_all[kb, core], q, (((1,), (1,)), ((), ())), preferred_element_type=F32
                    )
                    + bias_ref[core * toks : (core + 1) * toks, :]
                )
                s_buf[slot, core] = scores
                here = jnp.max(scores, axis=0, keepdims=True)
                peak = here if peak is None else jnp.maximum(peak, here)
            if not first:
                old_top = top[h]
                peak = jnp.maximum(old_top, peak)
                shrinks[h] = jnp.exp2((old_top - peak) * factor)
            top[h] = peak
            tops[h] = peak

        def weigh(h):
            slot = h % 2
            for core in range(2):
                for r in range(0, toks, PIECE):
                    p_buf[slot, core * toks + r : core * toks + r + PIECE, :] = jnp.exp2(
                        (s_buf[slot, core, r : r + PIECE, :] - tops[h]) * factor
                    ).astype(BF16)

        def mix(h):
            slot = h % 2
            part = jnp.dot(v_ext[...], p_buf[slot], preferred_element_type=F32)[: head_dim + 8]
            acc[h] = part if first else acc[h] * shrinks[h] + part

        for i in range(heads + 2):
            if i < heads:
                score(i)
            if 0 <= i - 1 < heads:
                weigh(i - 1)
            if i >= 2:
                mix(i - 2)

    def await_aside(index, zi):
        for ring in kv_rings:
            ring.wait_aside(index, zi)

    def attend_step(s):
        def one(d, carry):
            zi = jnp.where(d == 0, z - s + nz, z + s) % nz
            await_aside(2 * s - 1 + d, zi)

            @pl.when(zi < z)
            def _():
                block(zi, False)

            return carry

        lax.fori_loop(0, 2, one, 0)

    v_ext[head_dim:, :] = jnp.ones((16, 2 * toks), BF16)
    await_aside(0, z)
    block(z, True)
    for s in range(1, steps):
        kv_rings[0].step(s)
        kv_rings[1].step(s)
        attend_step(s)
    kv_rings[0].final()
    kv_rings[1].final()
    last = kv_rings[0].origin(0, steps)
    await_aside(nz - 1, last)

    @pl.when(last < z)
    def _():
        block(last, False)

    down_copy(1 - t).wait_recv()
    half_cols = heads * head_dim
    low = None
    for h in range(heads):
        out = acc[h, :head_dim, :] / acc[h, head_dim : head_dim + 1, :]
        factor_cols = down_buf[
            home, :, pl.ds(pl.multiple_of((y % 2) * half_cols + h * head_dim, head_dim), head_dim)
        ]
        part = jnp.dot(factor_cols, out.astype(BF16), preferred_element_type=F32)
        low = part if low is None else low + part
        att[:, h * head_dim : (h + 1) * head_dim] = jnp.transpose(out).astype(BF16)

    def low_copy(b, core):
        return remote(
            low_src.at[b],
            low_in.at[y],
            low_send.at[b, core],
            low_recv.at[y],
            ctx=z * NY + 2 * t + b,
            tp=core,
        )

    def low_own(b, core):
        return jnp.logical_and(2 * t + b == y, t == core)

    for b in range(2):
        low_src[b] = low[:, b * rows : (b + 1) * rows]
    for b in range(2):
        for core in range(2):

            @pl.when(jnp.logical_not(low_own(b, core)))
            def _():
                low_copy(b, core).start()

            @pl.when(low_own(b, core))
            def _():
                low_in[y] = low_src[b]

    for b in range(2):

        @pl.when(2 * t + b != y)
        def _():
            remote(
                back_all.at[b], back_all.at[b], back_send.at[0], back_recv.at[b], **sibling
            ).wait_recv()

    back = jnp.concatenate([back_all[0], back_all[1]], axis=1)
    down_part = jnp.dot(back, att[...], preferred_element_type=F32)
    for r in range(2):
        for h in range(heads):
            dred_src[r * heads + h] = down_part[8 * r : 8 * r + 8, h * 128 : (h + 1) * 128].astype(BF16)
    blocks = count // 2

    def dred_owner(i):
        return (i // heads) * blocks + (y % 2) * heads + i % heads

    def dred_copy(i):
        return remote(
            dred_src.at[i],
            dred_in.at[2 * z + t],
            dred_send.at[i],
            dred_recv.at[2 * z + t],
            ctx=dred_owner(i),
            tp=home,
        )

    def dred_own(i):
        return jnp.logical_and(dred_owner(i) == me, home == t)

    def dred_start(i, carry):
        @pl.when(jnp.logical_not(dred_own(i)))
        def _():
            dred_copy(i).start()

        @pl.when(dred_own(i))
        def _():
            dred_in[2 * z + t] = dred_src[i]

        return carry

    lax.fori_loop(0, 2 * heads, dred_start, 0)

    for src_y in range(NY):

        @pl.when(jnp.logical_or(src_y != y, home != t))
        def _():
            remote(
                low_in.at[src_y], low_in.at[src_y], low_send.at[0, 0], low_recv.at[src_y], **sibling
            ).wait_recv()

    low = low_in[0]
    for src_y in range(1, NY):
        low = low + low_in[src_y]
    low = low.astype(BF16)
    low_out[...] = low

    for c in range(count):
        red_src[c] = jnp.dot(
            low, grad_ref[:, c * 128 : (c + 1) * 128], preferred_element_type=F32
        ).astype(BF16)

    def red_copy(o):
        to = (me + o) % count
        return remote(
            red_src.at[to], red_in.at[o - 1], red_send.at[o - 1], red_recv.at[o - 1], ctx=to
        )

    def red_start(o, carry):
        red_copy(o).start()
        return carry

    lax.fori_loop(1, count, red_start, 0)

    def att_dest(kvl):
        return att_out.at[:, pl.ds(pl.multiple_of(kvl * half_cols, half_cols), half_cols)]

    def att_copy(b):
        return remote(
            att.at[pl.ds(b * rows, rows)],
            att_dest(y % 2),
            att_send.at[b],
            att_recv.at[y % 2],
            ctx=z * NY + 2 * t + b,
            tp=home,
        )

    for b in range(2):

        @pl.when(jnp.logical_not(home_own(b)))
        def _():
            att_copy(b).start()

        @pl.when(home_own(b))
        def _():
            att_out[:, pl.ds(pl.multiple_of((y % 2) * half_cols, half_cols), half_cols)] = att[
                b * rows : (b + 1) * rows
            ]

    down_y = 2 * t + (me % blocks) // heads

    def dred_add(i, carry):
        @pl.when(jnp.logical_or(down_y != y, i != 2 * z + t))
        def _():
            remote(
                dred_in.at[i], dred_in.at[i], dred_send.at[0], dred_recv.at[i], **sibling
            ).wait_recv()

        return carry + dred_in[i].astype(F32)

    down_sum = lax.fori_loop(0, 2 * nz, dred_add, jnp.zeros((8, 128), F32))

    def red_add(o, so_far):
        red_copy(o).wait_recv()
        return so_far + red_in[o - 1].astype(F32)

    up_sum = lax.fori_loop(1, count, red_add, red_src[me].astype(F32))
    all_buf[me] = jnp.concatenate([up_sum, down_sum], axis=0).astype(BF16)
    squares = jnp.sum(up_sum * up_sum, axis=0, keepdims=True) + jnp.sum(
        down_sum * down_sum, axis=0, keepdims=True
    )
    sq_src[...] = jnp.broadcast_to(jnp.sum(squares, axis=1, keepdims=True), sq_src.shape)

    def sq_copy(i):
        osec, ot = peers[i]
        return remote(
            sq_src,
            sq_in.at[i],
            sq_send.at[i],
            sq_recv.at[i],
            section=(section + osec) % sections,
            tp=(t + ot) % 2,
        )

    for i in range(len(peers)):
        sq_copy(i).start()

    def spread(buf, sends, recvs):
        def copy(o):
            to = (me + o) % count
            return remote(buf.at[me], buf.at[me], sends.at[o - 1], recvs.at[o - 1], ctx=to)

        def arrive(o):
            of = (me - o + count) % count
            return remote(buf.at[of], buf.at[of], sends.at[o - 1], recvs.at[o - 1], ctx=of)

        def each(act):
            def one(o, carry):
                act(o)
                return carry

            lax.fori_loop(1, count, one, 0)

        return (
            lambda: each(lambda o: copy(o).start()),
            lambda: each(lambda o: arrive(o).wait_recv()),
            lambda: each(lambda o: copy(o).wait_send()),
        )

    all_start, all_wait, all_drain = spread(all_buf, all_send, all_recv)
    sqa_start, sqa_wait, sqa_drain = spread(sq_all, sqa_send, sqa_recv)
    all_start()
    squares = sq_src[...]
    for i in range(len(peers)):
        sq_copy(i).wait_recv()
        squares = squares + sq_in[i]
    sq_all[me] = squares
    sqa_start()

    for ring in w_rings + kv_rings:
        ring.drain()
    for oy in range(1, NY):
        doc_copy(oy).wait_send()
        x_copy(oy).wait_send()
        scatter_copy(0, oy).wait_send()
        scatter_copy(1, oy).wait_send()

    @pl.when(t != home)
    def _():
        x_copy(0).wait_send()

    @pl.when(t == home)
    def _():
        for oy in range(1, NY):
            back_pass(oy).wait_send()

    for d, s in doc_hops:
        doc_pass(d, s).wait_send()
    down_copy(t).wait_send()
    square_copy.wait_send()
    back_copy.wait_send()
    for b in range(2):

        @pl.when(jnp.logical_not(home_own(b)))
        def _():
            q_copy(b).wait_send()
            att_copy(b).wait_send()

        for core in range(2):

            @pl.when(jnp.logical_not(low_own(b, core)))
            def _():
                low_copy(b, core).wait_send()

    def dred_drain(i, carry):
        @pl.when(jnp.logical_not(dred_own(i)))
        def _():
            dred_copy(i).wait_send()

        return carry

    lax.fori_loop(0, 2 * heads, dred_drain, 0)

    def red_drain(o, carry):
        red_copy(o).wait_send()
        return carry

    lax.fori_loop(1, count, red_drain, 0)
    for kvl in range(2):

        @pl.when(jnp.logical_or(2 * t + kvl != y, home != t))
        def _():
            dest = att_dest(kvl)
            remote(dest, dest, att_send.at[0], att_recv.at[kvl], **sibling).wait_recv()

    all_wait()
    all_drain()
    for i in range(len(peers)):
        sq_copy(i).wait_send()
    sqa_wait()
    sqa_drain()


def finish_kernel(
    ceiling,
    att_hbm,
    low_hbm,
    all_hbm,
    sq_hbm,
    up_hbm,
    att_out,
    adapter_out,
    gdown_out,
    gup_out,
    att_ref,
    low_ref,
    all_ref,
    sq_ref,
    up_ref,
    adapter,
    gdown,
    gup,
    in_sem,
    out_sem,
):
    count = all_ref.shape[0]
    rank, rows = low_ref.shape
    width = up_ref.shape[1]
    blocks = count // 2
    ins = [
        pltpu.make_async_copy(src, dst, in_sem.at[i])
        for i, (src, dst) in enumerate(
            (
                (low_hbm, low_ref),
                (up_hbm, up_ref),
                (sq_hbm, sq_ref),
                (all_hbm, all_ref),
                (att_hbm.at[pl.ds(0, rows // 2)], att_ref.at[pl.ds(0, rows // 2)]),
                (att_hbm.at[pl.ds(rows // 2, rows // 2)], att_ref.at[pl.ds(rows // 2, rows // 2)]),
            )
        )
    ]
    outs = []

    def put(src, dst):
        copy = pltpu.make_async_copy(src, dst, out_sem.at[len(outs)])
        copy.start()
        outs.append(copy)

    for copy in ins:
        copy.start()
    ins[0].wait()
    ins[1].wait()
    part = rows // 4
    low = jnp.transpose(low_ref[...].astype(F32)).astype(BF16)
    for i in range(4):
        adapter[i * part : (i + 1) * part, :] = jnp.dot(
            low[i * part : (i + 1) * part], up_ref[...], preferred_element_type=F32
        ).astype(BF16)
        put(adapter.at[pl.ds(i * part, part)], adapter_out.at[pl.ds(i * part, part)])
    for i in range(2):
        ins[4 + i].wait()
        half = pl.ds(i * (rows // 2), rows // 2)
        put(att_ref.at[half], att_out.at[half])
    ins[2].wait()
    ins[3].wait()
    norm = sq_ref[0]
    for c in range(1, count):
        norm = norm + sq_ref[c]
    clip = jnp.minimum(1.0, ceiling / (jnp.sqrt(norm[0:1, 0:1]) + 1e-06))
    for c in range(count):
        r0 = 8 * (c // blocks)
        c0 = 128 * (c % blocks)
        gup[:, c * 128 : (c + 1) * 128] = all_ref[c, 0:rank, :].astype(F32) * clip
        gdown[r0 : r0 + 8, c0 : c0 + 128] = all_ref[c, rank : rank + 8, :].astype(F32) * clip
    put(gup, gup_out)
    put(gdown, gdown_out)
    for copy in outs:
        copy.wait()


def per_device(hidden, gain, queries, key_value_weight, adapt_down, adapt_up, out_grad, doc_ids):
    nz = lax.axis_size("ctx") // NY
    sections = lax.axis_size("section")
    rows, width = hidden.shape[1:]
    depth, kv_count = key_value_weight.shape[1:3]
    head_dim = key_value_weight.shape[-1]
    heads = queries.shape[2]
    group = heads // kv_count
    rank, local_query = adapt_down.shape[1:]
    toks = 2 * rows
    half = head_dim // 2
    freqs = 1000000.0 ** (-jnp.arange(half, dtype=F32) * 2.0 / head_dim)
    freqs = jnp.concatenate([freqs, freqs])[None]
    w = key_value_weight[0].transpose(2, 0, 1, 3).reshape(2, depth, kv_count * head_dim)

    vmem = pl.BlockSpec(memory_space=pltpu.VMEM)
    hbm = pl.BlockSpec(memory_space=pl.ANY)
    dma = pltpu.SemaphoreType.DMA
    steps = nz // 2
    count = nz * NY
    peers = 2 * sections - 1
    chunk = rank + 8
    att, low, summed, squares = pl.pallas_call(
        lambda *refs: main_kernel(nz, sections, *refs),
        out_shape=(
            jax.ShapeDtypeStruct((rows, local_query), BF16),
            jax.ShapeDtypeStruct((rank, rows), BF16),
            jax.ShapeDtypeStruct((count, chunk, 128), BF16),
            jax.ShapeDtypeStruct((count, 8, 128), F32),
        ),
        in_specs=[hbm, vmem, hbm, hbm, vmem, hbm, hbm, hbm, vmem],
        out_specs=[vmem] * 4,
        scratch_shapes=[
            pltpu.VMEM((rows, width), BF16),
            pltpu.VMEM((rows, heads, head_dim), BF16),
            pltpu.VMEM((kv_count, group, rows, head_dim), BF16),
            pltpu.VMEM((rows, width), BF16),
            pltpu.VMEM((rank, width), BF16),
            pltpu.VMEM((rank, local_query), BF16),
            pltpu.VMEM((toks, head_dim), F32),
            pltpu.VMEM((toks, head_dim), F32),
            pltpu.VMEM((2, 2, nz * depth, kv_count * head_dim), BF16),
            pltpu.VMEM((NY, rows, depth * nz // 2), BF16),
            pltpu.VMEM((toks, depth * nz), BF16),
            pltpu.VMEM((rows, 128), F32),
            pltpu.VMEM((rows, 128), F32),
            pltpu.VMEM((rank, rows), F32),
            pltpu.VMEM((rank, rows), F32),
            pltpu.VMEM((rank, rows), BF16),
            pltpu.VMEM((2, rank, rows), BF16),
            pltpu.VMEM((2, rank, local_query), BF16),
            pltpu.VMEM((NY, 8, rows), jnp.int32),
            pltpu.VMEM((nz, 8, rows), jnp.int32),
            pltpu.VMEM((NY, toks, head_dim), F32),
            pltpu.VMEM((NY - 1, toks, head_dim), F32),
            pltpu.VMEM((NY, toks, head_dim), BF16),
            pltpu.VMEM((NY - 1, toks, head_dim), BF16),
            pltpu.VMEM((nz, 2, toks, head_dim), BF16),
            pltpu.VMEM((nz, 2, head_dim, toks), BF16),
            pltpu.VMEM((group, toks, head_dim), BF16),
            pltpu.VMEM((2 * toks, toks), F32),
            pltpu.VMEM((group, 1, toks), F32),
            pltpu.VMEM((2, 2, toks, toks), F32),
            pltpu.VMEM((2, 2 * toks, toks), BF16),
            pltpu.VMEM((head_dim + 16, 2 * toks), BF16),
            pltpu.VMEM((group, head_dim + 8, toks), F32),
            pltpu.VMEM((toks, group * head_dim), BF16),
            pltpu.VMEM((2, rank, rows), F32),
            pltpu.VMEM((NY, rank, rows), F32),
            pltpu.VMEM((count, rank, 128), BF16),
            pltpu.VMEM((count - 1, rank, 128), BF16),
            pltpu.VMEM((2 * group, 8, 128), BF16),
            pltpu.VMEM((2 * nz, 8, 128), BF16),
            pltpu.VMEM((8, 128), F32),
            pltpu.VMEM((peers, 8, 128), F32),
            dma((2, 2, steps)),
            dma((2, 2, steps)),
            dma((2, nz)),
            dma((2, nz)),
            dma((2, 2, steps)),
            dma((2, 2, steps)),
            dma((2, nz)),
            dma((2, nz)),
            dma((2, steps)),
            dma((2, steps)),
            dma((NY,)),
            dma((2, 2)),
            dma((2,)),
            dma((2,)),
            dma((2, NY - 1)),
            dma((2, NY - 1)),
            dma((NY - 1,)),
            dma((NY - 1,)),
            dma((3,)),
            dma((3,)),
            dma((NY - 1,)),
            dma((2,)),
            dma((2,)),
            dma((2,)),
            dma((2, 2)),
            dma((NY,)),
            dma((count - 1,)),
            dma((count - 1,)),
            dma((2 * group,)),
            dma((2 * nz,)),
            dma((count - 1,)),
            dma((count - 1,)),
            dma((peers,)),
            dma((peers,)),
            dma((count - 1,)),
            dma((count - 1,)),
            dma((8,)),
            dma((2,)),
        ],
        compiler_params=pltpu.CompilerParams(collective_id=0, has_side_effects=True),
        name="main",
    )(
        hidden[0],
        gain,
        w,
        queries[0],
        freqs,
        out_grad[0],
        adapt_up[0],
        adapt_down[0],
        doc_ids[None],
    )

    ceiling = 0.5 * math.sqrt(sections * rank * (local_query + width) * 2)
    return pl.pallas_call(
        lambda *refs: finish_kernel(ceiling, *refs),
        out_shape=(
            jax.ShapeDtypeStruct((rows, local_query), BF16),
            jax.ShapeDtypeStruct((rows, width), BF16),
            jax.ShapeDtypeStruct((rank, local_query), F32),
            jax.ShapeDtypeStruct((rank, width), F32),
        ),
        in_specs=[hbm] * 5,
        out_specs=[hbm] * 4,
        scratch_shapes=[
            pltpu.VMEM((rows, local_query), BF16),
            pltpu.VMEM((rank, rows), BF16),
            pltpu.VMEM((count, chunk, 128), BF16),
            pltpu.VMEM((count, 8, 128), F32),
            pltpu.VMEM((rank, width), BF16),
            pltpu.VMEM((rows, width), BF16),
            pltpu.VMEM((rank, local_query), F32),
            pltpu.VMEM((rank, width), F32),
            dma((6,)),
            dma((8,)),
        ],
        name="finish",
    )(att, low, summed, squares, adapt_up[0])


def solution(mesh):
    def step(*args):
        return tuple(out[None] for out in per_device(*args))

    return jax.shard_map(
        step,
        mesh=mesh,
        in_specs=(
            P("section", "ctx", "tp"),
            P("section", "tp"),
            P("section", "ctx", "tp", None),
            P("section", "ctx", "tp", None, None),
            P("section", None, "tp"),
            P("section", None, "tp"),
            P("section", "ctx", "tp"),
            P("ctx"),
        ),
        out_specs=(
            P("section", "ctx", "tp"),
            P("section", "ctx", "tp"),
            P("section", None, "tp"),
            P("section", None, "tp"),
        ),
        check_vma=False,
    )
```

```python
import math

import jax
import jax.numpy as jnp
import numpy as np
from jax import lax
from jax.experimental import pallas as pl
from jax.experimental.pallas import tpu as pltpu
from jax.sharding import PartitionSpec as P

MESH = pl.DeviceIdType.MESH
NY = 4
PIECE = 64
F32 = jnp.float32
BF16 = jnp.bfloat16


def remote(src, dst, send_sem, recv_sem, **where):
    return pltpu.make_async_remote_copy(
        src_ref=src,
        dst_ref=dst,
        send_sem=send_sem,
        recv_sem=recv_sem,
        device_id=where,
        device_id_type=MESH,
    )


def position():
    ctx = lax.axis_index("ctx")
    return ctx // NY, ctx % NY, lax.axis_index("tp")


class Ring:
    def __init__(self, nz, block, half, send, recv, sib_send=None, sib_recv=None):
        self.nz, self.steps = nz, nz // 2
        self.block, self.half = block, half
        self.send, self.recv = send, recv
        self.sib_send, self.sib_recv = sib_send, sib_recv
        self.z, self.y, self.t = position()

    def origin(self, d, s):
        return (self.z - s + self.nz) % self.nz if d == 0 else (self.z + s) % self.nz

    def neighbour(self, d):
        z = (self.z + 1) % self.nz if d == 0 else (self.z + self.nz - 1) % self.nz
        return dict(ctx=z * NY + self.y, tp=self.t)

    def piece(self, zi, d, s):
        return self.half(zi, d, self.t) if s == self.steps else self.block(zi, self.t)

    def hop(self, d, s, src=None):
        piece = self.piece(self.origin(d, s - 1), d, s)
        return remote(
            piece if src is None else src,
            piece,
            self.send.at[d, s - 1],
            self.recv.at[d, s - 1],
            **self.neighbour(d),
        )

    def arrival(self, d, s):
        piece = self.piece(self.origin(d, s), d, s)
        return remote(
            piece, piece, self.send.at[d, s - 1], self.recv.at[d, s - 1], **self.neighbour(d)
        )

    def aside(self, index, zi, core, src=None):
        piece = self.block(zi, core)
        return remote(
            piece if src is None else src,
            piece,
            self.sib_send.at[index],
            self.sib_recv.at[index],
            tp=1 - self.t,
        )

    def start(self, src=None):
        for d in (0, 1):
            self.hop(d, 1, src).start()
        if self.sib_send is not None:
            self.aside(0, self.z, self.t, src).start()

    def step(self, s):
        for d in (0, 1):
            self.arrival(d, s).wait_recv()
            self.hop(d, s + 1).start()
            if self.sib_send is not None:
                self.aside(2 * s - 1 + d, self.origin(d, s), self.t).start()

    def final(self):
        for d in (0, 1):
            self.arrival(d, self.steps).wait_recv()
        if self.sib_send is not None:
            self.aside(self.nz - 1, self.origin(0, self.steps), self.t).start()

    def asides(self):
        yield 0, self.z
        for s in range(1, self.steps):
            for d in (0, 1):
                yield 2 * s - 1 + d, self.origin(d, s)
        yield self.nz - 1, self.origin(0, self.steps)

    def wait_aside(self, index, zi):
        self.aside(index, zi, 1 - self.t).wait_recv()

    def wait_sibling(self):
        for index, zi in self.asides():
            self.wait_aside(index, zi)

    def drain(self):
        for d in (0, 1):
            for s in range(1, self.steps + 1):
                self.hop(d, s).wait_send()
        if self.sib_send is not None:
            for index, zi in self.asides():
                self.aside(index, zi, self.t).wait_send()


def main_kernel(
    nz,
    sections,
    hid_hbm,
    gain_ref,
    w_hbm,
    q_hbm,
    freq_ref,
    grad_hbm,
    up_hbm,
    down_hbm,
    doc_ref,
    att_hbm,
    low_out,
    all_buf,
    norm_out,
    hid_ref,
    q_raw,
    q_ref,
    grad_ref,
    up_ref,
    down_ref,
    cos_ref,
    sin_ref,
    w_raw,
    w_wide,
    w_buf,
    normed,
    x_buf,
    square_src,
    square_in,
    back_part,
    back_in,
    back_own,
    back_all,
    down_buf,
    doc_in,
    doc_all,
    k_part,
    k_in,
    v_part,
    v_in,
    k_all,
    v_all,
    q_all,
    bias_ref,
    top,
    s_buf,
    p_buf,
    v_ext,
    acc,
    att,
    low_src,
    low_in,
    red_src,
    red_in,
    dred_src,
    dred_in,
    sq_src,
    sq_in,
    sq_all,
    att_out,
    w_send,
    w_recv,
    ws_send,
    ws_recv,
    kv_send,
    kv_recv,
    kvs_send,
    kvs_recv,
    d_send,
    d_recv,
    x_send,
    x_recv,
    q_send,
    q_recv,
    rs_send,
    rs_recv,
    dy_send,
    dy_recv,
    pair_send,
    pair_recv,
    back_send,
    back_recv,
    att_send,
    att_recv,
    low_send,
    low_recv,
    red_send,
    red_recv,
    dred_send,
    dred_recv,
    all_send,
    all_recv,
    sq_send,
    sq_recv,
    sqa_send,
    sqa_recv,
    load_sem,
    own_sem,
):
    z, y, t = position()
    section = lax.axis_index("section")
    rows, width = hid_ref.shape
    depth = w_buf.shape[2] // nz
    cols = depth * nz // 2
    head_dim = k_all.shape[-1]
    heads = q_all.shape[0]
    toks = 2 * rows
    keys = 2 * toks
    rank = up_ref.shape[0]
    count = nz * NY
    me = z * NY + y
    steps = nz // 2
    home = y // 2
    sibling = dict(tp=1 - t)
    peers = [(osec, ot) for osec in range(sections) for ot in range(2) if osec or ot]

    barrier = pltpu.get_barrier_semaphore()

    def greet(**where):
        pl.semaphore_signal(barrier, inc=1, device_id=where, device_id_type=MESH)

    greet(ctx=(z + 1) % nz * NY + y)
    greet(ctx=(z + nz - 1) % nz * NY + y)
    for oy in range(NY):
        for ot in range(2):
            if oy or ot:
                greet(ctx=z * NY + (y + oy) % NY, tp=(t + ot) % 2)
    for osec, ot in peers:
        if osec:
            greet(section=(section + osec) % sections, tp=(t + ot) % 2)
    slab = rows // 4
    hid_loads = [
        pltpu.make_async_copy(
            hid_hbm.at[pl.ds(i * slab, slab)], hid_ref.at[pl.ds(i * slab, slab)], load_sem.at[i]
        )
        for i in range(4)
    ]
    late_loads = [
        pltpu.make_async_copy(src, dst, load_sem.at[4 + i])
        for i, (src, dst) in enumerate(
            ((q_hbm, q_raw), (grad_hbm, grad_ref), (up_hbm, up_ref), (down_hbm, down_ref))
        )
    ]
    w_load = pltpu.make_async_copy(w_hbm, w_raw, own_sem.at[0])
    w_load.start()
    for load in hid_loads:
        load.start()
    own_rows = pl.ds(pl.multiple_of(z * depth, depth), depth)
    w_load.wait()
    w_wide[...] = w_raw[...].astype(F32)
    for p in (0, 1):
        for h in range(2):
            w_buf[p, t, own_rows, h * head_dim : (h + 1) * head_dim] = w_wide[
                pl.ds(2 * h + p, depth, stride=4), :
            ].astype(BF16)
    pl.semaphore_wait(barrier, 2 + 2 * NY - 1 + 2 * (sections - 1))

    def w_block(p):
        return lambda zi, core: w_buf.at[p, core, pl.ds(pl.multiple_of(zi * depth, depth), depth)]

    def w_half(p):
        return lambda zi, h, core: w_buf.at[
            p, core, pl.ds(pl.multiple_of(zi * depth + h * (depth // 2), depth // 2), depth // 2)
        ]

    def kv_block(buf):
        return lambda zi, core: buf.at[zi, core]

    def kv_half(buf):
        size = buf.shape[2] // 2
        return lambda zi, h, core: buf.at[zi, core, pl.ds(h * size, size)]

    w_rings = [
        Ring(nz, w_block(p), w_half(p), w_send.at[p], w_recv.at[p], ws_send.at[p], ws_recv.at[p])
        for p in (0, 1)
    ]
    kv_rings = [
        Ring(nz, kv_block(buf), kv_half(buf), kv_send.at[p], kv_recv.at[p], kvs_send.at[p], kvs_recv.at[p])
        for p, buf in ((0, k_all), (1, v_all))
    ]

    w_rings[0].start()
    w_rings[1].start()
    for load in late_loads:
        load.start()

    doc_own = doc_in.at[0]
    doc_in[0] = jnp.broadcast_to(doc_ref[...], doc_in.shape[1:])

    def doc_copy(oy):
        return remote(
            doc_own,
            doc_in.at[oy],
            dy_send.at[oy - 1],
            dy_recv.at[oy - 1],
            ctx=z * NY + (y + oy) % NY,
        )

    for oy in range(1, NY):
        doc_copy(oy).start()

    def down_copy(core):
        return remote(down_ref, down_buf.at[core], pair_send.at[0], pair_recv.at[0], **sibling)

    for i, load in enumerate(hid_loads):
        load.wait()
        hid = hid_ref[i * slab : (i + 1) * slab, :].astype(F32)
        square = jnp.sum(hid * hid, axis=1, keepdims=True)
        square_src[i * slab : (i + 1) * slab, :] = jnp.broadcast_to(square, (slab, 128))
    square_copy = remote(square_src, square_in, pair_send.at[1], pair_recv.at[1], **sibling)
    square_copy.start()
    square_copy.wait_recv()
    mean = (square_src[:, :1] + square_in[:, :1]) * (1.0 / (2 * width))
    scale = lax.rsqrt(mean + 1e-06)

    def x_dest(b, core):
        return x_buf.at[pl.ds(b * rows, rows), pl.ds(pl.multiple_of(core * cols, cols), cols)]

    def x_copy(oy):
        yd = (y + oy) % NY
        return remote(
            normed.at[yd],
            x_dest(y % 2, t),
            x_send.at[oy],
            x_recv.at[y % 2, t],
            ctx=z * NY + yd,
            tp=home,
        )

    for yd in range(NY):
        for zl in range(nz // 2):
            start = (zl * NY + yd) * depth
            piece = hid_ref[:, start : start + depth].astype(F32)
            gain = gain_ref[:, start : start + depth].astype(F32)
            normed[yd, :, zl * depth : (zl + 1) * depth] = (piece * scale * gain).astype(BF16)
    for oy in range(1, NY):
        x_copy(oy).start()

    @pl.when(t != home)
    def _():
        x_copy(0).start()

    @pl.when(t == home)
    def _():
        x_buf[
            pl.ds(pl.multiple_of((y % 2) * rows, rows), rows),
            pl.ds(pl.multiple_of(t * cols, cols), cols),
        ] = normed[y]

    late_loads[0].wait()
    turned_q = jnp.transpose(q_raw[...].astype(F32), (1, 0, 2)).astype(BF16)
    q_ref[...] = turned_q.reshape(q_ref.shape)

    def q_dest(b):
        return q_all.at[:, pl.ds(b * rows, rows)]

    def q_copy(kvl):
        return remote(
            q_ref.at[kvl],
            q_dest(y % 2),
            q_send.at[kvl],
            q_recv.at[y % 2],
            ctx=z * NY + 2 * t + kvl,
            tp=home,
        )

    def home_own(kvl):
        return jnp.logical_and(2 * t + kvl == y, home == t)

    for kvl in range(2):

        @pl.when(jnp.logical_not(home_own(kvl)))
        def _():
            q_copy(kvl).start()

        @pl.when(home_own(kvl))
        def _():
            q_all[:, pl.ds(pl.multiple_of((y % 2) * rows, rows), rows), :] = q_ref[kvl]

    for oy in range(1, NY):
        doc_copy(oy).wait_recv()
    line = lax.broadcasted_iota(jnp.int32, doc_in.shape[1:], 0)
    group = jnp.where(line == y, doc_in[0], 0)
    for oy in range(1, NY):
        group = jnp.where(line == (y + NY - oy) % NY, doc_in[oy], group)
    doc_all[z] = group

    def doc_pass(d, s):
        zi = (z - s + 1 + nz) % nz if d == 0 else (z + s - 1) % nz
        to = (z + 1) % nz if d == 0 else (z + nz - 1) % nz
        return remote(
            doc_all.at[zi], doc_all.at[zi], d_send.at[d, s - 1], d_recv.at[d, s - 1], ctx=to * NY + y
        )

    def doc_arrive(d, s):
        zi = (z - s + nz) % nz if d == 0 else (z + s) % nz
        to = (z + 1) % nz if d == 0 else (z + nz - 1) % nz
        return remote(
            doc_all.at[zi], doc_all.at[zi], d_send.at[d, s - 1], d_recv.at[d, s - 1], ctx=to * NY + y
        )

    doc_hops = [(0, s) for s in range(1, steps + 1)] + [(1, s) for s in range(1, steps)]

    def doc_step(s):
        for d in (0, 1):
            if (d, s) in doc_hops:
                doc_arrive(d, s).wait_recv()
                if (d, s + 1) in doc_hops:
                    doc_pass(d, s + 1).start()

    for d in (0, 1):
        if (d, 1) in doc_hops:
            doc_pass(d, 1).start()

    late_loads[3].wait()
    down_copy(t).start()
    down_buf[t] = down_ref[...]
    late_loads[1].wait()
    late_loads[2].wait()
    back_part[...] = lax.dot_general(
        up_ref[...], grad_ref[...], (((1,), (1,)), ((), ())), preferred_element_type=F32
    )
    back_copy = remote(back_part, back_in, pair_send.at[2], pair_recv.at[2], **sibling)
    back_copy.start()

    def back_pass(oy):
        return remote(
            back_own,
            back_all.at[y % 2],
            back_send.at[oy - 1],
            back_recv.at[y % 2],
            ctx=z * NY + (y + oy) % NY,
        )

    for s in range(1, steps):
        w_rings[0].step(s)
        w_rings[1].step(s)
        doc_step(s)
        if s == 2:
            lane = lax.broadcasted_iota(jnp.int32, cos_ref.shape, 1)
            token = lax.broadcasted_iota(jnp.int32, cos_ref.shape, 0) + (z * 2 + t) * toks
            angles = token.astype(F32) * freq_ref[...]
            cos_ref[...] = jnp.cos(angles)
            sine = jnp.sin(angles)
            sin_ref[...] = jnp.where(lane < head_dim // 2, -sine, sine)
        if s == 1:
            back_copy.wait_recv()
            back_own[...] = (back_part[...] + back_in[...]).astype(BF16)

            @pl.when(t == home)
            def _():
                for oy in range(1, NY):
                    back_pass(oy).start()
                back_all[y % 2] = back_own[...]

    def x_wait():
        for b in range(2):
            for core in range(2):

                @pl.when(jnp.logical_or(2 * t + b != y, t != core))
                def _():
                    dest = x_dest(b, core)
                    remote(dest, dest, x_send.at[0], x_recv.at[b, core], **sibling).wait_recv()

    def project(p, part):
        for core in range(2):
            partial = jnp.dot(x_buf[...], w_buf[p, core], preferred_element_type=F32)
            for hl in range(2):
                part[2 * core + hl] = partial[:, hl * head_dim : (hl + 1) * head_dim].astype(part.dtype)

    def scatter_copy(p, oy):
        part, into = ((k_part, k_in), (v_part, v_in))[p]
        yd = (y + oy) % NY
        return remote(
            part.at[yd],
            into.at[oy - 1],
            rs_send.at[p, oy - 1],
            rs_recv.at[p, oy - 1],
            ctx=z * NY + yd,
        )

    def collect(p):
        part, into = ((k_part, k_in), (v_part, v_in))[p]
        for oy in range(1, NY):
            scatter_copy(p, oy).wait_recv()
        whole = part[y].astype(F32)
        for oy in range(1, NY):
            whole = whole + into[oy - 1].astype(F32)
        return whole

    def rope(v):
        return (v * cos_ref[...] + pltpu.roll(v, head_dim // 2, 1) * sin_ref[...]).astype(BF16)

    x_wait()
    w_rings[0].final()
    w_rings[0].wait_sibling()
    project(0, k_part)
    for oy in range(1, NY):
        scatter_copy(0, oy).start()
    w_rings[1].final()
    w_rings[1].wait_sibling()
    project(1, v_part)
    for oy in range(1, NY):
        scatter_copy(1, oy).start()

    for b in range(2):

        @pl.when(jnp.logical_or(2 * t + b != y, home != t))
        def _():
            dest = q_dest(b)
            remote(dest, dest, q_send.at[0], q_recv.at[b], **sibling).wait_recv()

    for h in range(heads):
        q_all[h] = rope(q_all[h].astype(F32))
    doc_step(steps)
    q_doc = jnp.concatenate(
        [
            jnp.sum(jnp.where(line == 2 * t + b, doc_all[z].astype(F32), 0.0), axis=0, keepdims=True)
            for b in range(2)
        ],
        axis=1,
    )

    q_pos = (z * 2 + t) * toks + lax.broadcasted_iota(jnp.int32, (keys, toks), 1)
    k_pos = lax.broadcasted_iota(jnp.int32, (keys, toks), 0)

    def mask(kb, carry):
        turned = jnp.transpose(doc_all[kb].astype(F32))
        k_doc = jnp.concatenate([turned[:, j : j + 1] for j in range(NY)], axis=0)
        allowed = jnp.logical_and(k_doc == q_doc, k_pos + kb * keys <= q_pos)
        bias_ref[kb] = jnp.where(allowed, 0.0, -1e30)
        return carry

    lax.fori_loop(0, nz, mask, 0)

    k_all[z, t] = rope(collect(0))
    kv_rings[0].start()
    v_all[z, t] = jnp.transpose(collect(1)).astype(BF16)
    kv_rings[1].start()

    factor = head_dim ** (-0.5) * math.log2(math.e)

    def block(kb, first):
        for core in range(2):
            v_ext[:head_dim, core * toks : (core + 1) * toks] = v_all[kb, core]

        tops, shrinks = {}, {}

        def score(h):
            q = q_all[h]
            slot = h % 2
            peak = None
            for core in range(2):
                scores = (
                    lax.dot_general(
                        k_all[kb, core], q, (((1,), (1,)), ((), ())), preferred_element_type=F32
                    )
                    + bias_ref[kb, core * toks : (core + 1) * toks, :]
                )
                s_buf[slot, core] = scores
                here = jnp.max(scores, axis=0, keepdims=True)
                peak = here if peak is None else jnp.maximum(peak, here)
            if not first:
                old_top = top[h]
                peak = jnp.maximum(old_top, peak)
                shrinks[h] = jnp.exp2((old_top - peak) * factor)
            top[h] = peak
            tops[h] = peak

        def weigh(h):
            slot = h % 2
            for core in range(2):
                for r in range(0, toks, PIECE):
                    p_buf[slot, core * toks + r : core * toks + r + PIECE, :] = jnp.exp2(
                        (s_buf[slot, core, r : r + PIECE, :] - tops[h]) * factor
                    ).astype(BF16)

        def mix(h):
            slot = h % 2
            part = jnp.dot(v_ext[...], p_buf[slot], preferred_element_type=F32)[: head_dim + 8]
            acc[h] = part if first else acc[h] * shrinks[h] + part

        for i in range(heads + 2):
            if i < heads:
                score(i)
            if 0 <= i - 1 < heads:
                weigh(i - 1)
            if i >= 2:
                mix(i - 2)

    def await_aside(index, zi):
        for ring in kv_rings:
            ring.wait_aside(index, zi)

    def attend_step(s):
        def one(d, carry):
            zi = jnp.where(d == 0, z - s + nz, z + s) % nz
            await_aside(2 * s - 1 + d, zi)

            @pl.when(zi < z)
            def _():
                block(zi, False)

            return carry

        lax.fori_loop(0, 2, one, 0)

    v_ext[head_dim:, :] = jnp.ones((16, 2 * toks), BF16)
    await_aside(0, z)
    block(z, True)
    for s in range(1, steps):
        kv_rings[0].step(s)
        kv_rings[1].step(s)
        attend_step(s)
    kv_rings[0].final()
    kv_rings[1].final()
    last = kv_rings[0].origin(0, steps)
    await_aside(nz - 1, last)

    @pl.when(last < z)
    def _():
        block(last, False)

    down_copy(1 - t).wait_recv()
    half_cols = heads * head_dim
    low = None
    for h in range(heads):
        out = acc[h, :head_dim, :] / acc[h, head_dim : head_dim + 1, :]
        factor_cols = down_buf[
            home, :, pl.ds(pl.multiple_of((y % 2) * half_cols + h * head_dim, head_dim), head_dim)
        ]
        part = jnp.dot(factor_cols, out.astype(BF16), preferred_element_type=F32)
        low = part if low is None else low + part
        att[:, h * head_dim : (h + 1) * head_dim] = jnp.transpose(out).astype(BF16)

    def low_copy(b, core):
        return remote(
            low_src.at[b],
            low_in.at[y],
            low_send.at[b, core],
            low_recv.at[y],
            ctx=z * NY + 2 * t + b,
            tp=core,
        )

    def low_own(b, core):
        return jnp.logical_and(2 * t + b == y, t == core)

    for b in range(2):
        low_src[b] = low[:, b * rows : (b + 1) * rows]
    for b in range(2):
        for core in range(2):

            @pl.when(jnp.logical_not(low_own(b, core)))
            def _():
                low_copy(b, core).start()

            @pl.when(low_own(b, core))
            def _():
                low_in[y] = low_src[b]

    for b in range(2):

        @pl.when(2 * t + b != y)
        def _():
            remote(
                back_all.at[b], back_all.at[b], back_send.at[0], back_recv.at[b], **sibling
            ).wait_recv()

    back = jnp.concatenate([back_all[0], back_all[1]], axis=1)
    down_part = jnp.dot(back, att[...], preferred_element_type=F32)
    for r in range(2):
        for h in range(heads):
            dred_src[r * heads + h] = down_part[8 * r : 8 * r + 8, h * 128 : (h + 1) * 128].astype(BF16)
    blocks = count // 2

    def dred_owner(i):
        return (i // heads) * blocks + (y % 2) * heads + i % heads

    def dred_copy(i):
        return remote(
            dred_src.at[i],
            dred_in.at[2 * z + t],
            dred_send.at[i],
            dred_recv.at[2 * z + t],
            ctx=dred_owner(i),
            tp=home,
        )

    def dred_own(i):
        return jnp.logical_and(dred_owner(i) == me, home == t)

    def dred_start(i, carry):
        @pl.when(jnp.logical_not(dred_own(i)))
        def _():
            dred_copy(i).start()

        @pl.when(dred_own(i))
        def _():
            dred_in[2 * z + t] = dred_src[i]

        return carry

    lax.fori_loop(0, 2 * heads, dred_start, 0)

    for src_y in range(NY):

        @pl.when(jnp.logical_or(src_y != y, home != t))
        def _():
            remote(
                low_in.at[src_y], low_in.at[src_y], low_send.at[0, 0], low_recv.at[src_y], **sibling
            ).wait_recv()

    low = low_in[0]
    for src_y in range(1, NY):
        low = low + low_in[src_y]
    low = low.astype(BF16)
    low_out[...] = low

    for c in range(count):
        red_src[c] = jnp.dot(
            low, grad_ref[:, c * 128 : (c + 1) * 128], preferred_element_type=F32
        ).astype(BF16)

    def red_copy(o):
        to = (me + o) % count
        return remote(
            red_src.at[to], red_in.at[o - 1], red_send.at[o - 1], red_recv.at[o - 1], ctx=to
        )

    def red_start(o, carry):
        red_copy(o).start()
        return carry

    lax.fori_loop(1, count, red_start, 0)

    def att_dest(kvl):
        return att_out.at[:, pl.ds(pl.multiple_of(kvl * half_cols, half_cols), half_cols)]

    def att_copy(b):
        return remote(
            att.at[pl.ds(b * rows, rows)],
            att_dest(y % 2),
            att_send.at[b],
            att_recv.at[y % 2],
            ctx=z * NY + 2 * t + b,
            tp=home,
        )

    for b in range(2):

        @pl.when(jnp.logical_not(home_own(b)))
        def _():
            att_copy(b).start()

        @pl.when(home_own(b))
        def _():
            att_out[:, pl.ds(pl.multiple_of((y % 2) * half_cols, half_cols), half_cols)] = att[
                b * rows : (b + 1) * rows
            ]

    down_y = 2 * t + (me % blocks) // heads

    def dred_add(i, carry):
        @pl.when(jnp.logical_or(down_y != y, i != 2 * z + t))
        def _():
            remote(
                dred_in.at[i], dred_in.at[i], dred_send.at[0], dred_recv.at[i], **sibling
            ).wait_recv()

        return carry + dred_in[i].astype(F32)

    down_sum = lax.fori_loop(0, 2 * nz, dred_add, jnp.zeros((8, 128), F32))

    def red_add(o, so_far):
        red_copy(o).wait_recv()
        return so_far + red_in[o - 1].astype(F32)

    up_sum = lax.fori_loop(1, count, red_add, red_src[me].astype(F32))
    all_buf[me] = jnp.concatenate([up_sum, down_sum], axis=0).astype(BF16)
    squares = jnp.sum(up_sum * up_sum, axis=0, keepdims=True) + jnp.sum(
        down_sum * down_sum, axis=0, keepdims=True
    )
    sq_src[...] = jnp.broadcast_to(jnp.sum(squares, axis=1, keepdims=True), sq_src.shape)

    def sq_copy(i):
        osec, ot = peers[i]
        return remote(
            sq_src,
            sq_in.at[i],
            sq_send.at[i],
            sq_recv.at[i],
            section=(section + osec) % sections,
            tp=(t + ot) % 2,
        )

    for i in range(len(peers)):
        sq_copy(i).start()

    def spread(buf, sends, recvs):
        def copy(o):
            to = (me + o) % count
            return remote(buf.at[me], buf.at[me], sends.at[o - 1], recvs.at[o - 1], ctx=to)

        def arrive(o):
            of = (me - o + count) % count
            return remote(buf.at[of], buf.at[of], sends.at[o - 1], recvs.at[o - 1], ctx=of)

        def each(act):
            def one(o, carry):
                act(o)
                return carry

            lax.fori_loop(1, count, one, 0)

        return (
            lambda: each(lambda o: copy(o).start()),
            lambda: each(lambda o: arrive(o).wait_recv()),
            lambda: each(lambda o: copy(o).wait_send()),
        )

    all_start, all_wait, all_drain = spread(all_buf, all_send, all_recv)
    sqa_start, sqa_wait, sqa_drain = spread(sq_all, sqa_send, sqa_recv)
    all_start()
    squares = sq_src[...]
    for i in range(len(peers)):
        sq_copy(i).wait_recv()
        squares = squares + sq_in[i]
    sq_all[me] = squares
    sqa_start()

    for ring in w_rings + kv_rings:
        ring.drain()
    for oy in range(1, NY):
        doc_copy(oy).wait_send()
        x_copy(oy).wait_send()
        scatter_copy(0, oy).wait_send()
        scatter_copy(1, oy).wait_send()

    @pl.when(t != home)
    def _():
        x_copy(0).wait_send()

    @pl.when(t == home)
    def _():
        for oy in range(1, NY):
            back_pass(oy).wait_send()

    for d, s in doc_hops:
        doc_pass(d, s).wait_send()
    down_copy(t).wait_send()
    square_copy.wait_send()
    back_copy.wait_send()
    for b in range(2):

        @pl.when(jnp.logical_not(home_own(b)))
        def _():
            q_copy(b).wait_send()
            att_copy(b).wait_send()

        for core in range(2):

            @pl.when(jnp.logical_not(low_own(b, core)))
            def _():
                low_copy(b, core).wait_send()

    def dred_drain(i, carry):
        @pl.when(jnp.logical_not(dred_own(i)))
        def _():
            dred_copy(i).wait_send()

        return carry

    lax.fori_loop(0, 2 * heads, dred_drain, 0)

    def red_drain(o, carry):
        red_copy(o).wait_send()
        return carry

    lax.fori_loop(1, count, red_drain, 0)
    for kvl in range(2):

        @pl.when(jnp.logical_or(2 * t + kvl != y, home != t))
        def _():
            dest = att_dest(kvl)
            remote(dest, dest, att_send.at[0], att_recv.at[kvl], **sibling).wait_recv()

    att_store = pltpu.make_async_copy(att_out, att_hbm, own_sem.at[1])
    att_store.start()
    all_wait()
    all_drain()
    for i in range(len(peers)):
        sq_copy(i).wait_send()
    sqa_wait()
    sqa_drain()
    norm = sq_all[0]
    for c in range(1, count):
        norm = norm + sq_all[c]
    norm_out[...] = norm
    att_store.wait()


def finish_kernel(
    ceiling,
    att_hbm,
    low_hbm,
    all_hbm,
    sq_hbm,
    up_hbm,
    att_out,
    adapter_out,
    gdown_out,
    gup_out,
    att_ref,
    low_ref,
    all_ref,
    sq_ref,
    up_ref,
    adapter,
    gdown,
    gup,
    in_sem,
    out_sem,
):
    count = all_ref.shape[0]
    rank, rows = low_ref.shape
    width = up_ref.shape[1]
    blocks = count // 2
    ins = [
        pltpu.make_async_copy(src, dst, in_sem.at[i])
        for i, (src, dst) in enumerate(
            (
                (low_hbm, low_ref),
                (up_hbm, up_ref),
                (sq_hbm, sq_ref),
                (all_hbm, all_ref),
                (att_hbm.at[pl.ds(0, rows // 2)], att_ref.at[pl.ds(0, rows // 2)]),
                (att_hbm.at[pl.ds(rows // 2, rows // 2)], att_ref.at[pl.ds(rows // 2, rows // 2)]),
            )
        )
    ]
    outs = []

    def put(src, dst):
        copy = pltpu.make_async_copy(src, dst, out_sem.at[len(outs)])
        copy.start()
        outs.append(copy)

    for copy in ins:
        copy.start()
    ins[0].wait()
    ins[1].wait()
    part = rows // 4
    low = jnp.transpose(low_ref[...].astype(F32)).astype(BF16)
    for i in range(4):
        adapter[i * part : (i + 1) * part, :] = jnp.dot(
            low[i * part : (i + 1) * part], up_ref[...], preferred_element_type=F32
        ).astype(BF16)
        put(adapter.at[pl.ds(i * part, part)], adapter_out.at[pl.ds(i * part, part)])
    for i in range(2):
        ins[4 + i].wait()
        half = pl.ds(i * (rows // 2), rows // 2)
        put(att_ref.at[half], att_out.at[half])
    ins[2].wait()
    ins[3].wait()
    clip = jnp.minimum(1.0, ceiling / (jnp.sqrt(sq_ref[0:1, 0:1]) + 1e-06))
    for c in range(count):
        r0 = 8 * (c // blocks)
        c0 = 128 * (c % blocks)
        gup[:, c * 128 : (c + 1) * 128] = all_ref[c, 0:rank, :].astype(F32) * clip
        gdown[r0 : r0 + 8, c0 : c0 + 128] = all_ref[c, rank : rank + 8, :].astype(F32) * clip
    put(gup, gup_out)
    put(gdown, gdown_out)
    for copy in outs:
        copy.wait()


def per_device(hidden, gain, queries, key_value_weight, adapt_down, adapt_up, out_grad, doc_ids):
    nz = lax.axis_size("ctx") // NY
    sections = lax.axis_size("section")
    rows, width = hidden.shape[1:]
    depth, kv_count = key_value_weight.shape[1:3]
    head_dim = key_value_weight.shape[-1]
    heads = queries.shape[2]
    group = heads // kv_count
    rank, local_query = adapt_down.shape[1:]
    toks = 2 * rows
    half = head_dim // 2
    freqs = (1000000.0 ** (-np.arange(half) * 2.0 / head_dim)).astype(np.float32)
    freqs = jnp.asarray(np.concatenate([freqs, freqs])[None])
    w = key_value_weight.reshape(depth * kv_count * 2, head_dim)

    vmem = pl.BlockSpec(memory_space=pltpu.VMEM)
    hbm = pl.BlockSpec(memory_space=pl.ANY)
    dma = pltpu.SemaphoreType.DMA
    steps = nz // 2
    count = nz * NY
    peers = 2 * sections - 1
    chunk = rank + 8
    att, low, summed, squares = pl.pallas_call(
        lambda *refs: main_kernel(nz, sections, *refs),
        out_shape=(
            jax.ShapeDtypeStruct((rows, local_query), BF16),
            jax.ShapeDtypeStruct((rank, rows), BF16),
            jax.ShapeDtypeStruct((count, chunk, 128), BF16),
            jax.ShapeDtypeStruct((8, 128), F32),
        ),
        in_specs=[hbm, vmem, hbm, hbm, vmem, hbm, hbm, hbm, vmem],
        out_specs=[hbm, vmem, vmem, vmem],
        scratch_shapes=[
            pltpu.VMEM((rows, width), BF16),
            pltpu.VMEM((rows, heads, head_dim), BF16),
            pltpu.VMEM((kv_count, group, rows, head_dim), BF16),
            pltpu.VMEM((rows, width), BF16),
            pltpu.VMEM((rank, width), BF16),
            pltpu.VMEM((rank, local_query), BF16),
            pltpu.VMEM((toks, head_dim), F32),
            pltpu.VMEM((toks, head_dim), F32),
            pltpu.VMEM((depth * kv_count * 2, head_dim), BF16),
            pltpu.VMEM((depth * kv_count * 2, head_dim), F32),
            pltpu.VMEM((2, 2, nz * depth, kv_count * head_dim), BF16),
            pltpu.VMEM((NY, rows, depth * nz // 2), BF16),
            pltpu.VMEM((toks, depth * nz), BF16),
            pltpu.VMEM((rows, 128), F32),
            pltpu.VMEM((rows, 128), F32),
            pltpu.VMEM((rank, rows), F32),
            pltpu.VMEM((rank, rows), F32),
            pltpu.VMEM((rank, rows), BF16),
            pltpu.VMEM((2, rank, rows), BF16),
            pltpu.VMEM((2, rank, local_query), BF16),
            pltpu.VMEM((NY, 8, rows), jnp.int32),
            pltpu.VMEM((nz, 8, rows), jnp.int32),
            pltpu.VMEM((NY, toks, head_dim), F32),
            pltpu.VMEM((NY - 1, toks, head_dim), F32),
            pltpu.VMEM((NY, toks, head_dim), BF16),
            pltpu.VMEM((NY - 1, toks, head_dim), BF16),
            pltpu.VMEM((nz, 2, toks, head_dim), BF16),
            pltpu.VMEM((nz, 2, head_dim, toks), BF16),
            pltpu.VMEM((group, toks, head_dim), BF16),
            pltpu.VMEM((nz, 2 * toks, toks), F32),
            pltpu.VMEM((group, 1, toks), F32),
            pltpu.VMEM((2, 2, toks, toks), F32),
            pltpu.VMEM((2, 2 * toks, toks), BF16),
            pltpu.VMEM((head_dim + 16, 2 * toks), BF16),
            pltpu.VMEM((group, head_dim + 8, toks), F32),
            pltpu.VMEM((toks, group * head_dim), BF16),
            pltpu.VMEM((2, rank, rows), F32),
            pltpu.VMEM((NY, rank, rows), F32),
            pltpu.VMEM((count, rank, 128), BF16),
            pltpu.VMEM((count - 1, rank, 128), BF16),
            pltpu.VMEM((2 * group, 8, 128), BF16),
            pltpu.VMEM((2 * nz, 8, 128), BF16),
            pltpu.VMEM((8, 128), F32),
            pltpu.VMEM((peers, 8, 128), F32),
            pltpu.VMEM((count, 8, 128), F32),
            pltpu.VMEM((rows, local_query), BF16),
            dma((2, 2, steps)),
            dma((2, 2, steps)),
            dma((2, nz)),
            dma((2, nz)),
            dma((2, 2, steps)),
            dma((2, 2, steps)),
            dma((2, nz)),
            dma((2, nz)),
            dma((2, steps)),
            dma((2, steps)),
            dma((NY,)),
            dma((2, 2)),
            dma((2,)),
            dma((2,)),
            dma((2, NY - 1)),
            dma((2, NY - 1)),
            dma((NY - 1,)),
            dma((NY - 1,)),
            dma((3,)),
            dma((3,)),
            dma((NY - 1,)),
            dma((2,)),
            dma((2,)),
            dma((2,)),
            dma((2, 2)),
            dma((NY,)),
            dma((count - 1,)),
            dma((count - 1,)),
            dma((2 * group,)),
            dma((2 * nz,)),
            dma((count - 1,)),
            dma((count - 1,)),
            dma((peers,)),
            dma((peers,)),
            dma((count - 1,)),
            dma((count - 1,)),
            dma((8,)),
            dma((2,)),
        ],
        compiler_params=pltpu.CompilerParams(collective_id=0, has_side_effects=True),
        name="main",
    )(
        hidden[0],
        gain,
        w,
        queries[0],
        freqs,
        out_grad[0],
        adapt_up[0],
        adapt_down[0],
        doc_ids[None],
    )

    ceiling = 0.5 * math.sqrt(sections * rank * (local_query + width) * 2)
    return pl.pallas_call(
        lambda *refs: finish_kernel(ceiling, *refs),
        out_shape=(
            jax.ShapeDtypeStruct((rows, local_query), BF16),
            jax.ShapeDtypeStruct((rows, width), BF16),
            jax.ShapeDtypeStruct((rank, local_query), F32),
            jax.ShapeDtypeStruct((rank, width), F32),
        ),
        in_specs=[hbm] * 5,
        out_specs=[hbm] * 4,
        scratch_shapes=[
            pltpu.VMEM((rows, local_query), BF16),
            pltpu.VMEM((rank, rows), BF16),
            pltpu.VMEM((count, chunk, 128), BF16),
            pltpu.VMEM((8, 128), F32),
            pltpu.VMEM((rank, width), BF16),
            pltpu.VMEM((rows, width), BF16),
            pltpu.VMEM((rank, local_query), F32),
            pltpu.VMEM((rank, width), F32),
            dma((6,)),
            dma((8,)),
        ],
        name="finish",
    )(att, low, summed, squares, adapt_up[0])


def solution(mesh):
    def step(*args):
        return tuple(out[None] for out in per_device(*args))

    return jax.shard_map(
        step,
        mesh=mesh,
        in_specs=(
            P("section", "ctx", "tp"),
            P("section", "tp"),
            P("section", "ctx", "tp", None),
            P("section", "ctx", "tp", None, None),
            P("section", None, "tp"),
            P("section", None, "tp"),
            P("section", "ctx", "tp"),
            P("ctx"),
        ),
        out_specs=(
            P("section", "ctx", "tp"),
            P("section", "ctx", "tp"),
            P("section", None, "tp"),
            P("section", None, "tp"),
        ),
        check_vma=False,
    )
```

```python
import math

import jax
import jax.numpy as jnp
import numpy as np
from jax import lax
from jax.experimental import pallas as pl
from jax.experimental.pallas import tpu as pltpu
from jax.sharding import PartitionSpec as P

MESH = pl.DeviceIdType.MESH
NY = 4
PIECE = 64
F32 = jnp.float32
BF16 = jnp.bfloat16


def remote(src, dst, send_sem, recv_sem, **where):
    return pltpu.make_async_remote_copy(
        src_ref=src,
        dst_ref=dst,
        send_sem=send_sem,
        recv_sem=recv_sem,
        device_id=where,
        device_id_type=MESH,
    )


def position():
    ctx = lax.axis_index("ctx")
    return ctx // NY, ctx % NY, lax.axis_index("tp")


class Ring:
    def __init__(self, nz, half, send, recv, sib_send, sib_recv):
        self.nz, self.steps = nz, nz // 2
        self.half = half
        self.send, self.recv = send, recv
        self.sib_send, self.sib_recv = sib_send, sib_recv
        self.z, self.y, self.t = position()

    def origin(self, d, s):
        return (self.z - s + self.nz) % self.nz if d == 0 else (self.z + s) % self.nz

    def neighbour(self, d):
        z = (self.z + 1) % self.nz if d == 0 else (self.z + self.nz - 1) % self.nz
        return dict(ctx=z * NY + self.y, tp=self.t)

    def carried(self, d, s):
        return (0, 1) if s < self.steps else (d,)

    def copy(self, d, s, zi, i):
        piece = self.half(zi, i, self.t)
        return remote(
            piece,
            piece,
            self.send.at[d, s - 1, i],
            self.recv.at[d, s - 1, i],
            **self.neighbour(d),
        )

    def hop(self, d, s, i):
        return self.copy(d, s, self.origin(d, s - 1), i)

    def arrival(self, d, s, i):
        return self.copy(d, s, self.origin(d, s), i)

    def aside(self, index, zi, core, i):
        piece = self.half(zi, i, core)
        return remote(
            piece, piece, self.sib_send.at[index, i], self.sib_recv.at[index, i], tp=1 - self.t
        )

    def start(self):
        for i in (0, 1):
            for d in (0, 1):
                if i in self.carried(d, 1):
                    self.hop(d, 1, i).start()
        for i in (0, 1):
            self.aside(0, self.z, self.t, i).start()

    def step(self, s):
        for i in (0, 1):
            for d in (0, 1):
                self.arrival(d, s, i).wait_recv()
                if i in self.carried(d, s + 1):
                    self.hop(d, s + 1, i).start()
                self.aside(2 * s - 1 + d, self.origin(d, s), self.t, i).start()

    def final(self):
        for d in (0, 1):
            self.arrival(d, self.steps, d).wait_recv()
            self.aside(self.nz - 1, self.origin(0, self.steps), self.t, d).start()

    def asides(self):
        yield 0, self.z
        for s in range(1, self.steps):
            for d in (0, 1):
                yield 2 * s - 1 + d, self.origin(d, s)
        yield self.nz - 1, self.origin(0, self.steps)

    def wait_aside(self, index, zi):
        for i in (0, 1):
            self.aside(index, zi, 1 - self.t, i).wait_recv()

    def wait_sibling(self):
        for index, zi in self.asides():
            self.wait_aside(index, zi)

    def drain(self):
        for d in (0, 1):
            for s in range(1, self.steps + 1):
                for i in self.carried(d, s):
                    self.hop(d, s, i).wait_send()
        for index, zi in self.asides():
            for i in (0, 1):
                self.aside(index, zi, self.t, i).wait_send()


def main_kernel(
    nz,
    sections,
    hid_hbm,
    gain_ref,
    w_hbm,
    q_hbm,
    freq_ref,
    grad_hbm,
    up_hbm,
    down_hbm,
    doc_ref,
    att_hbm,
    low_out,
    all_buf,
    norm_out,
    hid_ref,
    q_raw,
    q_ref,
    grad_ref,
    up_ref,
    down_ref,
    cos_ref,
    sin_ref,
    w_raw,
    w_wide,
    w_buf,
    normed,
    x_buf,
    square_src,
    square_in,
    back_part,
    back_in,
    back_own,
    back_all,
    down_buf,
    doc_in,
    doc_all,
    k_part,
    k_in,
    v_part,
    v_in,
    k_all,
    v_all,
    q_all,
    bias_ref,
    top,
    s_buf,
    p_buf,
    v_ext,
    acc,
    att,
    low_src,
    low_in,
    red_src,
    red_in,
    dred_src,
    dred_in,
    sq_src,
    sq_in,
    sq_all,
    att_out,
    w_send,
    w_recv,
    ws_send,
    ws_recv,
    kv_send,
    kv_recv,
    kvs_send,
    kvs_recv,
    d_send,
    d_recv,
    x_send,
    x_recv,
    q_send,
    q_recv,
    rs_send,
    rs_recv,
    dy_send,
    dy_recv,
    pair_send,
    pair_recv,
    back_send,
    back_recv,
    att_send,
    att_recv,
    low_send,
    low_recv,
    red_send,
    red_recv,
    dred_send,
    dred_recv,
    all_send,
    all_recv,
    sq_send,
    sq_recv,
    sqa_send,
    sqa_recv,
    load_sem,
    own_sem,
):
    z, y, t = position()
    section = lax.axis_index("section")
    rows, width = hid_ref.shape
    depth = w_buf.shape[2] // nz
    cols = depth * nz // 2
    head_dim = k_all.shape[-1]
    heads = q_all.shape[0]
    toks = 2 * rows
    keys = 2 * toks
    rank = up_ref.shape[0]
    count = nz * NY
    me = z * NY + y
    steps = nz // 2
    home = y // 2
    sibling = dict(tp=1 - t)
    peers = [(osec, ot) for osec in range(sections) for ot in range(2) if osec or ot]

    barrier = pltpu.get_barrier_semaphore()

    def greet(**where):
        pl.semaphore_signal(barrier, inc=1, device_id=where, device_id_type=MESH)

    greet(ctx=(z + 1) % nz * NY + y)
    greet(ctx=(z + nz - 1) % nz * NY + y)
    for oy in range(NY):
        for ot in range(2):
            if oy or ot:
                greet(ctx=z * NY + (y + oy) % NY, tp=(t + ot) % 2)
    for osec, ot in peers:
        if osec:
            greet(section=(section + osec) % sections, tp=(t + ot) % 2)
    slab = rows // 4
    hid_loads = [
        pltpu.make_async_copy(
            hid_hbm.at[pl.ds(i * slab, slab)], hid_ref.at[pl.ds(i * slab, slab)], load_sem.at[i]
        )
        for i in range(4)
    ]
    late_loads = [
        pltpu.make_async_copy(src, dst, load_sem.at[4 + i])
        for i, (src, dst) in enumerate(
            ((q_hbm, q_raw), (grad_hbm, grad_ref), (up_hbm, up_ref), (down_hbm, down_ref))
        )
    ]
    w_load = pltpu.make_async_copy(w_hbm, w_raw, own_sem.at[0])
    w_load.start()
    for load in hid_loads:
        load.start()
    own_rows = pl.ds(pl.multiple_of(z * depth, depth), depth)
    w_load.wait()
    w_wide[...] = w_raw[...].astype(F32)
    for p in (0, 1):
        for h in range(2):
            w_buf[p, t, own_rows, h * head_dim : (h + 1) * head_dim] = w_wide[
                pl.ds(2 * h + p, depth, stride=4), :
            ].astype(BF16)
    pl.semaphore_wait(barrier, 2 + 2 * NY - 1 + 2 * (sections - 1))

    def w_half(p):
        return lambda zi, h, core: w_buf.at[
            p, core, pl.ds(pl.multiple_of(zi * depth + h * (depth // 2), depth // 2), depth // 2)
        ]

    def kv_half(buf):
        size = buf.shape[2] // 2
        return lambda zi, h, core: buf.at[zi, core, pl.ds(h * size, size)]

    w_rings = [
        Ring(nz, w_half(p), w_send.at[p], w_recv.at[p], ws_send.at[p], ws_recv.at[p])
        for p in (0, 1)
    ]
    kv_rings = [
        Ring(nz, kv_half(buf), kv_send.at[p], kv_recv.at[p], kvs_send.at[p], kvs_recv.at[p])
        for p, buf in ((0, k_all), (1, v_all))
    ]

    w_rings[0].start()
    for load in late_loads:
        load.start()

    doc_own = doc_in.at[0]
    doc_in[0] = jnp.broadcast_to(doc_ref[...], doc_in.shape[1:])

    def doc_copy(oy):
        return remote(
            doc_own,
            doc_in.at[oy],
            dy_send.at[oy - 1],
            dy_recv.at[oy - 1],
            ctx=z * NY + (y + oy) % NY,
        )

    for oy in range(1, NY):
        doc_copy(oy).start()

    def down_copy(core):
        return remote(down_ref, down_buf.at[core], pair_send.at[0], pair_recv.at[0], **sibling)

    for i, load in enumerate(hid_loads):
        load.wait()
        hid = hid_ref[i * slab : (i + 1) * slab, :].astype(F32)
        square = jnp.sum(hid * hid, axis=1, keepdims=True)
        square_src[i * slab : (i + 1) * slab, :] = jnp.broadcast_to(square, (slab, 128))
    square_copy = remote(square_src, square_in, pair_send.at[1], pair_recv.at[1], **sibling)
    square_copy.start()
    square_copy.wait_recv()
    mean = (square_src[:, :1] + square_in[:, :1]) * (1.0 / (2 * width))
    scale = lax.rsqrt(mean + 1e-06)

    def x_dest(b, core):
        return x_buf.at[pl.ds(b * rows, rows), pl.ds(pl.multiple_of(core * cols, cols), cols)]

    def x_copy(oy):
        yd = (y + oy) % NY
        return remote(
            normed.at[yd],
            x_dest(y % 2, t),
            x_send.at[oy],
            x_recv.at[y % 2, t],
            ctx=z * NY + yd,
            tp=home,
        )

    for yd in range(NY):
        for zl in range(nz // 2):
            start = (zl * NY + yd) * depth
            piece = hid_ref[:, start : start + depth].astype(F32)
            gain = gain_ref[:, start : start + depth].astype(F32)
            normed[yd, :, zl * depth : (zl + 1) * depth] = (piece * scale * gain).astype(BF16)
    for oy in range(1, NY):
        x_copy(oy).start()

    @pl.when(t != home)
    def _():
        x_copy(0).start()

    @pl.when(t == home)
    def _():
        x_buf[
            pl.ds(pl.multiple_of((y % 2) * rows, rows), rows),
            pl.ds(pl.multiple_of(t * cols, cols), cols),
        ] = normed[y]

    late_loads[0].wait()
    turned_q = jnp.transpose(q_raw[...].astype(F32), (1, 0, 2)).astype(BF16)
    q_ref[...] = turned_q.reshape(q_ref.shape)

    def q_dest(b):
        return q_all.at[:, pl.ds(b * rows, rows)]

    def q_copy(kvl):
        return remote(
            q_ref.at[kvl],
            q_dest(y % 2),
            q_send.at[kvl],
            q_recv.at[y % 2],
            ctx=z * NY + 2 * t + kvl,
            tp=home,
        )

    def home_own(kvl):
        return jnp.logical_and(2 * t + kvl == y, home == t)

    for kvl in range(2):

        @pl.when(jnp.logical_not(home_own(kvl)))
        def _():
            q_copy(kvl).start()

        @pl.when(home_own(kvl))
        def _():
            q_all[:, pl.ds(pl.multiple_of((y % 2) * rows, rows), rows), :] = q_ref[kvl]

    for oy in range(1, NY):
        doc_copy(oy).wait_recv()
    line = lax.broadcasted_iota(jnp.int32, doc_in.shape[1:], 0)
    group = jnp.where(line == y, doc_in[0], 0)
    for oy in range(1, NY):
        group = jnp.where(line == (y + NY - oy) % NY, doc_in[oy], group)
    doc_all[z] = group

    def doc_pass(d, s):
        zi = (z - s + 1 + nz) % nz if d == 0 else (z + s - 1) % nz
        to = (z + 1) % nz if d == 0 else (z + nz - 1) % nz
        return remote(
            doc_all.at[zi], doc_all.at[zi], d_send.at[d, s - 1], d_recv.at[d, s - 1], ctx=to * NY + y
        )

    def doc_arrive(d, s):
        zi = (z - s + nz) % nz if d == 0 else (z + s) % nz
        to = (z + 1) % nz if d == 0 else (z + nz - 1) % nz
        return remote(
            doc_all.at[zi], doc_all.at[zi], d_send.at[d, s - 1], d_recv.at[d, s - 1], ctx=to * NY + y
        )

    doc_hops = [(0, s) for s in range(1, steps + 1)] + [(1, s) for s in range(1, steps)]

    def doc_step(s):
        for d in (0, 1):
            if (d, s) in doc_hops:
                doc_arrive(d, s).wait_recv()
                if (d, s + 1) in doc_hops:
                    doc_pass(d, s + 1).start()

    for d in (0, 1):
        if (d, 1) in doc_hops:
            doc_pass(d, 1).start()

    late_loads[3].wait()
    down_copy(t).start()
    down_buf[t] = down_ref[...]
    late_loads[1].wait()
    late_loads[2].wait()
    back_part[...] = lax.dot_general(
        up_ref[...], grad_ref[...], (((1,), (1,)), ((), ())), preferred_element_type=F32
    )
    back_copy = remote(back_part, back_in, pair_send.at[2], pair_recv.at[2], **sibling)
    back_copy.start()

    def back_pass(oy):
        return remote(
            back_own,
            back_all.at[y % 2],
            back_send.at[oy - 1],
            back_recv.at[y % 2],
            ctx=z * NY + (y + oy) % NY,
        )

    for s in range(1, steps):
        w_rings[0].step(s)
        if s == max(1, steps - 2):
            w_rings[1].start()
        doc_step(s)
        if s == 2:
            lane = lax.broadcasted_iota(jnp.int32, cos_ref.shape, 1)
            token = lax.broadcasted_iota(jnp.int32, cos_ref.shape, 0) + (z * 2 + t) * toks
            angles = token.astype(F32) * freq_ref[...]
            cos_ref[...] = jnp.cos(angles)
            sine = jnp.sin(angles)
            sin_ref[...] = jnp.where(lane < head_dim // 2, -sine, sine)
        if s == 1:
            back_copy.wait_recv()
            back_own[...] = (back_part[...] + back_in[...]).astype(BF16)

            @pl.when(t == home)
            def _():
                for oy in range(1, NY):
                    back_pass(oy).start()
                back_all[y % 2] = back_own[...]

    def x_wait():
        for b in range(2):
            for core in range(2):

                @pl.when(jnp.logical_or(2 * t + b != y, t != core))
                def _():
                    dest = x_dest(b, core)
                    remote(dest, dest, x_send.at[0], x_recv.at[b, core], **sibling).wait_recv()

    def project(p, part):
        w_rings[p].final()
        for core in (t, 1 - t):
            if core is not t:
                w_rings[p].wait_sibling()
            partial = jnp.dot(x_buf[...], w_buf[p, core], preferred_element_type=F32)
            for hl in range(2):
                part[2 * core + hl] = partial[:, hl * head_dim : (hl + 1) * head_dim].astype(part.dtype)

    def scatter_copy(p, oy):
        part, into = ((k_part, k_in), (v_part, v_in))[p]
        yd = (y + oy) % NY
        return remote(
            part.at[yd],
            into.at[oy - 1],
            rs_send.at[p, oy - 1],
            rs_recv.at[p, oy - 1],
            ctx=z * NY + yd,
        )

    def collect(p):
        part, into = ((k_part, k_in), (v_part, v_in))[p]
        for oy in range(1, NY):
            scatter_copy(p, oy).wait_recv()
        whole = part[y].astype(F32)
        for oy in range(1, NY):
            whole = whole + into[oy - 1].astype(F32)
        return whole

    def rope(v):
        return (v * cos_ref[...] + pltpu.roll(v, head_dim // 2, 1) * sin_ref[...]).astype(BF16)

    w_rings[1].step(1)
    x_wait()
    project(0, k_part)
    for oy in range(1, NY):
        scatter_copy(0, oy).start()
    for s in range(2, steps):
        w_rings[1].step(s)
    project(1, v_part)
    for oy in range(1, NY):
        scatter_copy(1, oy).start()

    for b in range(2):

        @pl.when(jnp.logical_or(2 * t + b != y, home != t))
        def _():
            dest = q_dest(b)
            remote(dest, dest, q_send.at[0], q_recv.at[b], **sibling).wait_recv()

    for h in range(heads):
        q_all[h] = rope(q_all[h].astype(F32))
    doc_step(steps)
    q_doc = jnp.concatenate(
        [
            jnp.sum(jnp.where(line == 2 * t + b, doc_all[z].astype(F32), 0.0), axis=0, keepdims=True)
            for b in range(2)
        ],
        axis=1,
    )

    q_pos = (z * 2 + t) * toks + lax.broadcasted_iota(jnp.int32, (keys, toks), 1)
    k_pos = lax.broadcasted_iota(jnp.int32, (keys, toks), 0)

    def mask(kb, carry):
        turned = jnp.transpose(doc_all[kb].astype(F32))
        k_doc = jnp.concatenate([turned[:, j : j + 1] for j in range(NY)], axis=0)
        allowed = jnp.logical_and(k_doc == q_doc, k_pos + kb * keys <= q_pos)
        bias_ref[kb] = jnp.where(allowed, 0.0, -1e30)
        return carry

    lax.fori_loop(0, nz, mask, 0)

    k_all[z, t] = rope(collect(0))
    kv_rings[0].start()
    v_all[z, t] = jnp.transpose(collect(1)).astype(BF16)
    kv_rings[1].start()

    factor = head_dim ** (-0.5) * math.log2(math.e)

    def block(kb, first):
        for core in range(2):
            v_ext[:head_dim, core * toks : (core + 1) * toks] = v_all[kb, core]

        tops, shrinks = {}, {}

        def score(h):
            q = q_all[h]
            slot = h % 2
            peak = None
            for core in range(2):
                scores = (
                    lax.dot_general(
                        k_all[kb, core], q, (((1,), (1,)), ((), ())), preferred_element_type=F32
                    )
                    + bias_ref[kb, core * toks : (core + 1) * toks, :]
                )
                s_buf[slot, core] = scores
                here = jnp.max(scores, axis=0, keepdims=True)
                peak = here if peak is None else jnp.maximum(peak, here)
            if not first:
                old_top = top[h]
                peak = jnp.maximum(old_top, peak)
                shrinks[h] = jnp.exp2((old_top - peak) * factor)
            top[h] = peak
            tops[h] = peak

        def weigh(h):
            slot = h % 2
            for core in range(2):
                for r in range(0, toks, PIECE):
                    p_buf[slot, core * toks + r : core * toks + r + PIECE, :] = jnp.exp2(
                        (s_buf[slot, core, r : r + PIECE, :] - tops[h]) * factor
                    ).astype(BF16)

        def mix(h):
            slot = h % 2
            part = jnp.dot(v_ext[...], p_buf[slot], preferred_element_type=F32)[: head_dim + 8]
            acc[h] = part if first else acc[h] * shrinks[h] + part

        for i in range(heads + 2):
            if i < heads:
                score(i)
            if 0 <= i - 1 < heads:
                weigh(i - 1)
            if i >= 2:
                mix(i - 2)

    def await_aside(index, zi):
        for ring in kv_rings:
            ring.wait_aside(index, zi)

    def attend_step(s):
        def one(d, carry):
            zi = jnp.where(d == 0, z - s + nz, z + s) % nz
            await_aside(2 * s - 1 + d, zi)

            @pl.when(zi < z)
            def _():
                block(zi, False)

            return carry

        lax.fori_loop(0, 2, one, 0)

    v_ext[head_dim:, :] = jnp.ones((16, 2 * toks), BF16)
    await_aside(0, z)
    block(z, True)
    for s in range(1, steps):
        kv_rings[0].step(s)
        kv_rings[1].step(s)
        attend_step(s)
    kv_rings[0].final()
    kv_rings[1].final()
    last = kv_rings[0].origin(0, steps)
    await_aside(nz - 1, last)

    @pl.when(last < z)
    def _():
        block(last, False)

    down_copy(1 - t).wait_recv()
    half_cols = heads * head_dim
    low = None
    for h in range(heads):
        out = acc[h, :head_dim, :] / acc[h, head_dim : head_dim + 1, :]
        factor_cols = down_buf[
            home, :, pl.ds(pl.multiple_of((y % 2) * half_cols + h * head_dim, head_dim), head_dim)
        ]
        part = jnp.dot(factor_cols, out.astype(BF16), preferred_element_type=F32)
        low = part if low is None else low + part
        att[:, h * head_dim : (h + 1) * head_dim] = jnp.transpose(out).astype(BF16)

    def low_copy(b, core):
        return remote(
            low_src.at[b],
            low_in.at[y],
            low_send.at[b, core],
            low_recv.at[y],
            ctx=z * NY + 2 * t + b,
            tp=core,
        )

    def low_own(b, core):
        return jnp.logical_and(2 * t + b == y, t == core)

    for b in range(2):
        low_src[b] = low[:, b * rows : (b + 1) * rows]
    for b in range(2):
        for core in range(2):

            @pl.when(jnp.logical_not(low_own(b, core)))
            def _():
                low_copy(b, core).start()

            @pl.when(low_own(b, core))
            def _():
                low_in[y] = low_src[b]

    for b in range(2):

        @pl.when(2 * t + b != y)
        def _():
            remote(
                back_all.at[b], back_all.at[b], back_send.at[0], back_recv.at[b], **sibling
            ).wait_recv()

    back = jnp.concatenate([back_all[0], back_all[1]], axis=1)
    down_part = jnp.dot(back, att[...], preferred_element_type=F32)
    for r in range(2):
        for h in range(heads):
            dred_src[r * heads + h] = down_part[8 * r : 8 * r + 8, h * 128 : (h + 1) * 128].astype(BF16)
    blocks = count // 2

    def dred_owner(i):
        return (i // heads) * blocks + (y % 2) * heads + i % heads

    def dred_copy(i):
        return remote(
            dred_src.at[i],
            dred_in.at[2 * z + t],
            dred_send.at[i],
            dred_recv.at[2 * z + t],
            ctx=dred_owner(i),
            tp=home,
        )

    def dred_own(i):
        return jnp.logical_and(dred_owner(i) == me, home == t)

    def dred_start(i, carry):
        @pl.when(jnp.logical_not(dred_own(i)))
        def _():
            dred_copy(i).start()

        @pl.when(dred_own(i))
        def _():
            dred_in[2 * z + t] = dred_src[i]

        return carry

    lax.fori_loop(0, 2 * heads, dred_start, 0)

    for src_y in range(NY):

        @pl.when(jnp.logical_or(src_y != y, home != t))
        def _():
            remote(
                low_in.at[src_y], low_in.at[src_y], low_send.at[0, 0], low_recv.at[src_y], **sibling
            ).wait_recv()

    low = low_in[0]
    for src_y in range(1, NY):
        low = low + low_in[src_y]
    low = low.astype(BF16)
    low_out[...] = low

    for c in range(count):
        red_src[c] = jnp.dot(
            low, grad_ref[:, c * 128 : (c + 1) * 128], preferred_element_type=F32
        ).astype(BF16)

    def red_copy(o):
        to = (me + o) % count
        return remote(
            red_src.at[to], red_in.at[o - 1], red_send.at[o - 1], red_recv.at[o - 1], ctx=to
        )

    def red_start(o, carry):
        red_copy(o).start()
        return carry

    lax.fori_loop(1, count, red_start, 0)

    def att_dest(kvl):
        return att_out.at[:, pl.ds(pl.multiple_of(kvl * half_cols, half_cols), half_cols)]

    def att_copy(b):
        return remote(
            att.at[pl.ds(b * rows, rows)],
            att_dest(y % 2),
            att_send.at[b],
            att_recv.at[y % 2],
            ctx=z * NY + 2 * t + b,
            tp=home,
        )

    for b in range(2):

        @pl.when(jnp.logical_not(home_own(b)))
        def _():
            att_copy(b).start()

        @pl.when(home_own(b))
        def _():
            att_out[:, pl.ds(pl.multiple_of((y % 2) * half_cols, half_cols), half_cols)] = att[
                b * rows : (b + 1) * rows
            ]

    down_y = 2 * t + (me % blocks) // heads

    def dred_add(i, carry):
        @pl.when(jnp.logical_or(down_y != y, i != 2 * z + t))
        def _():
            remote(
                dred_in.at[i], dred_in.at[i], dred_send.at[0], dred_recv.at[i], **sibling
            ).wait_recv()

        return carry + dred_in[i].astype(F32)

    down_sum = lax.fori_loop(0, 2 * nz, dred_add, jnp.zeros((8, 128), F32))

    def red_add(o, so_far):
        red_copy(o).wait_recv()
        return so_far + red_in[o - 1].astype(F32)

    up_sum = lax.fori_loop(1, count, red_add, red_src[me].astype(F32))
    all_buf[me] = jnp.concatenate([up_sum, down_sum], axis=0).astype(BF16)
    squares = jnp.sum(up_sum * up_sum, axis=0, keepdims=True) + jnp.sum(
        down_sum * down_sum, axis=0, keepdims=True
    )
    sq_src[...] = jnp.broadcast_to(jnp.sum(squares, axis=1, keepdims=True), sq_src.shape)

    def sq_copy(i):
        osec, ot = peers[i]
        return remote(
            sq_src,
            sq_in.at[i],
            sq_send.at[i],
            sq_recv.at[i],
            section=(section + osec) % sections,
            tp=(t + ot) % 2,
        )

    for i in range(len(peers)):
        sq_copy(i).start()

    def spread(buf, sends, recvs):
        def copy(o):
            to = (me + o) % count
            return remote(buf.at[me], buf.at[me], sends.at[o - 1], recvs.at[o - 1], ctx=to)

        def arrive(o):
            of = (me - o + count) % count
            return remote(buf.at[of], buf.at[of], sends.at[o - 1], recvs.at[o - 1], ctx=of)

        def each(act):
            def one(o, carry):
                act(o)
                return carry

            lax.fori_loop(1, count, one, 0)

        return (
            lambda: each(lambda o: copy(o).start()),
            lambda: each(lambda o: arrive(o).wait_recv()),
            lambda: each(lambda o: copy(o).wait_send()),
        )

    all_start, all_wait, all_drain = spread(all_buf, all_send, all_recv)
    sqa_start, sqa_wait, sqa_drain = spread(sq_all, sqa_send, sqa_recv)
    all_start()
    squares = sq_src[...]
    for i in range(len(peers)):
        sq_copy(i).wait_recv()
        squares = squares + sq_in[i]
    sq_all[me] = squares
    sqa_start()

    for ring in w_rings + kv_rings:
        ring.drain()
    for oy in range(1, NY):
        doc_copy(oy).wait_send()
        x_copy(oy).wait_send()
        scatter_copy(0, oy).wait_send()
        scatter_copy(1, oy).wait_send()

    @pl.when(t != home)
    def _():
        x_copy(0).wait_send()

    @pl.when(t == home)
    def _():
        for oy in range(1, NY):
            back_pass(oy).wait_send()

    for d, s in doc_hops:
        doc_pass(d, s).wait_send()
    down_copy(t).wait_send()
    square_copy.wait_send()
    back_copy.wait_send()
    for b in range(2):

        @pl.when(jnp.logical_not(home_own(b)))
        def _():
            q_copy(b).wait_send()
            att_copy(b).wait_send()

        for core in range(2):

            @pl.when(jnp.logical_not(low_own(b, core)))
            def _():
                low_copy(b, core).wait_send()

    def dred_drain(i, carry):
        @pl.when(jnp.logical_not(dred_own(i)))
        def _():
            dred_copy(i).wait_send()

        return carry

    lax.fori_loop(0, 2 * heads, dred_drain, 0)

    def red_drain(o, carry):
        red_copy(o).wait_send()
        return carry

    lax.fori_loop(1, count, red_drain, 0)
    for kvl in range(2):

        @pl.when(jnp.logical_or(2 * t + kvl != y, home != t))
        def _():
            dest = att_dest(kvl)
            remote(dest, dest, att_send.at[0], att_recv.at[kvl], **sibling).wait_recv()

    att_store = pltpu.make_async_copy(att_out, att_hbm, own_sem.at[1])
    att_store.start()
    all_wait()
    all_drain()
    for i in range(len(peers)):
        sq_copy(i).wait_send()
    sqa_wait()
    sqa_drain()
    norm = sq_all[0]
    for c in range(1, count):
        norm = norm + sq_all[c]
    norm_out[...] = norm
    att_store.wait()


def finish_kernel(
    ceiling,
    att_hbm,
    low_hbm,
    all_hbm,
    sq_hbm,
    up_hbm,
    att_out,
    adapter_out,
    gdown_out,
    gup_out,
    att_ref,
    low_ref,
    all_ref,
    sq_ref,
    up_ref,
    adapter,
    gdown,
    gup,
    in_sem,
    out_sem,
):
    count = all_ref.shape[0]
    rank, rows = low_ref.shape
    width = up_ref.shape[1]
    blocks = count // 2
    ins = [
        pltpu.make_async_copy(src, dst, in_sem.at[i])
        for i, (src, dst) in enumerate(
            (
                (low_hbm, low_ref),
                (up_hbm, up_ref),
                (sq_hbm, sq_ref),
                (all_hbm, all_ref),
                (att_hbm.at[pl.ds(0, rows // 2)], att_ref.at[pl.ds(0, rows // 2)]),
                (att_hbm.at[pl.ds(rows // 2, rows // 2)], att_ref.at[pl.ds(rows // 2, rows // 2)]),
            )
        )
    ]
    outs = []

    def put(src, dst):
        copy = pltpu.make_async_copy(src, dst, out_sem.at[len(outs)])
        copy.start()
        outs.append(copy)

    for copy in ins:
        copy.start()
    ins[0].wait()
    ins[1].wait()
    part = rows // 4
    low = jnp.transpose(low_ref[...].astype(F32)).astype(BF16)
    for i in range(4):
        adapter[i * part : (i + 1) * part, :] = jnp.dot(
            low[i * part : (i + 1) * part], up_ref[...], preferred_element_type=F32
        ).astype(BF16)
        put(adapter.at[pl.ds(i * part, part)], adapter_out.at[pl.ds(i * part, part)])
    for i in range(2):
        ins[4 + i].wait()
        half = pl.ds(i * (rows // 2), rows // 2)
        put(att_ref.at[half], att_out.at[half])
    ins[2].wait()
    ins[3].wait()
    clip = jnp.minimum(1.0, ceiling / (jnp.sqrt(sq_ref[0:1, 0:1]) + 1e-06))
    for c in range(count):
        r0 = 8 * (c // blocks)
        c0 = 128 * (c % blocks)
        gup[:, c * 128 : (c + 1) * 128] = all_ref[c, 0:rank, :].astype(F32) * clip
        gdown[r0 : r0 + 8, c0 : c0 + 128] = all_ref[c, rank : rank + 8, :].astype(F32) * clip
    put(gup, gup_out)
    put(gdown, gdown_out)
    for copy in outs:
        copy.wait()


def per_device(hidden, gain, queries, key_value_weight, adapt_down, adapt_up, out_grad, doc_ids):
    nz = lax.axis_size("ctx") // NY
    sections = lax.axis_size("section")
    rows, width = hidden.shape[1:]
    depth, kv_count = key_value_weight.shape[1:3]
    head_dim = key_value_weight.shape[-1]
    heads = queries.shape[2]
    group = heads // kv_count
    rank, local_query = adapt_down.shape[1:]
    toks = 2 * rows
    half = head_dim // 2
    freqs = (1000000.0 ** (-np.arange(half) * 2.0 / head_dim)).astype(np.float32)
    freqs = jnp.asarray(np.concatenate([freqs, freqs])[None])
    w = key_value_weight.reshape(depth * kv_count * 2, head_dim)

    vmem = pl.BlockSpec(memory_space=pltpu.VMEM)
    hbm = pl.BlockSpec(memory_space=pl.ANY)
    dma = pltpu.SemaphoreType.DMA
    steps = nz // 2
    count = nz * NY
    peers = 2 * sections - 1
    chunk = rank + 8
    att, low, summed, squares = pl.pallas_call(
        lambda *refs: main_kernel(nz, sections, *refs),
        out_shape=(
            jax.ShapeDtypeStruct((rows, local_query), BF16),
            jax.ShapeDtypeStruct((rank, rows), BF16),
            jax.ShapeDtypeStruct((count, chunk, 128), BF16),
            jax.ShapeDtypeStruct((8, 128), F32),
        ),
        in_specs=[hbm, vmem, hbm, hbm, vmem, hbm, hbm, hbm, vmem],
        out_specs=[hbm, vmem, vmem, vmem],
        scratch_shapes=[
            pltpu.VMEM((rows, width), BF16),
            pltpu.VMEM((rows, heads, head_dim), BF16),
            pltpu.VMEM((kv_count, group, rows, head_dim), BF16),
            pltpu.VMEM((rows, width), BF16),
            pltpu.VMEM((rank, width), BF16),
            pltpu.VMEM((rank, local_query), BF16),
            pltpu.VMEM((toks, head_dim), F32),
            pltpu.VMEM((toks, head_dim), F32),
            pltpu.VMEM((depth * kv_count * 2, head_dim), BF16),
            pltpu.VMEM((depth * kv_count * 2, head_dim), F32),
            pltpu.VMEM((2, 2, nz * depth, kv_count * head_dim), BF16),
            pltpu.VMEM((NY, rows, depth * nz // 2), BF16),
            pltpu.VMEM((toks, depth * nz), BF16),
            pltpu.VMEM((rows, 128), F32),
            pltpu.VMEM((rows, 128), F32),
            pltpu.VMEM((rank, rows), F32),
            pltpu.VMEM((rank, rows), F32),
            pltpu.VMEM((rank, rows), BF16),
            pltpu.VMEM((2, rank, rows), BF16),
            pltpu.VMEM((2, rank, local_query), BF16),
            pltpu.VMEM((NY, 8, rows), jnp.int32),
            pltpu.VMEM((nz, 8, rows), jnp.int32),
            pltpu.VMEM((NY, toks, head_dim), F32),
            pltpu.VMEM((NY - 1, toks, head_dim), F32),
            pltpu.VMEM((NY, toks, head_dim), BF16),
            pltpu.VMEM((NY - 1, toks, head_dim), BF16),
            pltpu.VMEM((nz, 2, toks, head_dim), BF16),
            pltpu.VMEM((nz, 2, head_dim, toks), BF16),
            pltpu.VMEM((group, toks, head_dim), BF16),
            pltpu.VMEM((nz, 2 * toks, toks), F32),
            pltpu.VMEM((group, 1, toks), F32),
            pltpu.VMEM((2, 2, toks, toks), F32),
            pltpu.VMEM((2, 2 * toks, toks), BF16),
            pltpu.VMEM((head_dim + 16, 2 * toks), BF16),
            pltpu.VMEM((group, head_dim + 8, toks), F32),
            pltpu.VMEM((toks, group * head_dim), BF16),
            pltpu.VMEM((2, rank, rows), F32),
            pltpu.VMEM((NY, rank, rows), F32),
            pltpu.VMEM((count, rank, 128), BF16),
            pltpu.VMEM((count - 1, rank, 128), BF16),
            pltpu.VMEM((2 * group, 8, 128), BF16),
            pltpu.VMEM((2 * nz, 8, 128), BF16),
            pltpu.VMEM((8, 128), F32),
            pltpu.VMEM((peers, 8, 128), F32),
            pltpu.VMEM((count, 8, 128), F32),
            pltpu.VMEM((rows, local_query), BF16),
            dma((2, 2, steps, 2)),
            dma((2, 2, steps, 2)),
            dma((2, nz, 2)),
            dma((2, nz, 2)),
            dma((2, 2, steps, 2)),
            dma((2, 2, steps, 2)),
            dma((2, nz, 2)),
            dma((2, nz, 2)),
            dma((2, steps)),
            dma((2, steps)),
            dma((NY,)),
            dma((2, 2)),
            dma((2,)),
            dma((2,)),
            dma((2, NY - 1)),
            dma((2, NY - 1)),
            dma((NY - 1,)),
            dma((NY - 1,)),
            dma((3,)),
            dma((3,)),
            dma((NY - 1,)),
            dma((2,)),
            dma((2,)),
            dma((2,)),
            dma((2, 2)),
            dma((NY,)),
            dma((count - 1,)),
            dma((count - 1,)),
            dma((2 * group,)),
            dma((2 * nz,)),
            dma((count - 1,)),
            dma((count - 1,)),
            dma((peers,)),
            dma((peers,)),
            dma((count - 1,)),
            dma((count - 1,)),
            dma((8,)),
            dma((2,)),
        ],
        compiler_params=pltpu.CompilerParams(collective_id=0, has_side_effects=True),
        name="main",
    )(
        hidden[0],
        gain,
        w,
        queries[0],
        freqs,
        out_grad[0],
        adapt_up[0],
        adapt_down[0],
        doc_ids[None],
    )

    ceiling = 0.5 * math.sqrt(sections * rank * (local_query + width) * 2)
    return pl.pallas_call(
        lambda *refs: finish_kernel(ceiling, *refs),
        out_shape=(
            jax.ShapeDtypeStruct((rows, local_query), BF16),
            jax.ShapeDtypeStruct((rows, width), BF16),
            jax.ShapeDtypeStruct((rank, local_query), F32),
            jax.ShapeDtypeStruct((rank, width), F32),
        ),
        in_specs=[hbm] * 5,
        out_specs=[hbm] * 4,
        scratch_shapes=[
            pltpu.VMEM((rows, local_query), BF16),
            pltpu.VMEM((rank, rows), BF16),
            pltpu.VMEM((count, chunk, 128), BF16),
            pltpu.VMEM((8, 128), F32),
            pltpu.VMEM((rank, width), BF16),
            pltpu.VMEM((rows, width), BF16),
            pltpu.VMEM((rank, local_query), F32),
            pltpu.VMEM((rank, width), F32),
            dma((6,)),
            dma((8,)),
        ],
        name="finish",
    )(att, low, summed, squares, adapt_up[0])


def solution(mesh):
    def step(*args):
        return tuple(out[None] for out in per_device(*args))

    return jax.shard_map(
        step,
        mesh=mesh,
        in_specs=(
            P("section", "ctx", "tp"),
            P("section", "tp"),
            P("section", "ctx", "tp", None),
            P("section", "ctx", "tp", None, None),
            P("section", None, "tp"),
            P("section", None, "tp"),
            P("section", "ctx", "tp"),
            P("ctx"),
        ),
        out_specs=(
            P("section", "ctx", "tp"),
            P("section", "ctx", "tp"),
            P("section", None, "tp"),
            P("section", None, "tp"),
        ),
        check_vma=False,
    )
```

```python
import math

import jax
import jax.numpy as jnp
import numpy as np
from jax import lax
from jax.experimental import pallas as pl
from jax.experimental.pallas import tpu as pltpu
from jax.sharding import PartitionSpec as P

MESH = pl.DeviceIdType.MESH
NY = 4
PIECE = 64
F32 = jnp.float32
BF16 = jnp.bfloat16


def remote(src, dst, send_sem, recv_sem, **where):
    return pltpu.make_async_remote_copy(
        src_ref=src,
        dst_ref=dst,
        send_sem=send_sem,
        recv_sem=recv_sem,
        device_id=where,
        device_id_type=MESH,
    )


def position():
    ctx = lax.axis_index("ctx")
    return ctx // NY, ctx % NY, lax.axis_index("tp")


class Ring:
    def __init__(self, nz, block, half, send, recv, sib_send=None, sib_recv=None):
        self.nz, self.steps = nz, nz // 2
        self.block, self.half = block, half
        self.send, self.recv = send, recv
        self.sib_send, self.sib_recv = sib_send, sib_recv
        self.z, self.y, self.t = position()

    def origin(self, d, s):
        return (self.z - s + self.nz) % self.nz if d == 0 else (self.z + s) % self.nz

    def neighbour(self, d):
        z = (self.z + 1) % self.nz if d == 0 else (self.z + self.nz - 1) % self.nz
        return dict(ctx=z * NY + self.y, tp=self.t)

    def piece(self, zi, d, s):
        return self.half(zi, d, self.t) if s == self.steps else self.block(zi, self.t)

    def hop(self, d, s, src=None):
        piece = self.piece(self.origin(d, s - 1), d, s)
        return remote(
            piece if src is None else src,
            piece,
            self.send.at[d, s - 1],
            self.recv.at[d, s - 1],
            **self.neighbour(d),
        )

    def arrival(self, d, s):
        piece = self.piece(self.origin(d, s), d, s)
        return remote(
            piece, piece, self.send.at[d, s - 1], self.recv.at[d, s - 1], **self.neighbour(d)
        )

    def aside(self, index, zi, core, src=None):
        piece = self.block(zi, core)
        return remote(
            piece if src is None else src,
            piece,
            self.sib_send.at[index],
            self.sib_recv.at[index],
            tp=1 - self.t,
        )

    def start(self, src=None):
        for d in (0, 1):
            self.hop(d, 1, src).start()
        if self.sib_send is not None:
            self.aside(0, self.z, self.t, src).start()

    def step(self, s):
        for d in (0, 1):
            self.arrival(d, s).wait_recv()
            self.hop(d, s + 1).start()
            if self.sib_send is not None:
                self.aside(2 * s - 1 + d, self.origin(d, s), self.t).start()

    def final(self):
        for d in (0, 1):
            self.arrival(d, self.steps).wait_recv()
        if self.sib_send is not None:
            self.aside(self.nz - 1, self.origin(0, self.steps), self.t).start()

    def asides(self):
        yield 0, self.z
        for s in range(1, self.steps):
            for d in (0, 1):
                yield 2 * s - 1 + d, self.origin(d, s)
        yield self.nz - 1, self.origin(0, self.steps)

    def wait_aside(self, index, zi):
        self.aside(index, zi, 1 - self.t).wait_recv()

    def wait_sibling(self):
        for index, zi in self.asides():
            self.wait_aside(index, zi)

    def drain(self):
        for d in (0, 1):
            for s in range(1, self.steps + 1):
                self.hop(d, s).wait_send()
        if self.sib_send is not None:
            for index, zi in self.asides():
                self.aside(index, zi, self.t).wait_send()


def main_kernel(
    nz,
    sections,
    hid_hbm,
    gain_ref,
    w_hbm,
    q_hbm,
    freq_ref,
    grad_hbm,
    up_hbm,
    down_hbm,
    doc_ref,
    att_hbm,
    low_out,
    all_buf,
    norm_out,
    hid_ref,
    q_raw,
    q_ref,
    grad_ref,
    up_ref,
    down_ref,
    cos_ref,
    sin_ref,
    w_raw,
    w_wide,
    w_buf,
    normed,
    x_buf,
    square_src,
    square_in,
    back_part,
    back_in,
    back_own,
    back_all,
    down_buf,
    doc_in,
    doc_all,
    k_part,
    k_in,
    v_part,
    v_in,
    k_all,
    v_all,
    q_all,
    bias_ref,
    top,
    s_buf,
    p_buf,
    v_ext,
    acc,
    att,
    low_src,
    low_in,
    red_src,
    red_in,
    dred_src,
    dred_in,
    sq_src,
    sq_in,
    sq_all,
    att_out,
    w_send,
    w_recv,
    ws_send,
    ws_recv,
    kv_send,
    kv_recv,
    kvs_send,
    kvs_recv,
    d_send,
    d_recv,
    x_send,
    x_recv,
    q_send,
    q_recv,
    rs_send,
    rs_recv,
    dy_send,
    dy_recv,
    pair_send,
    pair_recv,
    back_send,
    back_recv,
    att_send,
    att_recv,
    low_send,
    low_recv,
    red_send,
    red_recv,
    dred_send,
    dred_recv,
    all_send,
    all_recv,
    sq_send,
    sq_recv,
    sqa_send,
    sqa_recv,
    load_sem,
    own_sem,
):
    z, y, t = position()
    section = lax.axis_index("section")
    rows, width = hid_ref.shape
    depth = w_buf.shape[2] // nz
    cols = depth * nz // 2
    head_dim = k_all.shape[-1]
    heads = q_all.shape[0]
    toks = 2 * rows
    keys = 2 * toks
    rank = up_ref.shape[0]
    count = nz * NY
    me = z * NY + y
    steps = nz // 2
    home = y // 2
    sibling = dict(tp=1 - t)
    peers = [(osec, ot) for osec in range(sections) for ot in range(2) if osec or ot]

    barrier = pltpu.get_barrier_semaphore()

    def greet(**where):
        pl.semaphore_signal(barrier, inc=1, device_id=where, device_id_type=MESH)

    greet(ctx=(z + 1) % nz * NY + y)
    greet(ctx=(z + nz - 1) % nz * NY + y)
    for oy in range(NY):
        for ot in range(2):
            if oy or ot:
                greet(ctx=z * NY + (y + oy) % NY, tp=(t + ot) % 2)
    for osec, ot in peers:
        if osec:
            greet(section=(section + osec) % sections, tp=(t + ot) % 2)
    slab = rows // 4
    hid_loads = [
        pltpu.make_async_copy(
            hid_hbm.at[pl.ds(i * slab, slab)], hid_ref.at[pl.ds(i * slab, slab)], load_sem.at[i]
        )
        for i in range(4)
    ]
    late_loads = [
        pltpu.make_async_copy(src, dst, load_sem.at[4 + i])
        for i, (src, dst) in enumerate(
            ((q_hbm, q_raw), (grad_hbm, grad_ref), (up_hbm, up_ref), (down_hbm, down_ref))
        )
    ]
    w_load = pltpu.make_async_copy(w_hbm, w_raw, own_sem.at[0])
    w_load.start()
    for load in hid_loads:
        load.start()
    own_rows = pl.ds(pl.multiple_of(z * depth, depth), depth)
    w_load.wait()
    w_wide[...] = w_raw[...].astype(F32)
    for p in (0, 1):
        for h in range(2):
            w_buf[p, t, own_rows, h * head_dim : (h + 1) * head_dim] = w_wide[
                pl.ds(2 * h + p, depth, stride=4), :
            ].astype(BF16)
    pl.semaphore_wait(barrier, 2 + 2 * NY - 1 + 2 * (sections - 1))

    def w_block(p):
        return lambda zi, core: w_buf.at[p, core, pl.ds(pl.multiple_of(zi * depth, depth), depth)]

    def w_half(p):
        return lambda zi, h, core: w_buf.at[
            p, core, pl.ds(pl.multiple_of(zi * depth + h * (depth // 2), depth // 2), depth // 2)
        ]

    def kv_block(buf):
        return lambda zi, core: buf.at[zi, core]

    def kv_half(buf):
        size = buf.shape[2] // 2
        return lambda zi, h, core: buf.at[zi, core, pl.ds(h * size, size)]

    w_rings = [
        Ring(nz, w_block(p), w_half(p), w_send.at[p], w_recv.at[p], ws_send.at[p], ws_recv.at[p])
        for p in (0, 1)
    ]
    kv_rings = [
        Ring(nz, kv_block(buf), kv_half(buf), kv_send.at[p], kv_recv.at[p], kvs_send.at[p], kvs_recv.at[p])
        for p, buf in ((0, k_all), (1, v_all))
    ]

    w_rings[0].start()
    w_rings[1].start()
    for load in late_loads:
        load.start()

    doc_own = doc_in.at[0]
    doc_in[0] = jnp.broadcast_to(doc_ref[...], doc_in.shape[1:])

    def doc_copy(oy):
        return remote(
            doc_own,
            doc_in.at[oy],
            dy_send.at[oy - 1],
            dy_recv.at[oy - 1],
            ctx=z * NY + (y + oy) % NY,
        )

    for oy in range(1, NY):
        doc_copy(oy).start()

    def down_copy(core):
        return remote(down_ref, down_buf.at[core], pair_send.at[0], pair_recv.at[0], **sibling)

    for i, load in enumerate(hid_loads):
        load.wait()
        hid = hid_ref[i * slab : (i + 1) * slab, :].astype(F32)
        square = jnp.sum(hid * hid, axis=1, keepdims=True)
        square_src[i * slab : (i + 1) * slab, :] = jnp.broadcast_to(square, (slab, 128))
    square_copy = remote(square_src, square_in, pair_send.at[1], pair_recv.at[1], **sibling)
    square_copy.start()
    square_copy.wait_recv()
    mean = (square_src[:, :1] + square_in[:, :1]) * (1.0 / (2 * width))
    scale = lax.rsqrt(mean + 1e-06)

    def x_dest(b, core):
        return x_buf.at[pl.ds(b * rows, rows), pl.ds(pl.multiple_of(core * cols, cols), cols)]

    def x_copy(oy):
        yd = (y + oy) % NY
        return remote(
            normed.at[yd],
            x_dest(y % 2, t),
            x_send.at[oy],
            x_recv.at[y % 2, t],
            ctx=z * NY + yd,
            tp=home,
        )

    for yd in range(NY):
        for zl in range(nz // 2):
            start = (zl * NY + yd) * depth
            piece = hid_ref[:, start : start + depth].astype(F32)
            gain = gain_ref[:, start : start + depth].astype(F32)
            normed[yd, :, zl * depth : (zl + 1) * depth] = (piece * scale * gain).astype(BF16)
    for oy in range(1, NY):
        x_copy(oy).start()

    @pl.when(t != home)
    def _():
        x_copy(0).start()

    @pl.when(t == home)
    def _():
        x_buf[
            pl.ds(pl.multiple_of((y % 2) * rows, rows), rows),
            pl.ds(pl.multiple_of(t * cols, cols), cols),
        ] = normed[y]

    late_loads[0].wait()
    turned_q = jnp.transpose(q_raw[...].astype(F32), (1, 0, 2)).astype(BF16)
    q_ref[...] = turned_q.reshape(q_ref.shape)

    def q_dest(b):
        return q_all.at[:, pl.ds(b * rows, rows)]

    def q_copy(kvl):
        return remote(
            q_ref.at[kvl],
            q_dest(y % 2),
            q_send.at[kvl],
            q_recv.at[y % 2],
            ctx=z * NY + 2 * t + kvl,
            tp=home,
        )

    def home_own(kvl):
        return jnp.logical_and(2 * t + kvl == y, home == t)

    for kvl in range(2):

        @pl.when(jnp.logical_not(home_own(kvl)))
        def _():
            q_copy(kvl).start()

        @pl.when(home_own(kvl))
        def _():
            q_all[:, pl.ds(pl.multiple_of((y % 2) * rows, rows), rows), :] = q_ref[kvl]

    for oy in range(1, NY):
        doc_copy(oy).wait_recv()
    line = lax.broadcasted_iota(jnp.int32, doc_in.shape[1:], 0)
    group = jnp.where(line == y, doc_in[0], 0)
    for oy in range(1, NY):
        group = jnp.where(line == (y + NY - oy) % NY, doc_in[oy], group)
    doc_all[z] = group

    def doc_pass(d, s):
        zi = (z - s + 1 + nz) % nz if d == 0 else (z + s - 1) % nz
        to = (z + 1) % nz if d == 0 else (z + nz - 1) % nz
        return remote(
            doc_all.at[zi], doc_all.at[zi], d_send.at[d, s - 1], d_recv.at[d, s - 1], ctx=to * NY + y
        )

    def doc_arrive(d, s):
        zi = (z - s + nz) % nz if d == 0 else (z + s) % nz
        to = (z + 1) % nz if d == 0 else (z + nz - 1) % nz
        return remote(
            doc_all.at[zi], doc_all.at[zi], d_send.at[d, s - 1], d_recv.at[d, s - 1], ctx=to * NY + y
        )

    doc_hops = [(0, s) for s in range(1, steps + 1)] + [(1, s) for s in range(1, steps)]

    def doc_step(s):
        for d in (0, 1):
            if (d, s) in doc_hops:
                doc_arrive(d, s).wait_recv()
                if (d, s + 1) in doc_hops:
                    doc_pass(d, s + 1).start()

    for d in (0, 1):
        if (d, 1) in doc_hops:
            doc_pass(d, 1).start()

    late_loads[3].wait()
    down_copy(t).start()
    down_buf[t] = down_ref[...]
    late_loads[1].wait()
    late_loads[2].wait()
    back_part[...] = lax.dot_general(
        up_ref[...], grad_ref[...], (((1,), (1,)), ((), ())), preferred_element_type=F32
    )
    back_copy = remote(back_part, back_in, pair_send.at[2], pair_recv.at[2], **sibling)
    back_copy.start()

    def back_pass(oy):
        return remote(
            back_own,
            back_all.at[y % 2],
            back_send.at[oy - 1],
            back_recv.at[y % 2],
            ctx=z * NY + (y + oy) % NY,
        )

    for s in range(1, steps):
        w_rings[0].step(s)
        w_rings[1].step(s)
        doc_step(s)
        if s == 2:
            lane = lax.broadcasted_iota(jnp.int32, cos_ref.shape, 1)
            token = lax.broadcasted_iota(jnp.int32, cos_ref.shape, 0) + (z * 2 + t) * toks
            angles = token.astype(F32) * freq_ref[...]
            cos_ref[...] = jnp.cos(angles)
            sine = jnp.sin(angles)
            sin_ref[...] = jnp.where(lane < head_dim // 2, -sine, sine)
        if s == 1:
            back_copy.wait_recv()
            back_own[...] = (back_part[...] + back_in[...]).astype(BF16)

            @pl.when(t == home)
            def _():
                for oy in range(1, NY):
                    back_pass(oy).start()
                back_all[y % 2] = back_own[...]

    def x_wait():
        for b in range(2):
            for core in range(2):

                @pl.when(jnp.logical_or(2 * t + b != y, t != core))
                def _():
                    dest = x_dest(b, core)
                    remote(dest, dest, x_send.at[0], x_recv.at[b, core], **sibling).wait_recv()

    def project(p, part):
        for core in range(2):
            partial = jnp.dot(x_buf[...], w_buf[p, core], preferred_element_type=F32)
            for hl in range(2):
                part[2 * core + hl] = partial[:, hl * head_dim : (hl + 1) * head_dim].astype(part.dtype)

    def scatter_copy(p, oy):
        part, into = ((k_part, k_in), (v_part, v_in))[p]
        yd = (y + oy) % NY
        return remote(
            part.at[yd],
            into.at[oy - 1],
            rs_send.at[p, oy - 1],
            rs_recv.at[p, oy - 1],
            ctx=z * NY + yd,
        )

    def collect(p):
        part, into = ((k_part, k_in), (v_part, v_in))[p]
        for oy in range(1, NY):
            scatter_copy(p, oy).wait_recv()
        whole = part[y].astype(F32)
        for oy in range(1, NY):
            whole = whole + into[oy - 1].astype(F32)
        return whole

    def rope(v):
        return (v * cos_ref[...] + pltpu.roll(v, head_dim // 2, 1) * sin_ref[...]).astype(BF16)

    x_wait()
    w_rings[0].final()
    w_rings[0].wait_sibling()
    project(0, k_part)
    for oy in range(1, NY):
        scatter_copy(0, oy).start()
    w_rings[1].final()
    w_rings[1].wait_sibling()
    project(1, v_part)
    for oy in range(1, NY):
        scatter_copy(1, oy).start()

    for b in range(2):

        @pl.when(jnp.logical_or(2 * t + b != y, home != t))
        def _():
            dest = q_dest(b)
            remote(dest, dest, q_send.at[0], q_recv.at[b], **sibling).wait_recv()

    for h in range(heads):
        q_all[h] = rope(q_all[h].astype(F32))
    doc_step(steps)
    q_doc = jnp.concatenate(
        [
            jnp.sum(jnp.where(line == 2 * t + b, doc_all[z].astype(F32), 0.0), axis=0, keepdims=True)
            for b in range(2)
        ],
        axis=1,
    )

    q_pos = (z * 2 + t) * toks + lax.broadcasted_iota(jnp.int32, (keys, toks), 1)
    k_pos = lax.broadcasted_iota(jnp.int32, (keys, toks), 0)

    def mask(kb, carry):
        turned = jnp.transpose(doc_all[kb].astype(F32))
        k_doc = jnp.concatenate([turned[:, j : j + 1] for j in range(NY)], axis=0)
        allowed = jnp.logical_and(k_doc == q_doc, k_pos + kb * keys <= q_pos)
        bias_ref[kb] = jnp.where(allowed, 0.0, -1e30)
        return carry

    lax.fori_loop(0, nz, mask, 0)

    k_all[z, t] = rope(collect(0))
    kv_rings[0].start()
    v_all[z, t] = jnp.transpose(collect(1)).astype(BF16)
    kv_rings[1].start()

    factor = head_dim ** (-0.5) * math.log2(math.e)

    def block(kb, first):
        for core in range(2):
            v_ext[:head_dim, core * toks : (core + 1) * toks] = v_all[kb, core]

        tops, shrinks = {}, {}

        def score(h):
            q = q_all[h]
            slot = h % 2
            peak = None
            for core in range(2):
                scores = (
                    lax.dot_general(
                        k_all[kb, core], q, (((1,), (1,)), ((), ())), preferred_element_type=F32
                    )
                    + bias_ref[kb, core * toks : (core + 1) * toks, :]
                )
                s_buf[slot, core] = scores
                here = jnp.max(scores, axis=0, keepdims=True)
                peak = here if peak is None else jnp.maximum(peak, here)
            if not first:
                old_top = top[h]
                peak = jnp.maximum(old_top, peak)
                shrinks[h] = jnp.exp2((old_top - peak) * factor)
            top[h] = peak
            tops[h] = peak

        def weigh(h):
            slot = h % 2
            for core in range(2):
                for r in range(0, toks, PIECE):
                    p_buf[slot, core * toks + r : core * toks + r + PIECE, :] = jnp.exp2(
                        (s_buf[slot, core, r : r + PIECE, :] - tops[h]) * factor
                    ).astype(BF16)

        def mix(h):
            slot = h % 2
            part = jnp.dot(v_ext[...], p_buf[slot], preferred_element_type=F32)[: head_dim + 8]
            acc[h] = part if first else acc[h] * shrinks[h] + part

        for i in range(heads + 2):
            if i < heads:
                score(i)
            if 0 <= i - 1 < heads:
                weigh(i - 1)
            if i >= 2:
                mix(i - 2)

    def await_aside(index, zi):
        for ring in kv_rings:
            ring.wait_aside(index, zi)

    def attend_step(s):
        def one(d, carry):
            zi = jnp.where(d == 0, z - s + nz, z + s) % nz
            await_aside(2 * s - 1 + d, zi)

            @pl.when(zi < z)
            def _():
                block(zi, False)

            return carry

        lax.fori_loop(0, 2, one, 0)

    v_ext[head_dim:, :] = jnp.ones((16, 2 * toks), BF16)
    await_aside(0, z)
    block(z, True)
    for s in range(1, steps):
        kv_rings[0].step(s)
        kv_rings[1].step(s)
        attend_step(s)
    kv_rings[0].final()
    kv_rings[1].final()
    last = kv_rings[0].origin(0, steps)
    await_aside(nz - 1, last)

    @pl.when(last < z)
    def _():
        block(last, False)

    down_copy(1 - t).wait_recv()
    half_cols = heads * head_dim
    low = None
    for h in range(heads):
        out = acc[h, :head_dim, :] / acc[h, head_dim : head_dim + 1, :]
        factor_cols = down_buf[
            home, :, pl.ds(pl.multiple_of((y % 2) * half_cols + h * head_dim, head_dim), head_dim)
        ]
        part = jnp.dot(factor_cols, out.astype(BF16), preferred_element_type=F32)
        low = part if low is None else low + part
        att[:, h * head_dim : (h + 1) * head_dim] = jnp.transpose(out).astype(BF16)

    def low_copy(b, core):
        return remote(
            low_src.at[b],
            low_in.at[y],
            low_send.at[b, core],
            low_recv.at[y],
            ctx=z * NY + 2 * t + b,
            tp=core,
        )

    def low_own(b, core):
        return jnp.logical_and(2 * t + b == y, t == core)

    for b in range(2):
        low_src[b] = low[:, b * rows : (b + 1) * rows]
    for b in range(2):
        for core in range(2):

            @pl.when(jnp.logical_not(low_own(b, core)))
            def _():
                low_copy(b, core).start()

            @pl.when(low_own(b, core))
            def _():
                low_in[y] = low_src[b]

    for b in range(2):

        @pl.when(2 * t + b != y)
        def _():
            remote(
                back_all.at[b], back_all.at[b], back_send.at[0], back_recv.at[b], **sibling
            ).wait_recv()

    back = jnp.concatenate([back_all[0], back_all[1]], axis=1)
    down_part = jnp.dot(back, att[...], preferred_element_type=F32)
    for r in range(2):
        for h in range(heads):
            dred_src[r * heads + h] = down_part[8 * r : 8 * r + 8, h * 128 : (h + 1) * 128].astype(BF16)
    blocks = count // 2

    def dred_owner(i):
        return (i // heads) * blocks + (y % 2) * heads + i % heads

    def dred_copy(i):
        return remote(
            dred_src.at[i],
            dred_in.at[2 * z + t],
            dred_send.at[i],
            dred_recv.at[2 * z + t],
            ctx=dred_owner(i),
            tp=home,
        )

    def dred_own(i):
        return jnp.logical_and(dred_owner(i) == me, home == t)

    def dred_start(i, carry):
        @pl.when(jnp.logical_not(dred_own(i)))
        def _():
            dred_copy(i).start()

        @pl.when(dred_own(i))
        def _():
            dred_in[2 * z + t] = dred_src[i]

        return carry

    lax.fori_loop(0, 2 * heads, dred_start, 0)

    def att_dest(kvl):
        return att_out.at[:, pl.ds(pl.multiple_of(kvl * half_cols, half_cols), half_cols)]

    def att_copy(b):
        return remote(
            att.at[pl.ds(b * rows, rows)],
            att_dest(y % 2),
            att_send.at[b],
            att_recv.at[y % 2],
            ctx=z * NY + 2 * t + b,
            tp=home,
        )

    for b in range(2):

        @pl.when(jnp.logical_not(home_own(b)))
        def _():
            att_copy(b).start()

        @pl.when(home_own(b))
        def _():
            att_out[:, pl.ds(pl.multiple_of((y % 2) * half_cols, half_cols), half_cols)] = att[
                b * rows : (b + 1) * rows
            ]

    for src_y in range(NY):

        @pl.when(jnp.logical_or(src_y != y, home != t))
        def _():
            remote(
                low_in.at[src_y], low_in.at[src_y], low_send.at[0, 0], low_recv.at[src_y], **sibling
            ).wait_recv()

    low = low_in[0]
    for src_y in range(1, NY):
        low = low + low_in[src_y]
    low = low.astype(BF16)
    low_out[...] = low

    for c in range(count):
        red_src[c] = jnp.dot(
            low, grad_ref[:, c * 128 : (c + 1) * 128], preferred_element_type=F32
        ).astype(BF16)

    def red_copy(o):
        to = (me + o) % count
        return remote(
            red_src.at[to], red_in.at[o - 1], red_send.at[o - 1], red_recv.at[o - 1], ctx=to
        )

    def red_start(o, carry):
        red_copy(o).start()
        return carry

    lax.fori_loop(1, count, red_start, 0)

    down_y = 2 * t + (me % blocks) // heads

    def dred_add(i, carry):
        @pl.when(jnp.logical_or(down_y != y, i != 2 * z + t))
        def _():
            remote(
                dred_in.at[i], dred_in.at[i], dred_send.at[0], dred_recv.at[i], **sibling
            ).wait_recv()

        return carry + dred_in[i].astype(F32)

    down_sum = lax.fori_loop(0, 2 * nz, dred_add, jnp.zeros((8, 128), F32))

    def red_add(o, so_far):
        red_copy(o).wait_recv()
        return so_far + red_in[o - 1].astype(F32)

    up_sum = lax.fori_loop(1, count, red_add, red_src[me].astype(F32))
    all_buf[me] = jnp.concatenate([up_sum, down_sum], axis=0).astype(BF16)
    squares = jnp.sum(up_sum * up_sum, axis=0, keepdims=True) + jnp.sum(
        down_sum * down_sum, axis=0, keepdims=True
    )
    sq_src[...] = jnp.broadcast_to(jnp.sum(squares, axis=1, keepdims=True), sq_src.shape)

    def sq_copy(i):
        osec, ot = peers[i]
        return remote(
            sq_src,
            sq_in.at[i],
            sq_send.at[i],
            sq_recv.at[i],
            section=(section + osec) % sections,
            tp=(t + ot) % 2,
        )

    for i in range(len(peers)):
        sq_copy(i).start()

    def spread(buf, sends, recvs):
        def copy(o):
            to = (me + o) % count
            return remote(buf.at[me], buf.at[me], sends.at[o - 1], recvs.at[o - 1], ctx=to)

        def arrive(o):
            of = (me - o + count) % count
            return remote(buf.at[of], buf.at[of], sends.at[o - 1], recvs.at[o - 1], ctx=of)

        def each(act):
            def one(o, carry):
                act(o)
                return carry

            lax.fori_loop(1, count, one, 0)

        return (
            lambda: each(lambda o: copy(o).start()),
            lambda: each(lambda o: arrive(o).wait_recv()),
            lambda: each(lambda o: copy(o).wait_send()),
        )

    all_start, all_wait, all_drain = spread(all_buf, all_send, all_recv)
    sqa_start, sqa_wait, sqa_drain = spread(sq_all, sqa_send, sqa_recv)
    all_start()
    squares = sq_src[...]
    for i in range(len(peers)):
        sq_copy(i).wait_recv()
        squares = squares + sq_in[i]
    sq_all[me] = squares
    sqa_start()

    for ring in w_rings + kv_rings:
        ring.drain()
    for oy in range(1, NY):
        doc_copy(oy).wait_send()
        x_copy(oy).wait_send()
        scatter_copy(0, oy).wait_send()
        scatter_copy(1, oy).wait_send()

    @pl.when(t != home)
    def _():
        x_copy(0).wait_send()

    @pl.when(t == home)
    def _():
        for oy in range(1, NY):
            back_pass(oy).wait_send()

    for d, s in doc_hops:
        doc_pass(d, s).wait_send()
    down_copy(t).wait_send()
    square_copy.wait_send()
    back_copy.wait_send()
    for b in range(2):

        @pl.when(jnp.logical_not(home_own(b)))
        def _():
            q_copy(b).wait_send()
            att_copy(b).wait_send()

        for core in range(2):

            @pl.when(jnp.logical_not(low_own(b, core)))
            def _():
                low_copy(b, core).wait_send()

    def dred_drain(i, carry):
        @pl.when(jnp.logical_not(dred_own(i)))
        def _():
            dred_copy(i).wait_send()

        return carry

    lax.fori_loop(0, 2 * heads, dred_drain, 0)

    def red_drain(o, carry):
        red_copy(o).wait_send()
        return carry

    lax.fori_loop(1, count, red_drain, 0)
    for kvl in range(2):

        @pl.when(jnp.logical_or(2 * t + kvl != y, home != t))
        def _():
            dest = att_dest(kvl)
            remote(dest, dest, att_send.at[0], att_recv.at[kvl], **sibling).wait_recv()

    att_store = pltpu.make_async_copy(att_out, att_hbm, own_sem.at[1])
    att_store.start()
    all_wait()
    all_drain()
    for i in range(len(peers)):
        sq_copy(i).wait_send()
    sqa_wait()
    sqa_drain()
    norm = sq_all[0]
    for c in range(1, count):
        norm = norm + sq_all[c]
    norm_out[...] = norm
    att_store.wait()


def finish_kernel(
    ceiling,
    att_hbm,
    low_hbm,
    all_hbm,
    sq_hbm,
    up_hbm,
    att_out,
    adapter_out,
    gdown_out,
    gup_out,
    att_ref,
    low_ref,
    all_ref,
    sq_ref,
    up_ref,
    adapter,
    gdown,
    gup,
    in_sem,
    out_sem,
):
    count = all_ref.shape[0]
    rank, rows = low_ref.shape
    width = up_ref.shape[1]
    blocks = count // 2
    ins = [
        pltpu.make_async_copy(src, dst, in_sem.at[i])
        for i, (src, dst) in enumerate(
            (
                (low_hbm, low_ref),
                (up_hbm, up_ref),
                (sq_hbm, sq_ref),
                (all_hbm, all_ref),
                (att_hbm.at[pl.ds(0, rows // 2)], att_ref.at[pl.ds(0, rows // 2)]),
                (att_hbm.at[pl.ds(rows // 2, rows // 2)], att_ref.at[pl.ds(rows // 2, rows // 2)]),
            )
        )
    ]
    outs = []

    def put(src, dst):
        copy = pltpu.make_async_copy(src, dst, out_sem.at[len(outs)])
        copy.start()
        outs.append(copy)

    for copy in ins:
        copy.start()
    ins[0].wait()
    ins[1].wait()
    part = rows // 4
    low = jnp.transpose(low_ref[...].astype(F32)).astype(BF16)
    for i in range(4):
        adapter[i * part : (i + 1) * part, :] = jnp.dot(
            low[i * part : (i + 1) * part], up_ref[...], preferred_element_type=F32
        ).astype(BF16)
        put(adapter.at[pl.ds(i * part, part)], adapter_out.at[pl.ds(i * part, part)])
    for i in range(2):
        ins[4 + i].wait()
        half = pl.ds(i * (rows // 2), rows // 2)
        put(att_ref.at[half], att_out.at[half])
    ins[2].wait()
    ins[3].wait()
    clip = jnp.minimum(1.0, ceiling / (jnp.sqrt(sq_ref[0:1, 0:1]) + 1e-06))
    for c in range(count):
        r0 = 8 * (c // blocks)
        c0 = 128 * (c % blocks)
        gup[:, c * 128 : (c + 1) * 128] = all_ref[c, 0:rank, :].astype(F32) * clip
        gdown[r0 : r0 + 8, c0 : c0 + 128] = all_ref[c, rank : rank + 8, :].astype(F32) * clip
    put(gup, gup_out)
    put(gdown, gdown_out)
    for copy in outs:
        copy.wait()


def per_device(hidden, gain, queries, key_value_weight, adapt_down, adapt_up, out_grad, doc_ids):
    nz = lax.axis_size("ctx") // NY
    sections = lax.axis_size("section")
    rows, width = hidden.shape[1:]
    depth, kv_count = key_value_weight.shape[1:3]
    head_dim = key_value_weight.shape[-1]
    heads = queries.shape[2]
    group = heads // kv_count
    rank, local_query = adapt_down.shape[1:]
    toks = 2 * rows
    half = head_dim // 2
    freqs = (1000000.0 ** (-np.arange(half) * 2.0 / head_dim)).astype(np.float32)
    freqs = jnp.asarray(np.concatenate([freqs, freqs])[None])
    w = key_value_weight.reshape(depth * kv_count * 2, head_dim)

    vmem = pl.BlockSpec(memory_space=pltpu.VMEM)
    hbm = pl.BlockSpec(memory_space=pl.ANY)
    dma = pltpu.SemaphoreType.DMA
    steps = nz // 2
    count = nz * NY
    peers = 2 * sections - 1
    chunk = rank + 8
    att, low, summed, squares = pl.pallas_call(
        lambda *refs: main_kernel(nz, sections, *refs),
        out_shape=(
            jax.ShapeDtypeStruct((rows, local_query), BF16),
            jax.ShapeDtypeStruct((rank, rows), BF16),
            jax.ShapeDtypeStruct((count, chunk, 128), BF16),
            jax.ShapeDtypeStruct((8, 128), F32),
        ),
        in_specs=[hbm, vmem, hbm, hbm, vmem, hbm, hbm, hbm, vmem],
        out_specs=[hbm, vmem, vmem, vmem],
        scratch_shapes=[
            pltpu.VMEM((rows, width), BF16),
            pltpu.VMEM((rows, heads, head_dim), BF16),
            pltpu.VMEM((kv_count, group, rows, head_dim), BF16),
            pltpu.VMEM((rows, width), BF16),
            pltpu.VMEM((rank, width), BF16),
            pltpu.VMEM((rank, local_query), BF16),
            pltpu.VMEM((toks, head_dim), F32),
            pltpu.VMEM((toks, head_dim), F32),
            pltpu.VMEM((depth * kv_count * 2, head_dim), BF16),
            pltpu.VMEM((depth * kv_count * 2, head_dim), F32),
            pltpu.VMEM((2, 2, nz * depth, kv_count * head_dim), BF16),
            pltpu.VMEM((NY, rows, depth * nz // 2), BF16),
            pltpu.VMEM((toks, depth * nz), BF16),
            pltpu.VMEM((rows, 128), F32),
            pltpu.VMEM((rows, 128), F32),
            pltpu.VMEM((rank, rows), F32),
            pltpu.VMEM((rank, rows), F32),
            pltpu.VMEM((rank, rows), BF16),
            pltpu.VMEM((2, rank, rows), BF16),
            pltpu.VMEM((2, rank, local_query), BF16),
            pltpu.VMEM((NY, 8, rows), jnp.int32),
            pltpu.VMEM((nz, 8, rows), jnp.int32),
            pltpu.VMEM((NY, toks, head_dim), F32),
            pltpu.VMEM((NY - 1, toks, head_dim), F32),
            pltpu.VMEM((NY, toks, head_dim), BF16),
            pltpu.VMEM((NY - 1, toks, head_dim), BF16),
            pltpu.VMEM((nz, 2, toks, head_dim), BF16),
            pltpu.VMEM((nz, 2, head_dim, toks), BF16),
            pltpu.VMEM((group, toks, head_dim), BF16),
            pltpu.VMEM((nz, 2 * toks, toks), F32),
            pltpu.VMEM((group, 1, toks), F32),
            pltpu.VMEM((2, 2, toks, toks), F32),
            pltpu.VMEM((2, 2 * toks, toks), BF16),
            pltpu.VMEM((head_dim + 16, 2 * toks), BF16),
            pltpu.VMEM((group, head_dim + 8, toks), F32),
            pltpu.VMEM((toks, group * head_dim), BF16),
            pltpu.VMEM((2, rank, rows), F32),
            pltpu.VMEM((NY, rank, rows), F32),
            pltpu.VMEM((count, rank, 128), BF16),
            pltpu.VMEM((count - 1, rank, 128), BF16),
            pltpu.VMEM((2 * group, 8, 128), BF16),
            pltpu.VMEM((2 * nz, 8, 128), BF16),
            pltpu.VMEM((8, 128), F32),
            pltpu.VMEM((peers, 8, 128), F32),
            pltpu.VMEM((count, 8, 128), F32),
            pltpu.VMEM((rows, local_query), BF16),
            dma((2, 2, steps)),
            dma((2, 2, steps)),
            dma((2, nz)),
            dma((2, nz)),
            dma((2, 2, steps)),
            dma((2, 2, steps)),
            dma((2, nz)),
            dma((2, nz)),
            dma((2, steps)),
            dma((2, steps)),
            dma((NY,)),
            dma((2, 2)),
            dma((2,)),
            dma((2,)),
            dma((2, NY - 1)),
            dma((2, NY - 1)),
            dma((NY - 1,)),
            dma((NY - 1,)),
            dma((3,)),
            dma((3,)),
            dma((NY - 1,)),
            dma((2,)),
            dma((2,)),
            dma((2,)),
            dma((2, 2)),
            dma((NY,)),
            dma((count - 1,)),
            dma((count - 1,)),
            dma((2 * group,)),
            dma((2 * nz,)),
            dma((count - 1,)),
            dma((count - 1,)),
            dma((peers,)),
            dma((peers,)),
            dma((count - 1,)),
            dma((count - 1,)),
            dma((8,)),
            dma((2,)),
        ],
        compiler_params=pltpu.CompilerParams(collective_id=0, has_side_effects=True),
        name="main",
    )(
        hidden[0],
        gain,
        w,
        queries[0],
        freqs,
        out_grad[0],
        adapt_up[0],
        adapt_down[0],
        doc_ids[None],
    )

    ceiling = 0.5 * math.sqrt(sections * rank * (local_query + width) * 2)
    return pl.pallas_call(
        lambda *refs: finish_kernel(ceiling, *refs),
        out_shape=(
            jax.ShapeDtypeStruct((rows, local_query), BF16),
            jax.ShapeDtypeStruct((rows, width), BF16),
            jax.ShapeDtypeStruct((rank, local_query), F32),
            jax.ShapeDtypeStruct((rank, width), F32),
        ),
        in_specs=[hbm] * 5,
        out_specs=[hbm] * 4,
        scratch_shapes=[
            pltpu.VMEM((rows, local_query), BF16),
            pltpu.VMEM((rank, rows), BF16),
            pltpu.VMEM((count, chunk, 128), BF16),
            pltpu.VMEM((8, 128), F32),
            pltpu.VMEM((rank, width), BF16),
            pltpu.VMEM((rows, width), BF16),
            pltpu.VMEM((rank, local_query), F32),
            pltpu.VMEM((rank, width), F32),
            dma((6,)),
            dma((8,)),
        ],
        name="finish",
    )(att, low, summed, squares, adapt_up[0])


def solution(mesh):
    def step(*args):
        return tuple(out[None] for out in per_device(*args))

    return jax.shard_map(
        step,
        mesh=mesh,
        in_specs=(
            P("section", "ctx", "tp"),
            P("section", "tp"),
            P("section", "ctx", "tp", None),
            P("section", "ctx", "tp", None, None),
            P("section", None, "tp"),
            P("section", None, "tp"),
            P("section", "ctx", "tp"),
            P("ctx"),
        ),
        out_specs=(
            P("section", "ctx", "tp"),
            P("section", "ctx", "tp"),
            P("section", None, "tp"),
            P("section", None, "tp"),
        ),
        check_vma=False,
    )
```
